32 devices in a mesh: groups: 2 (over x), gx: 16 (over z, y, core).
Axes of the slice: x: 2, y: 2, z: 4, core: 2. Of those that a mesh axis runs over, the one named last changes fastest.
Arguments:
- features: bfloat16 [128, 8, 8, 8, 128], P(('groups', 'gx')), parts along dimension 0, may hold values from -6 to 6
- fine_nbr: int32 [128, 27], P(('groups', 'gx')), parts along dimension 0, may hold values from -1 to 3, as said below
- fine_send: int32 [32, 2, 4], P(('groups', 'gx')), parts along dimension 0, may hold values from -1 to 3, as said below
- fine_parent: int32 [128], P(('groups', 'gx')), parts along dimension 0, may hold values from -1 to 127, as said below
- coarse_child: int32 [32, 8], P(('groups', 'gx')), parts along dimension 0, may hold values from -1 to 63, as said below
- coarse_nbr: int32 [32, 27], P(('groups', 'gx')), parts along dimension 0, may hold values from -1 to 15, as said below
- enc_fine_w: bfloat16 [27, 128, 128], replicated, may hold values from -0.15625 to 0.15625
- enc_coarse_w: bfloat16 [27, 128, 128], replicated, may hold values from -0.15625 to 0.15625
- dec_coarse_w: bfloat16 [27, 128, 128], replicated, may hold values from -0.15625 to 0.15625
- dec_fine_w: bfloat16 [27, 128, 128], replicated, may hold values from -0.15625 to 0.15625
Outputs:
- fine_out: bfloat16 [128, 8, 8, 8, 128], P(('groups', 'gx')), parts along dimension 0
The draws below stay inside these ranges and needn't reach their ends.
There are 2 independent parts, one for each index of `groups`. The reference program is written for one: setup_inputs(seed, part) draws one part's arguments, and reference() takes and returns one part's arrays. A program takes and returns all parts, laid end to end along the dimension named above; an argument that names none is the same for every part. Nothing has to cross between parts.
Inputs may be any that keep to these rules, and one draw needn't show every extreme that they name: `fine_nbr`: entry t of a fine slot on gx device d names the slot, on device d + dx, of the brick at brick offset (dx, dy, dz), or is -1 where there is none. A slot whose entry 13 is -1 holds no brick and all its entries are -1; entry 13 of a brick is its own slot. Adjacency is symmetric. `fine_send`: on device d, entry s of row 0 is s when slot s holds a brick with a neighbour on device d + 1, else -1; row 1 likewise for device d - 1. `fine_parent`: 8 g + o for a brick whose parent is coarse slot g at octant o, -1 for slots without a brick. Coarse slot g is held by gx device g, which lies in the same aligned group of four gx devices as the child's device. `coarse_child`: entry o of coarse slot g is the fine slot f with fine_parent[f] = 8 g + o, or -1 where there is none. `coarse_nbr`: entry t (taps ordered as for fine_nbr) is the coarse slot of the neighbouring coarse brick, or -1 where there is none; entry 13 is the brick's own slot; every neighbour is held by a gx device of the same or an adjacent aligned group of four, and neighbours with dx = 0 by a device of the same aligned group of four.
All inputs are finite; a program needn't handle non-finite values.
Results may differ from the reference program's by a relative error of at most 0.01.
Values may be sent and summed in bfloat16 or wider, within the bound.
No kernel may reach another device: no remote copies, remote signals or barrier semaphores. Data moves between devices by JAX's collectives and lax.ppermute only.
A program may use at most 128 MiB of HBM per device.

```python
import jax
import jax.numpy as jnp
import numpy as np
from jax import lax

C = 128
EDGE = 8
FB = 4
CB = 1
NF = 64
NC = 16
N_GX = 16


OFFSETS = (-1, 0, 1)


def geometry(key):
    keys = jax.random.split(jax.random.fold_in(key, 7), 6)
    columns = N_GX
    depth = FB // 2
    places = 2 * FB
    tap_x = jnp.asarray(np.repeat(np.array(OFFSETS), 9), jnp.int32)
    tap_y = jnp.asarray(np.tile(np.repeat(np.array(OFFSETS), 3), 3), jnp.int32)
    tap_z = jnp.asarray(np.tile(np.array(OFFSETS), 9), jnp.int32)
    counts = jax.random.randint(keys[0], (columns,), FB // 2, FB + 1)
    busiest = jax.random.randint(keys[1], (), 0, columns)
    counts = jnp.where(jnp.arange(columns) == busiest, FB, counts)
    place_order = jax.vmap(lambda sub: jax.random.permutation(sub, places))(jax.random.split(keys[2], columns))
    slot_order = jax.vmap(lambda sub: jax.random.permutation(sub, FB))(jax.random.split(keys[3], columns))
    rank = jnp.arange(FB, dtype=jnp.int32)
    live_place = jnp.where(rank[None, :] < counts[:, None], place_order[:, :FB], -1).astype(jnp.int32)
    column_ids = jnp.arange(columns, dtype=jnp.int32)[:, None]
    slot_place = jnp.full((columns, FB), -1, jnp.int32).at[column_ids, slot_order].set(live_place)
    target = jnp.where(slot_place >= 0, slot_place, places)
    place_slot = jnp.full((columns, places + 1), -1, jnp.int32).at[column_ids, target].set(jnp.broadcast_to(rank, (columns, FB)))[:, :places]
    live = slot_place >= 0
    fine_y = jnp.where(live, slot_place // depth, 0)
    fine_z = jnp.where(live, slot_place % depth, 0)
    near_x = column_ids[:, :, None] + tap_x
    near_y = fine_y[:, :, None] + tap_y
    near_z = fine_z[:, :, None] + tap_z
    inside = live[:, :, None] & (near_x >= 0) & (near_x < columns) & (near_y >= 0) & (near_y < 4)
    inside = inside & (near_z >= 0) & (near_z < depth)
    found = place_slot[jnp.clip(near_x, 0, columns - 1), jnp.clip(near_y, 0, 3) * depth + jnp.clip(near_z, 0, depth - 1)]
    fine_nbr = jnp.where(inside, found, -1).astype(jnp.int32)
    upward = jnp.any(fine_nbr[:, :, 18:] >= 0, axis=-1)
    downward = jnp.any(fine_nbr[:, :, :9] >= 0, axis=-1)
    fine_send = jnp.stack([jnp.where(upward, rank, -1), jnp.where(downward, rank, -1)], axis=1).astype(jnp.int32)
    quads = columns // 4
    coarse_depth = FB // 4
    coarse_order = jax.vmap(lambda sub: jax.random.permutation(sub, FB))(jax.random.split(keys[4], quads))

    def coarse_slot(coarse_x, coarse_y, coarse_z):
        local = coarse_x % 2 * (FB // 2) + coarse_y * coarse_depth + coarse_z
        return coarse_x // 2 * FB + coarse_order[coarse_x // 2, local]
    parent_x = column_ids // 2
    parent = coarse_slot(jnp.broadcast_to(parent_x, (columns, FB)), fine_y // 2, fine_z // 2)
    octant = column_ids % 2 * 4 + fine_y % 2 * 2 + fine_z % 2
    fine_parent = jnp.where(live, parent * 8 + octant, -1).astype(jnp.int32).reshape(NF)
    dump = NC * 8
    coarse_child = jnp.full((NC * 8 + 1,), -1, jnp.int32).at[jnp.where(fine_parent >= 0, fine_parent, dump)].set(jnp.arange(NF, dtype=jnp.int32))[:NC * 8].reshape(NC, 8)
    width_x = columns // 2
    grid_x = jnp.broadcast_to(jnp.arange(width_x, dtype=jnp.int32)[:, None, None], (width_x, 2, coarse_depth))
    grid_y = jnp.broadcast_to(jnp.arange(2, dtype=jnp.int32)[None, :, None], (width_x, 2, coarse_depth))
    grid_z = jnp.broadcast_to(jnp.arange(coarse_depth, dtype=jnp.int32)[None, None, :], (width_x, 2, coarse_depth))
    step_x = grid_x[..., None] + tap_x
    step_y = grid_y[..., None] + tap_y
    step_z = grid_z[..., None] + tap_z
    within = (step_x >= 0) & (step_x < width_x) & (step_y >= 0) & (step_y < 2) & (step_z >= 0) & (step_z < coarse_depth)
    neighbour = coarse_slot(jnp.clip(step_x, 0, width_x - 1), jnp.clip(step_y, 0, 1), jnp.clip(step_z, 0, coarse_depth - 1))
    neighbour = jnp.where(within, neighbour, -1).astype(jnp.int32).reshape(-1, 27)
    owners = coarse_slot(grid_x, grid_y, grid_z).reshape(-1)
    coarse_nbr = jnp.zeros((NC, 27), jnp.int32).at[owners].set(neighbour)
    return (fine_nbr.reshape(NF, 27), fine_send, fine_parent, coarse_child, coarse_nbr)


def draw_fine_nbr(key, part):
    return geometry(key)[0]


def draw_fine_send(key, part):
    return geometry(key)[1]


def draw_fine_parent(key, part):
    return geometry(key)[2]


def draw_coarse_child(key, part):
    return geometry(key)[3]


def draw_coarse_nbr(key, part):
    return geometry(key)[4]


def block_levels(key, extent, pieces, least, top_value):
    level, own = 1.0, jax.random.fold_in(key, 6)
    for axis_at, blocks in pieces:
        steps = jnp.exp(jax.random.uniform(jax.random.fold_in(own, axis_at), (blocks,), jnp.float32, least / len(pieces), top_value / len(pieces)))
        level = level * jnp.repeat(steps, extent[axis_at] // blocks).reshape([-1 if axis == axis_at else 1 for axis in range(len(extent))])
    return level


def scatter_about(stream_key, shape, scale, most, cuts=(), kind=jnp.bfloat16):
    values = jax.random.normal(stream_key, shape, jnp.float32) * scale
    if len(cuts) > 0:
        values = block_levels(stream_key, shape, cuts, -0.22, 0.18) * values
    return jnp.clip(values, min=-most, max=most).astype(kind)


def setup_inputs(seed: int = 0, part: int = 0) -> dict:
    seeds = jax.random.split(jax.random.key(seed), 11)
    part_keys = jax.random.split(jax.random.fold_in(seeds[10], part), 11)
    features = scatter_about(part_keys[0], (NF, EDGE, EDGE, EDGE, C), 1.0, 6.0, ((0, 16),))
    fine_nbr = draw_fine_nbr(jax.random.fold_in(jax.random.fold_in(seeds[10], part), 71), part)
    fine_send = draw_fine_send(jax.random.fold_in(jax.random.fold_in(seeds[10], part), 71), part)
    fine_parent = draw_fine_parent(jax.random.fold_in(jax.random.fold_in(seeds[10], part), 71), part)
    coarse_child = draw_coarse_child(jax.random.fold_in(jax.random.fold_in(seeds[10], part), 71), part)
    coarse_nbr = draw_coarse_nbr(jax.random.fold_in(jax.random.fold_in(seeds[10], part), 71), part)
    enc_fine_w = scatter_about(seeds[6], (27, C, C), (27 * C // 2) ** -0.5, 0.15625)
    enc_coarse_w = scatter_about(seeds[7], (27, C, C), (27 * C // 2) ** -0.5, 0.15625)
    dec_coarse_w = scatter_about(seeds[8], (27, C, C), (27 * C // 2) ** -0.5, 0.15625)
    dec_fine_w = scatter_about(seeds[9], (27, C, C), (27 * C // 2) ** -0.5, 0.15625)
    return dict(features=features, fine_nbr=fine_nbr, fine_send=fine_send, fine_parent=fine_parent, coarse_child=coarse_child, coarse_nbr=coarse_nbr, enc_fine_w=enc_fine_w, enc_coarse_w=enc_coarse_w, dec_coarse_w=dec_coarse_w, dec_fine_w=dec_fine_w)


OFFSETS = (-1, 0, 1)


def region(offset, edge):
    if offset < 0:
        return slice(edge - 1, edge)
    if offset == 0:
        return slice(0, edge)
    return slice(0, 1)


def assemble(tables, index, edge):
    layers = []
    for offset_x in OFFSETS:
        table = tables[offset_x + 1]
        rows = []
        for offset_y in OFFSETS:
            cells = []
            for offset_z in OFFSETS:
                tap = 9 * (offset_x + 1) + 3 * (offset_y + 1) + offset_z + 1
                piece = table[:, :, region(offset_y, edge), region(offset_z, edge), :]
                cells.append(jnp.take(piece, index[:, tap], axis=0))
            rows.append(jnp.concatenate(cells, axis=3))
        layers.append(jnp.concatenate(rows, axis=2))
    return jnp.concatenate(layers, axis=1)


def convolve(padded, weights, edge):
    count = padded.shape[0]
    width = padded.shape[-1]
    total = jnp.zeros((count * edge ** 3, width), jnp.float32)
    for first in range(3):
        columns = jnp.concatenate([padded[:, first:first + edge, second:second + edge, third:third + edge, :]
                                   for second in range(3) for third in range(3)], axis=-1)
        columns = columns.reshape(count * edge ** 3, 9 * width).astype(jnp.float32)
        kernel = weights[9 * first:9 * first + 9].reshape(9 * width, width).astype(jnp.float32)
        total = total + jnp.dot(columns, kernel, preferred_element_type=jnp.float32)
    return jax.nn.relu(total).astype(jnp.bfloat16).reshape(count, edge, edge, edge, width)


def layer(bricks, index, weights, block):
    edge = bricks.shape[1]
    width = bricks.shape[-1]
    table = jnp.concatenate([bricks, jnp.zeros((1,) + bricks.shape[1:], jnp.bfloat16)], axis=0)
    tables = [table[:, edge - 1:], table, table[:, :1]]
    blocks = index.reshape(-1, block, 27)
    result = lax.map(lambda part_index: convolve(assemble(tables, part_index, edge), weights, edge), blocks)
    return result.reshape(-1, edge, edge, edge, width)


def from_octants(blocks, half):
    count = blocks.shape[0]
    width = blocks.shape[-1]
    shaped = blocks.reshape(count, 2, 2, 2, half, half, half, width).transpose(0, 1, 4, 2, 5, 3, 6, 7)
    return shaped.reshape(count, 2 * half, 2 * half, 2 * half, width)


def to_octants(bricks, half):
    count = bricks.shape[0]
    width = bricks.shape[-1]
    shaped = bricks.reshape(count, 2, half, 2, half, 2, half, width).transpose(0, 1, 3, 5, 2, 4, 6, 7)
    return shaped.reshape(count * 8, half, half, half, width)


def reference(features, fine_nbr, fine_send, fine_parent, coarse_child, coarse_nbr,
              enc_fine_w, enc_coarse_w, dec_coarse_w, dec_fine_w):
    edge = features.shape[1]
    width = features.shape[-1]
    half = edge // 2
    tap_x = jnp.asarray(np.repeat(np.array(OFFSETS), 9), jnp.int32)
    slot = jnp.arange(NF, dtype=jnp.int32)
    device = slot // FB
    neighbour_device = device[:, None] + tap_x[None, :]
    target = neighbour_device * FB + fine_nbr
    row = jnp.where(tap_x > 0, 1, 0).astype(jnp.int32)[None, :]
    flat_send = fine_send.reshape(-1)
    listed = jnp.clip((neighbour_device * 2 + row) * FB + fine_nbr, 0, N_GX * 2 * FB - 1).astype(jnp.int32)
    valid = (fine_nbr >= 0) & ((tap_x[None, :] == 0) | (flat_send[listed] == fine_nbr))
    src_fine = jnp.where(valid, target, NF).astype(jnp.int32)

    enc_fine = layer(features, src_fine, enc_fine_w, FB)
    pooled = enc_fine.astype(jnp.float32).reshape(NF, half, 2, half, 2, half, 2, width).mean(axis=(2, 4, 6))
    pooled = pooled.astype(jnp.bfloat16)
    pooled_table = jnp.concatenate([pooled, jnp.zeros((1, half, half, half, width), jnp.bfloat16)], axis=0)
    child_index = jnp.where(coarse_child >= 0, coarse_child, NF).astype(jnp.int32)
    coarse_in = from_octants(pooled_table[child_index], half)

    src_coarse = jnp.where(coarse_nbr >= 0, coarse_nbr, NC).astype(jnp.int32)
    enc_coarse = layer(coarse_in, src_coarse, enc_coarse_w, CB)
    dec_coarse = layer(enc_coarse, src_coarse, dec_coarse_w, CB)

    octants = to_octants(dec_coarse, half)
    octant_table = jnp.concatenate([octants, jnp.zeros((1, half, half, half, width), jnp.bfloat16)], axis=0)
    parent_index = jnp.where(fine_parent >= 0, fine_parent, NC * 8).astype(jnp.int32)
    upsampled = octant_table[parent_index]
    upsampled = jnp.repeat(jnp.repeat(jnp.repeat(upsampled, 2, axis=1), 2, axis=2), 2, axis=3)
    dec_in = (enc_fine.astype(jnp.float32) + upsampled.astype(jnp.float32)).astype(jnp.bfloat16)
    return layer(dec_in, src_fine, dec_fine_w, FB)
```

```python
import functools

import jax
import jax.numpy as jnp
from jax import lax
from jax.experimental import pallas as pl
from jax.experimental.pallas import tpu as pltpu
from jax.sharding import PartitionSpec as P

LANES = 4
OFFSETS = (-1, 0, 1)
BF16 = jnp.bfloat16
F32 = jnp.float32
VMEM = pl.BlockSpec(memory_space=pltpu.VMEM)
SMEM = pl.BlockSpec(memory_space=pltpu.SMEM)
PARAMS = pltpu.CompilerParams(vmem_limit_bytes=60 << 20)


def tap(dx, dy, dz):
    return 9 * (dx + 1) + 3 * (dy + 1) + dz + 1


def z_shifts(center, below, above):
    edge = center.shape[1]
    z = lax.broadcasted_iota(jnp.int32, center.shape, 1)
    down = jnp.where(z == 0, pltpu.roll(below, 1, 1), pltpu.roll(center, 1, 1))
    up = jnp.where(z == edge - 1, pltpu.roll(above, edge - 1, 1), pltpu.roll(center, edge - 1, 1))
    return down, center, up


def columns(fetch, edge):
    parts = []
    for dy in OFFSETS:
        triple = [fetch(dy, dz) for dz in (0, -1, 1)]
        planes, rows, _, width = triple[0].shape
        flat = [v.reshape(planes * rows, edge, width) for v in triple]
        parts.append([s.reshape(planes, rows, edge, width) for s in z_shifts(*flat)])
    return [jnp.concatenate([part[k] for part in parts], axis=1) for k in range(3)]


def y_rows(load, dy, edge):
    if dy == 0:
        value = load(0, edge * edge)
    elif dy < 0:
        value = load(edge * edge - 2 * edge, 2 * edge)[:, edge:]
    else:
        value = load(0, 2 * edge)[:, :edge]
    planes, rows, width = value.shape
    return value.reshape(planes, rows // edge, edge, width)


def inner_kernel(nbr, x_ref, w_ref, out_ref, part_ref, even, odd):
    slots, edge, rows, width = x_ref.shape
    even[:, :, 0] = jnp.zeros_like(even[:, :, 0])
    even[:, :, edge + 1] = jnp.zeros_like(even[:, :, 0])
    odd[:, :, 0] = jnp.zeros_like(odd[:, :, 0])
    odd[:, :, edge + 1] = jnp.zeros_like(odd[:, :, 0])
    for b in range(slots):

        def fetch(dy, dz):
            slot = nbr[b, tap(0, dy, dz)]
            held = jnp.maximum(slot, 0)
            value = y_rows(lambda r, n: x_ref[held, :, r : r + n, :].astype(F32), dy, edge)
            return jnp.where(slot >= 0, value, 0.0)

        for k, full in enumerate(columns(fetch, edge)):
            even[b, k, 1 : edge + 1] = full.reshape(edge, rows + 2 * edge, width).astype(BF16)
            odd[b, k, 1 : edge + 1] = full[:, 1 : edge + 1].reshape(edge, rows, width).astype(BF16)
        taps = []
        for dx in range(3):
            for dy in OFFSETS:
                for k in range(3):
                    if dy == 0:
                        piece = odd[b, k, dx : dx + edge]
                    else:
                        first = (dy + 1) * edge
                        piece = even[b, k, dx : dx + edge, first : first + rows]
                    taps.append(piece.reshape(edge * rows, width))
        total = jnp.dot(jnp.concatenate(taps, axis=1), w_ref[...], preferred_element_type=F32)
        total = total.reshape(edge, rows, width)
        out_ref[b] = jnp.maximum(total, 0.0).astype(BF16)
        part_ref[b, 0] = total[0]
        part_ref[b, 1] = total[edge - 1]


def inner(x, nbr, weights):
    slots, edge, rows, width = x.shape
    return pl.pallas_call(
        inner_kernel,
        out_shape=(
            jax.ShapeDtypeStruct(x.shape, BF16),
            jax.ShapeDtypeStruct((slots, 2, rows, width), F32),
        ),
        in_specs=[SMEM, VMEM, VMEM],
        out_specs=(VMEM, VMEM),
        scratch_shapes=[
            pltpu.VMEM((slots, 3, edge + 2, rows + 2 * edge, width), BF16),
            pltpu.VMEM((slots, 3, edge + 2, rows, width), BF16),
        ],
        compiler_params=PARAMS,
        cost_estimate=pl.CostEstimate(
            flops=2 * slots * edge * rows * 27 * width * width,
            bytes_accessed=4 << 20,
            transcendentals=0,
        ),
        name="inner",
    )(nbr, x, weights)


def outer_planes(nbr, info, near_ref, far_ref, part_ref, w_ref, out_ref):
    slots, _, rows, width = part_ref.shape
    edge = rows // (rows // 8)
    is_odd = info[0, 0] == 1
    for side, dx in enumerate((-1, 1)):
        use_near = is_odd if side == 0 else jnp.logical_not(is_odd)
        bricks = []
        for b in range(slots):

            def fetch(dy, dz):
                slot = nbr[b, tap(dx, dy, dz)]
                held = jnp.maximum(slot, 0)

                def load(r, n):
                    near = near_ref[held, r : r + n, :].astype(F32)
                    far = far_ref[held, r : r + n, :].astype(F32)
                    return jnp.where(use_near, near, far)[None]

                return jnp.where(slot >= 0, y_rows(load, dy, edge), 0.0)

            shifted = columns(fetch, edge)
            taps = []
            for first in range(3):
                for k in range(3):
                    piece = shifted[k][0, first : first + edge]
                    taps.append(piece.reshape(rows, width).astype(BF16))
            bricks.append(jnp.concatenate(taps, axis=1))
        count = 9 * width
        start = 0 if side == 0 else 2 * count
        extra = jnp.dot(
            jnp.concatenate(bricks, axis=0),
            w_ref[start : start + count],
            preferred_element_type=F32,
        ).reshape(slots, rows, width)
        plane = 0 if side == 0 else out_ref.shape[1] - 1
        for b in range(slots):
            total = part_ref[b, side] + extra[b]
            out_ref[b, plane] = jnp.maximum(total, 0.0).astype(BF16)


def outer_kernel(nbr, info, near_ref, far_ref, part_ref, w_ref, main_ref, out_ref):
    out_ref[:, 1 : out_ref.shape[1] - 1] = main_ref[:, 1 : out_ref.shape[1] - 1]
    outer_planes(nbr, info, near_ref, far_ref, part_ref, w_ref, out_ref)


def outer(main, part, near, far, nbr, info, weights):
    return pl.pallas_call(
        outer_kernel,
        out_shape=jax.ShapeDtypeStruct(main.shape, BF16),
        in_specs=[SMEM, SMEM, VMEM, VMEM, VMEM, VMEM, VMEM],
        out_specs=VMEM,
        compiler_params=PARAMS,
        name="outer",
    )(nbr, info, near, far, part, weights, main)


def outer_pool_kernel(
    nbr, info, parent, near_ref, far_ref, part_ref, w_ref, main_ref, out_ref, pool_ref, rim_ref, sums
):
    slots, edge, rows, width = out_ref.shape
    half = edge // 2
    out_ref[:, 1 : edge - 1] = main_ref[:, 1 : edge - 1]
    outer_planes(nbr, info, near_ref, far_ref, part_ref, w_ref, out_ref)
    cells = half**3
    for b in range(slots):
        value = out_ref[b].astype(F32).reshape(half, 2, half, 2, edge, width)
        value = (value[:, 0, :, 0] + value[:, 0, :, 1]) + (value[:, 1, :, 0] + value[:, 1, :, 1])
        sums[b] = value.reshape(half * half * edge, width)
        low = sums[b, pl.ds(0, cells, stride=2), :]
        high = sums[b, pl.ds(1, cells, stride=2), :]
        pooled = (low + high) * 0.125
        pool_ref[b * cells : (b + 1) * cells, :] = pooled.astype(BF16)
        outer_x = (jnp.maximum(parent[0, b], 0) >> 2) & 1
        rim = jnp.where(outer_x == 0, pooled[: cells // 2], pooled[cells // 2 :])
        rim_ref[b * cells // 2 : (b + 1) * cells // 2, :] = rim.astype(BF16)


def outer_pool(main, part, near, far, nbr, info, parent, weights):
    slots, edge, rows, width = main.shape
    cells = (edge // 2) ** 3
    return pl.pallas_call(
        outer_pool_kernel,
        out_shape=(
            jax.ShapeDtypeStruct(main.shape, BF16),
            jax.ShapeDtypeStruct((slots * cells, width), BF16),
            jax.ShapeDtypeStruct((slots * cells // 2, width), BF16),
        ),
        in_specs=[SMEM, SMEM, SMEM, VMEM, VMEM, VMEM, VMEM, VMEM],
        out_specs=(VMEM, VMEM, VMEM),
        scratch_shapes=[pltpu.VMEM((slots, 2 * cells, width), F32)],
        compiler_params=PARAMS,
        name="outer_pool",
    )(nbr, info, parent, near, far, part, weights, main)


def source_row(rel, device, lane_y, lane_c):
    c = device & 1
    flip_y = ((device >> 1) & 1) ^ lane_y
    same = flip_y * 2 + (c ^ lane_c)
    below = 4 + 4 * lane_c + flip_y * 2 + (1 - c)
    above = 8 - 4 * lane_c + flip_y * 2 + c
    return jnp.where(rel == 0, same, jnp.where(rel < 0, below, above))


def coarse_kernel(coarse_slots, *refs):
    table, parent, info, send = refs[:4]
    blocks = refs[4:12]
    enc_ref, w1_ref, w2_ref, out_ref, near_ref, far_ref = refs[12:18]
    held, region, even, odd, mid, even2, odd2, spread, base_s, gone_s, row_s, there_s = refs[18:]
    slots, edge, rows, width = enc_ref.shape
    half = edge // 2
    plane = half * half
    cells = half * plane
    position = info[0, 1]
    group = position >> 2
    lane_y = (position >> 1) & 1
    lane_c = position & 1

    first = 0
    for ref in blocks:
        held[first : first + ref.shape[0]] = ref[...].astype(F32)
        first += ref.shape[0]
    full_rows = LANES * slots * cells
    zero_row = first
    held[zero_row : zero_row + cells] = jnp.zeros((cells, width), F32)

    def place(b, carry):
        own = parent[0, b]
        known = own >= 0
        own = jnp.maximum(own, 0)
        octant = own & 7
        brick = own >> 3
        bits = ((octant >> 2) & 1, (octant >> 1) & 1, octant & 1)
        home = source_row(0, brick // coarse_slots, lane_y, lane_c)
        home_slot = brick % coarse_slots
        sign = tuple(2 * bit - 1 for bit in bits)
        for cross in range(8):
            crossed = (cross >> 2, (cross >> 1) & 1, cross & 1)
            number = 13
            for scale, s, c in zip((9, 3, 1), sign, crossed):
                if c:
                    number = number + scale * s
            found = table[home, 8 * coarse_slots + home_slot * 27 + number]
            there_s[cross] = jnp.where(known & (found >= 0), 1, 0)
            found = jnp.maximum(found, 0)
            device = found // coarse_slots
            rel = (device >> 2) - group
            row_s[cross] = source_row(rel, device, lane_y, lane_c) * coarse_slots + found % coarse_slots
        for ex in OFFSETS:
            for ey in OFFSETS:
                for ez in OFFSETS:
                    cross = 0
                    flip = 0
                    for scale, bit, e in zip((4, 2, 1), bits, (ex, ey, ez)):
                        if e:
                            cross = cross + scale * (bit if e > 0 else 1 - bit)
                            flip += scale
                    there = there_s[cross] == 1
                    row = row_s[cross]
                    column = (row % coarse_slots) * 8 + (octant ^ flip)
                    row = row // coarse_slots
                    child = table[row, column]
                    valid = there & (child >= 0)
                    child = jnp.maximum(child, 0)
                    device = child // slots
                    slot = child % slots
                    rel = (device >> 2) - group
                    source = source_row(rel, device, lane_y, lane_c)
                    whole = (source * slots + slot) * cells + (2 * plane if ex < 0 else 0)
                    rim = full_rows + ((source - 4) * slots + slot) * (cells // 2)
                    base = jnp.where(rel == 0, whole, rim)
                    base = jnp.where(valid, base, zero_row)
                    base = pl.multiple_of(base, 16)
                    gone_s[b, tap(ex, ey, ez)] = jnp.where(there, 0, 1)
                    size = {-1: (0, half - 2, 2), 0: (2, 0, half), 1: (half + 2, 0, 2)}
                    x0, _, nx = size[ex]
                    y0, sy, ny = size[ey]
                    z0, sz, nz = size[ez]
                    for x in range(nx):
                        for y in range(ny):
                            at = base + (x * plane + (sy + y) * half + sz)
                            region[b, x0 + x, y0 + y, z0 : z0 + nz, :] = held[pl.ds(at, nz), :]
        return carry

    lax.fori_loop(0, slots, place, 0)

    def spread_taps(source, even_ref, odd_ref, b, size):
        value = source.reshape(-1, edge, width)
        for k in range(3):
            moved = value if k == 0 else pltpu.roll(value, edge - k, 1)
            moved = moved.reshape(size, size, edge, width)
            even_ref[b, k] = moved.reshape(size, size * edge, width).astype(BF16)
            inside = moved[:, 1 : size - 1]
            odd_ref[b, k] = inside.reshape(size, (size - 2) * edge, width).astype(BF16)

    def gather_taps(even_ref, odd_ref, size):
        inside = size - 2
        bricks = []
        for b in range(slots):
            taps = []
            for dx in range(3):
                for dy in range(3):
                    for k in range(3):
                        if dy == 1:
                            piece = odd_ref[b, k, dx : dx + inside]
                        else:
                            piece = even_ref[
                                b, k, dx : dx + inside, dy * edge : (dy + inside) * edge
                            ]
                        taps.append(piece.reshape(inside * inside * edge, width))
            bricks.append(jnp.concatenate(taps, axis=1))
        return jnp.concatenate(bricks, axis=0)

    for b in range(slots):
        spread_taps(region[b], even, odd, b, edge)
    inside = edge - 2
    coarse = jnp.dot(gather_taps(even, odd, edge), w1_ref[...], preferred_element_type=F32)
    coarse = jnp.maximum(coarse, 0.0).astype(BF16).astype(F32)
    mid[...] = coarse.reshape(slots, inside, inside, edge, width)

    def clear(b, carry):
        span = {-1: (0, 1), 0: (1, half), 1: (half + 1, 1)}
        for ex in OFFSETS:
            for ey in OFFSETS:
                for ez in OFFSETS:
                    if (ex, ey, ez) == (0, 0, 0):
                        continue

                    @pl.when(gone_s[b, tap(ex, ey, ez)] == 1)
                    def _():
                        x0, nx = span[ex]
                        y0, ny = span[ey]
                        z0, nz = span[ez]
                        mid[b, x0 : x0 + nx, y0 : y0 + ny, z0 : z0 + nz, :] = jnp.zeros(
                            (nx, ny, nz, width), F32
                        )

        return carry

    lax.fori_loop(0, slots, clear, 0)
    for b in range(slots):
        spread_taps(mid[b], even2, odd2, b, inside)
    fine = jnp.dot(gather_taps(even2, odd2, inside), w2_ref[...], preferred_element_type=F32)
    fine = jnp.maximum(fine, 0.0).astype(BF16).astype(F32)
    fine = fine.reshape(slots, plane * edge, width)
    is_odd = lane_c == 1
    for b in range(slots):
        value = jnp.where(parent[0, b] >= 0, fine[b], 0.0)
        spread[b, pl.ds(0, plane * edge, stride=2), :] = value
        spread[b, pl.ds(1, plane * edge, stride=2), :] = value
        up = spread[b].reshape(half, half, 2 * edge, width)[:, :, :edge]
        base = enc_ref[b].astype(F32).reshape(half, 2, half, 2, edge, width)
        total = base + up[:, None, :, None]
        total = total.reshape(edge, rows, width).astype(BF16)
        out_ref[b] = total
        last = jnp.where(send[0, b] == b, total[edge - 1], 0)
        head = jnp.where(send[1, b] == b, total[0], 0)
        near_ref[b] = jnp.where(is_odd, head, last)
        far_ref[b] = jnp.where(is_odd, last, head)


def coarse(table, parent, info, send, blocks, enc, w1, w2, coarse_slots):
    slots, edge, rows, width = enc.shape
    half = edge // 2
    inside = edge - 2
    total = sum(block.shape[0] for block in blocks)
    face = jax.ShapeDtypeStruct((slots, rows, width), BF16)
    return pl.pallas_call(
        functools.partial(coarse_kernel, coarse_slots),
        out_shape=(jax.ShapeDtypeStruct(enc.shape, BF16), face, face),
        in_specs=[SMEM] * 4 + [VMEM] * 11,
        out_specs=(VMEM, VMEM, VMEM),
        scratch_shapes=[
            pltpu.VMEM((total + half**3, width), F32),
            pltpu.VMEM((slots, edge, edge, edge, width), F32),
            pltpu.VMEM((slots, 3, edge, edge * edge, width), BF16),
            pltpu.VMEM((slots, 3, edge, inside * edge, width), BF16),
            pltpu.VMEM((slots, inside, inside, edge, width), F32),
            pltpu.VMEM((slots, 3, inside, inside * edge, width), BF16),
            pltpu.VMEM((slots, 3, inside, half * edge, width), BF16),
            pltpu.VMEM((slots, 2 * half * half * edge, width), F32),
            pltpu.SMEM((slots, 27), jnp.int32),
            pltpu.SMEM((slots, 27), jnp.int32),
            pltpu.SMEM((8,), jnp.int32),
            pltpu.SMEM((8,), jnp.int32),
        ],
        compiler_params=PARAMS,
        name="coarse",
    )(table, parent, info, send, *blocks, enc, w1, w2)


def per_device(
    features,
    fine_nbr,
    fine_send,
    fine_parent,
    coarse_child,
    coarse_nbr,
    enc_fine_w,
    enc_coarse_w,
    dec_coarse_w,
    dec_fine_w,
):
    slots, edge, _, _, width = features.shape
    coarse_slots = coarse_nbr.shape[0]
    size = lax.axis_size("gx")
    position = lax.axis_index("gx")
    is_odd = position % 2

    def swap(value, partner):
        pairs = [(i, partner(i)) for i in range(size) if 0 <= partner(i) < size]
        return lax.ppermute(value, "gx", pairs)

    def core(value):
        return swap(value, lambda i: i ^ 1)

    def next_chip(value):
        return swap(value, lambda i: i + 1 if i % 2 else i - 1)

    def across_y(value):
        return swap(value, lambda i: i ^ 2)

    def across_z(value):
        return swap(value, lambda i: i + 3 if i % 2 else i - 3)

    x = features.reshape(slots, edge, edge * edge, width)
    flat = [w.reshape(27 * width, width) for w in (enc_fine_w, enc_coarse_w, dec_coarse_w, dec_fine_w)]
    info = jnp.stack([is_odd, position]).astype(jnp.int32).reshape(1, 2)
    parent = fine_parent.reshape(1, slots)
    send = fine_send[0]
    listed = (send == jnp.arange(slots, dtype=jnp.int32)[None, :])[:, :, None, None]
    last = jnp.where(listed[0], x[:, edge - 1], jnp.zeros((), BF16))
    head = jnp.where(listed[1], x[:, 0], jnp.zeros((), BF16))
    far = next_chip(jnp.where(is_odd == 1, last, head))
    near = core(jnp.where(is_odd == 1, head, last))
    main, part = inner(x, fine_nbr, flat[0])
    enc, pooled, rim = outer_pool(main, part, near, far, fine_nbr, info, parent, flat[0])

    table = jnp.concatenate([coarse_child.reshape(1, -1), coarse_nbr.reshape(1, -1)], axis=1)
    table_c = core(table)
    rim_c = core(rim)
    pooled_c = core(pooled)
    chip_table = jnp.concatenate([table, table_c], axis=0)
    rim_z = across_z(jnp.concatenate([rim, rim_c], axis=0))
    table_z = across_z(chip_table)
    pooled_y = across_y(pooled)
    rim_zy = across_y(rim_z)
    table_y = across_y(chip_table)
    table_zy = across_y(table_z)
    pooled_yc = core(pooled_y)
    rim_zc = core(rim_z)
    rim_zyc = core(rim_zy)
    z_table = jnp.concatenate([table_z, table_zy], axis=0)
    tables = jnp.concatenate([chip_table, table_y, z_table, core(z_table)], axis=0)
    blocks = [pooled, pooled_c, pooled_y, pooled_yc, rim_z, rim_zy, rim_zc, rim_zyc]
    dec_in, near_face, far_face = coarse(
        tables, parent, info, send, blocks, enc, flat[1], flat[2], coarse_slots
    )
    far = next_chip(far_face)
    near = core(near_face)
    main, part = inner(dec_in, fine_nbr, flat[3])
    out = outer(main, part, near, far, fine_nbr, info, flat[3])
    return out.reshape(features.shape)


def solution(mesh):
    placed = (
        P(("groups", "gx"), None, None, None, None),
        P(("groups", "gx"), None),
        P(("groups", "gx"), None, None),
        P(("groups", "gx")),
        P(("groups", "gx"), None),
        P(("groups", "gx"), None),
        P(),
        P(),
        P(),
        P(),
    )
    return jax.shard_map(
        per_device,
        mesh=mesh,
        in_specs=placed,
        out_specs=P(("groups", "gx"), None, None, None, None),
        check_vma=False,
    )
```

```python
import functools

import jax
import jax.numpy as jnp
from jax import lax
from jax.experimental import pallas as pl
from jax.experimental.pallas import tpu as pltpu
from jax.sharding import PartitionSpec as P

LANES = 4
GROUP = 1
CONV_GROUP = 4
TILE = 16
OFFSETS = (-1, 0, 1)
BF16 = jnp.bfloat16
F32 = jnp.float32
VMEM = pl.BlockSpec(memory_space=pltpu.VMEM)
SMEM = pl.BlockSpec(memory_space=pltpu.SMEM)
PARAMS = pltpu.CompilerParams(vmem_limit_bytes=16 << 20)


def tap(dx, dy, dz):
    return 9 * (dx + 1) + 3 * (dy + 1) + dz + 1


def z_shifts(center, below, above):
    edge = center.shape[1]
    z = lax.broadcasted_iota(jnp.int32, center.shape, 1)
    down = jnp.where(z == 0, pltpu.roll(below, 1, 1), pltpu.roll(center, 1, 1))
    up = jnp.where(z == edge - 1, pltpu.roll(above, edge - 1, 1), pltpu.roll(center, edge - 1, 1))
    return down, center, up


def columns(fetch, edge):
    parts = []
    for dy in OFFSETS:
        triple = [fetch(dy, dz) for dz in (0, -1, 1)]
        planes, rows, _, width = triple[0].shape
        flat = [v.reshape(planes * rows, edge, width) for v in triple]
        parts.append([s.reshape(planes, rows, edge, width) for s in z_shifts(*flat)])
    return [jnp.concatenate([part[k] for part in parts], axis=1) for k in range(3)]


def y_rows(load, dy, edge):
    if dy == 0:
        value = load(0, edge * edge)
    elif dy < 0:
        value = load(edge * edge - 2 * edge, 2 * edge)[:, edge:]
    else:
        value = load(0, 2 * edge)[:, :edge]
    planes, rows, width = value.shape
    return value.reshape(planes, rows // edge, edge, width)


def pair_weights(w_ref, dxs, width):
    zero = jnp.zeros((3 * width, width), BF16)
    blocks = []
    for dx in dxs:
        for j in range(4):
            sides = []
            for p in range(2):
                dy = j - p
                first = (9 * dx + 3 * dy) * width
                sides.append(w_ref[first : first + 3 * width] if 0 <= dy < 3 else zero)
            blocks.append(jnp.concatenate(sides, axis=1))
    return jnp.concatenate(blocks, axis=0)


def pair_rows(full, j, pairs):
    planes, _, edge, width = full.shape
    picked = jnp.concatenate([full[:, j + 2 * i : j + 2 * i + 1] for i in range(pairs)], axis=1)
    return picked.reshape(planes, pairs * edge, width).astype(BF16)


def unpair(total, planes, pairs, edge, width):
    sides = [
        total[:, p * width : (p + 1) * width].reshape(planes, pairs, 1, edge, width) for p in range(2)
    ]
    return jnp.concatenate(sides, axis=2).reshape(planes, 2 * pairs * edge, width)


def inner_kernel(nbr, x_ref, w_ref, out_ref, part_ref, cols):
    slots, edge, rows, width = x_ref.shape
    pairs = edge // 2
    empty = jnp.zeros((slots, 4, 3, pairs * edge, width), BF16)
    cols[:, :, :, 0] = empty
    cols[:, :, :, edge + 1] = empty
    weights = pair_weights(w_ref, range(3), width)
    for group in range(0, slots, GROUP):
        bricks = []
        for b in range(group, group + GROUP):

            def fetch(dy, dz):
                slot = nbr[b, tap(0, dy, dz)]
                held = jnp.maximum(slot, 0)
                value = y_rows(lambda r, n: x_ref[held, :, r : r + n, :].astype(F32), dy, edge)
                return jnp.where(slot >= 0, value, 0.0)

            for k, full in enumerate(columns(fetch, edge)):
                for j in range(4):
                    cols[b, j, k, 1 : edge + 1] = pair_rows(full, j, pairs)
            taps = []
            for dx in range(3):
                for j in range(4):
                    for k in range(3):
                        taps.append(
                            cols[b, j, k, dx : dx + edge].reshape(edge * pairs * edge, width)
                        )
            bricks.append(jnp.concatenate(taps, axis=1))
        totals = jnp.dot(
            jnp.concatenate(bricks, axis=0), weights, preferred_element_type=F32
        )
        count = edge * pairs * edge
        for i in range(GROUP):
            b = group + i
            total = unpair(totals[i * count : (i + 1) * count], edge, pairs, edge, width)
            out_ref[b] = jnp.maximum(total, 0.0).astype(BF16)
            part_ref[b, 0] = total[0]
            part_ref[b, 1] = total[edge - 1]


def inner(x, nbr, weights):
    slots, edge, rows, width = x.shape
    return pl.pallas_call(
        inner_kernel,
        out_shape=(
            jax.ShapeDtypeStruct(x.shape, BF16),
            jax.ShapeDtypeStruct((slots, 2, rows, width), F32),
        ),
        in_specs=[SMEM, VMEM, VMEM],
        out_specs=(VMEM, VMEM),
        scratch_shapes=[
            pltpu.VMEM((slots, 4, 3, edge + 2, rows // 2, width), BF16),
        ],
        compiler_params=PARAMS,
        cost_estimate=pl.CostEstimate(
            flops=2 * slots * edge * rows * 27 * width * width,
            bytes_accessed=4 << 20,
            transcendentals=0,
        ),
        name="inner",
    )(nbr, x, weights)


def outer_planes(nbr, info, near_ref, far_ref, part_ref, w_ref, out_ref):
    slots, _, rows, width = part_ref.shape
    edge = out_ref.shape[1]
    pairs = edge // 2
    is_odd = info[0, 0] == 1
    for side, dx in enumerate((-1, 1)):
        use_near = is_odd if side == 0 else jnp.logical_not(is_odd)
        bricks = []
        for b in range(slots):

            def fetch(dy, dz):
                slot = nbr[b, tap(dx, dy, dz)]
                held = jnp.maximum(slot, 0)

                def load(r, n):
                    near = near_ref[held, r : r + n, :].astype(F32)
                    far = far_ref[held, r : r + n, :].astype(F32)
                    return jnp.where(use_near, near, far)[None]

                return jnp.where(slot >= 0, y_rows(load, dy, edge), 0.0)

            shifted = columns(fetch, edge)
            taps = []
            for j in range(4):
                for k in range(3):
                    taps.append(pair_rows(shifted[k], j, pairs).reshape(rows // 2, width))
            bricks.append(jnp.concatenate(taps, axis=1))
        extra = jnp.dot(
            jnp.concatenate(bricks, axis=0),
            pair_weights(w_ref, [dx + 1], width),
            preferred_element_type=F32,
        )
        extra = unpair(extra, slots, pairs, edge, width)
        plane = 0 if side == 0 else out_ref.shape[1] - 1
        for b in range(slots):
            total = part_ref[b, side] + extra[b]
            out_ref[b, plane] = jnp.maximum(total, 0.0).astype(BF16)


def outer_kernel(nbr, info, near_ref, far_ref, part_ref, w_ref, main_ref, out_ref):
    out_ref[:, 1 : out_ref.shape[1] - 1] = main_ref[:, 1 : out_ref.shape[1] - 1]
    outer_planes(nbr, info, near_ref, far_ref, part_ref, w_ref, out_ref)


def outer(main, part, near, far, nbr, info, weights):
    return pl.pallas_call(
        outer_kernel,
        out_shape=jax.ShapeDtypeStruct(main.shape, BF16),
        in_specs=[SMEM, SMEM, VMEM, VMEM, VMEM, VMEM, VMEM],
        out_specs=VMEM,
        compiler_params=PARAMS,
        name="outer",
    )(nbr, info, near, far, part, weights, main)


def outer_pool_kernel(
    nbr, info, parent, near_ref, far_ref, part_ref, w_ref, main_ref, code_ref, out_ref, pool_ref, rim_ref, sums
):
    slots, edge, rows, width = out_ref.shape
    half = edge // 2
    out_ref[:, 1 : edge - 1] = main_ref[:, 1 : edge - 1]
    outer_planes(nbr, info, near_ref, far_ref, part_ref, w_ref, out_ref)
    cells = half**3
    pool_ref[slots * cells :] = code_ref[...]
    rim_ref[slots * cells // 2 :] = code_ref[...]
    for b in range(slots):
        value = out_ref[b].astype(F32).reshape(half, 2, half, 2, edge, width)
        value = (value[:, 0, :, 0] + value[:, 0, :, 1]) + (value[:, 1, :, 0] + value[:, 1, :, 1])
        sums[b] = value.reshape(half * half * edge, width)
        low = sums[b, pl.ds(0, cells, stride=2), :]
        high = sums[b, pl.ds(1, cells, stride=2), :]
        pooled = (low + high) * 0.125
        pool_ref[b * cells : (b + 1) * cells, :] = pooled.astype(BF16)
        outer_x = (jnp.maximum(parent[0, b], 0) >> 2) & 1
        rim = jnp.where(outer_x == 0, pooled[: cells // 2], pooled[cells // 2 :])
        rim_ref[b * cells // 2 : (b + 1) * cells // 2, :] = rim.astype(BF16)


def outer_pool(main, part, near, far, nbr, info, parent, weights, codes):
    slots, edge, rows, width = main.shape
    cells = (edge // 2) ** 3
    return pl.pallas_call(
        outer_pool_kernel,
        out_shape=(
            jax.ShapeDtypeStruct(main.shape, BF16),
            jax.ShapeDtypeStruct((slots * cells + TILE, width), BF16),
            jax.ShapeDtypeStruct((slots * cells // 2 + TILE, width), BF16),
        ),
        in_specs=[SMEM, SMEM, SMEM, VMEM, VMEM, VMEM, VMEM, VMEM, VMEM],
        out_specs=(VMEM, VMEM, VMEM),
        scratch_shapes=[pltpu.VMEM((slots, 2 * cells, width), F32)],
        compiler_params=PARAMS,
        name="outer_pool",
    )(nbr, info, parent, near, far, part, weights, main, codes)


def source_row(rel, device, lane_y, lane_c):
    c = device & 1
    flip_y = ((device >> 1) & 1) ^ lane_y
    same = flip_y * 2 + (c ^ lane_c)
    below = 4 + 4 * lane_c + flip_y * 2 + (1 - c)
    above = 8 - 4 * lane_c + flip_y * 2 + c
    return jnp.where(rel == 0, same, jnp.where(rel < 0, below, above))


def x_pair_weights(w_ref, width):
    count = 9 * width
    zero = jnp.zeros((count, width), BF16)
    blocks = []
    for j in range(4):
        sides = [w_ref[(j - p) * count : (j - p + 1) * count] if 0 <= j - p < 3 else zero for p in range(2)]
        blocks.append(jnp.concatenate(sides, axis=1))
    return jnp.concatenate(blocks, axis=0)


def valid_conv(values, weights, cols, edge, width):
    size = values[0].shape[0]
    inside = size - 2
    pairs = inside // 2
    even, odd = cols
    bricks = []
    for b, value in enumerate(values):
        flat = value.reshape(size * size, edge, width)
        for k in range(3):
            moved = flat if k == 0 else pltpu.roll(flat, edge - k, 1)
            moved = moved.reshape(size, size, edge, width)
            even[b, k] = moved.reshape(size, size * edge, width).astype(BF16)
            odd[b, k] = moved[:, 1 : size - 1].reshape(size, inside * edge, width).astype(BF16)
        taps = []
        for j in range(4):
            for dy in range(3):
                for k in range(3):
                    if dy == 1:
                        planes = [odd[b, k, j + 2 * i] for i in range(pairs)]
                    else:
                        rows = slice(dy * edge, (dy + inside) * edge)
                        planes = [even[b, k, j + 2 * i, rows] for i in range(pairs)]
                    taps.append(jnp.concatenate(planes, axis=0))
        bricks.append(jnp.concatenate(taps, axis=1))
    rows = inside * edge
    outs = []
    for first in range(0, len(values), CONV_GROUP):
        picked = bricks[first : first + CONV_GROUP]
        total = jnp.dot(jnp.concatenate(picked, axis=0), weights, preferred_element_type=F32)
        total = jnp.maximum(total, 0.0).astype(BF16).astype(F32)
        for i in range(len(picked)):
            one = total[i * pairs * rows : (i + 1) * pairs * rows]
            sides = [one[:, p * width : (p + 1) * width].reshape(pairs, 1, rows, width) for p in range(2)]
            outs.append(jnp.concatenate(sides, axis=1).reshape(inside, inside, edge, width))
    return outs


def coarse_kernel(
    coarse_slots, parent, info, send, own_ref, core_ref, big_ref, bigc_ref, enc_ref, w1_ref, w2_ref,
    out_ref, near_ref, far_ref, held, codes, even, odd, even2, odd2, spread, table, row_s, there_s, sem,
):
    slots, edge, rows, width = enc_ref.shape
    half = edge // 2
    plane = half * half
    cells = half * plane
    position = info[0, 1]
    lane_y = (position >> 1) & 1
    lane_c = position & 1
    whole_rows = slots * cells
    rim_rows = whole_rows // 2
    rim_at = [0, rim_rows + TILE, 2 * rim_rows + whole_rows + 3 * TILE]
    rim_at.append(rim_at[2] + rim_rows + TILE)
    whole_at = 2 * (rim_rows + TILE)
    places = [(own_ref, 0, whole_rows), (core_ref, 0, whole_rows)]
    places += [(ref, whole_at, whole_rows) for ref in (big_ref, bigc_ref)]
    places += [(ref, at, rim_rows) for ref in (big_ref, bigc_ref) for at in rim_at]
    for i, (ref, at, count) in enumerate(places):
        line = ref[at + count : at + count + TILE].astype(F32)[:1]
        codes[i : i + 1] = line.astype(jnp.int32)
    copy = pltpu.make_async_copy(codes, table, sem)
    copy.start()
    first = 0
    for ref, at, count in places:
        held[first : first + count] = ref[at : at + count]
        first += count
    zero_row = first
    held[zero_row:] = jnp.zeros((cells, width), BF16)
    full_rows = LANES * whole_rows
    copy.wait()

    row_of = lax.broadcasted_iota(jnp.int32, (1, edge, width), 1)
    from_above = (row_of & 2) == 0
    center = (row_of >= 2) & (row_of < half + 2)
    regions = []
    masks = []
    for b in range(slots):
        own = parent[0, b]
        known = own >= 0
        own = jnp.maximum(own, 0)
        octant = own & 7
        brick = own >> 3
        bits = ((octant >> 2) & 1, (octant >> 1) & 1, octant & 1)
        home = source_row(0, brick // coarse_slots, lane_y, lane_c)
        home_slot = brick % coarse_slots
        sign = tuple(2 * bit - 1 for bit in bits)
        for cross in range(8):
            crossed = (cross >> 2, (cross >> 1) & 1, cross & 1)
            number = 13
            for scale, s, c in zip((9, 3, 1), sign, crossed):
                if c:
                    number = number + scale * s
            found = table[home, 8 * coarse_slots + home_slot * 27 + number] - 1
            there = known & (found >= 0)
            there_s[b, cross] = jnp.where(there, 1, 0)
            found = jnp.maximum(found, 0)
            rel = found // (LANES * coarse_slots) - 1
            lane = found // coarse_slots % LANES
            start = found % coarse_slots * 8
            row = source_row(rel, lane, lane_y, lane_c)
            row_s[b, cross] = jnp.where(there, (rel + 1) * 65536 + row * 1024 + start, -1)

        def base_of(ex, ey, ez):
            cross = 0
            flip = 0
            for scale, bit, e in zip((4, 2, 1), bits, (ex, ey, ez)):
                if e:
                    cross = cross + scale * (bit if e > 0 else 1 - bit)
                    flip += scale
            entry = row_s[b, cross]
            there = entry >= 0
            entry = jnp.maximum(entry, 0)
            rel = (entry >> 16) - 1
            child = table[(entry >> 10) & 63, (entry & 1023) + (octant ^ flip)] - 1
            valid = there & (child >= 0)
            child = jnp.maximum(child, 0)
            source = source_row(rel, child // slots, lane_y, lane_c)
            slot = child % slots
            whole = (source * slots + slot) * cells + (2 * plane if ex < 0 else 0)
            rim = full_rows + ((source - LANES) * slots + slot) * (cells // 2)
            base = jnp.where(rel == 0, whole, rim)
            return pl.multiple_of(jnp.where(valid, base, zero_row), TILE)

        x_parts = []
        for ex in OFFSETS:
            planes = half if ex == 0 else 2
            y_parts = []
            for ey in OFFSETS:
                picked = []
                for ez in OFFSETS:
                    value = held[pl.ds(base_of(ex, ey, ez), planes * plane), :].astype(F32)
                    value = value.reshape(planes, 2, edge, width)
                    if ey < 0:
                        value = value[:, 1:]
                    elif ey > 0:
                        value = value[:, :1]
                    picked.append(value.reshape(-1, edge, width))
                sides = jnp.where(from_above, picked[2], picked[0])
                first_y = jnp.where(center, pltpu.roll(picked[1], 2, 1), pltpu.roll(sides, edge - 2, 1))
                second_y = jnp.where(center, pltpu.roll(picked[1], edge - 2, 1), pltpu.roll(sides, 2, 1))
                shape = (planes, -1, 1, edge, width)
                both = jnp.concatenate([first_y.reshape(shape), second_y.reshape(shape)], axis=2)
                y_parts.append(both.reshape(planes, -1, edge, width))
            x_parts.append(jnp.concatenate(y_parts, axis=1))
        regions.append(jnp.concatenate(x_parts, axis=0))
        at_edge = jnp.where(bits[2] == 1, half + 1, 0)
        kinds = []
        for ex in OFFSETS:
            for ey in OFFSETS:
                cross = 0
                for scale, bit, e in zip((4, 2), bits, (ex, ey)):
                    if e:
                        cross = cross + scale * (bit if e > 0 else 1 - bit)
                kinds.append(jnp.where(row_of == at_edge, there_s[b, cross + 1], there_s[b, cross]) == 1)
        masks.append(kinds)

    mids = []
    for value, kinds in zip(valid_conv(regions, x_pair_weights(w1_ref, width), (even, odd), edge, width), masks):
        spans = ((0, 1), (1, half + 1), (half + 1, half + 2))
        x_parts = []
        for i, (x0, x1) in enumerate(spans):
            y_parts = []
            for n, (y0, y1) in enumerate(spans):
                y_parts.append(jnp.where(kinds[3 * i + n][None], value[x0:x1, y0:y1], 0.0))
            x_parts.append(jnp.concatenate(y_parts, axis=1))
        mids.append(jnp.concatenate(x_parts, axis=0))
    fines = valid_conv(mids, x_pair_weights(w2_ref, width), (even2, odd2), edge, width)
    is_odd = lane_c == 1
    for b in range(slots):
        value = jnp.where(parent[0, b] >= 0, fines[b], 0.0).reshape(plane * edge, width)
        spread[b, pl.ds(0, plane * edge, stride=2), :] = value
        spread[b, pl.ds(1, plane * edge, stride=2), :] = value
        up = spread[b].reshape(half, half, 2 * edge, width)[:, :, :edge]
        base = enc_ref[b].astype(F32).reshape(half, 2, half, 2, edge, width)
        total = base + up[:, None, :, None]
        total = total.reshape(edge, rows, width).astype(BF16)
        out_ref[b] = total
        last = jnp.where(send[0, b] == b, total[edge - 1], 0)
        head = jnp.where(send[1, b] == b, total[0], 0)
        near_ref[b] = jnp.where(is_odd, head, last)
        far_ref[b] = jnp.where(is_odd, last, head)


def coarse(parent, info, send, blocks, enc, w1, w2, coarse_slots):
    slots, edge, rows, width = enc.shape
    half = edge // 2
    inside = edge - 2
    total = 2 * LANES * slots * half**3 + half**3
    face = jax.ShapeDtypeStruct((slots, rows, width), BF16)
    return pl.pallas_call(
        functools.partial(coarse_kernel, coarse_slots),
        out_shape=(jax.ShapeDtypeStruct(enc.shape, BF16), face, face),
        in_specs=[SMEM] * 3 + [VMEM] * 7,
        out_specs=(VMEM, VMEM, VMEM),
        scratch_shapes=[
            pltpu.VMEM((total, width), BF16),
            pltpu.VMEM((TILE, width), jnp.int32),
            pltpu.VMEM((slots, 3, edge, edge * edge, width), BF16),
            pltpu.VMEM((slots, 3, edge, inside * edge, width), BF16),
            pltpu.VMEM((slots, 3, inside, inside * edge, width), BF16),
            pltpu.VMEM((slots, 3, inside, half * edge, width), BF16),
            pltpu.VMEM((slots, 2 * half * half * edge, width), F32),
            pltpu.SMEM((TILE, width), jnp.int32),
            pltpu.SMEM((slots, 8), jnp.int32),
            pltpu.SMEM((slots, 8), jnp.int32),
            pltpu.SemaphoreType.DMA,
        ],
        compiler_params=PARAMS,
        name="coarse",
    )(parent, info, send, *blocks, enc, w1, w2)


def encode(coarse_child, coarse_nbr, position, slots, width):
    coarse_slots = coarse_nbr.shape[0]
    child = jnp.where(coarse_child >= 0, coarse_child % (LANES * slots) + 1, 0)
    first = (position // LANES - 1) * LANES * coarse_slots
    neighbour = jnp.where(coarse_nbr >= 0, coarse_nbr - first + 1, 0)
    line = jnp.concatenate([child.reshape(1, -1), neighbour.reshape(1, -1)], axis=1)
    line = jnp.pad(line, ((0, TILE - 1), (0, width - line.shape[1])))
    return line.astype(BF16)


def per_device(
    features,
    fine_nbr,
    fine_send,
    fine_parent,
    coarse_child,
    coarse_nbr,
    enc_fine_w,
    enc_coarse_w,
    dec_coarse_w,
    dec_fine_w,
):
    slots, edge, _, _, width = features.shape
    coarse_slots = coarse_nbr.shape[0]
    size = lax.axis_size("gx")
    position = lax.axis_index("gx")
    is_odd = position % 2

    def swap(value, partner):
        pairs = [(i, partner(i)) for i in range(size) if 0 <= partner(i) < size]
        return lax.ppermute(value, "gx", pairs)

    def core(value):
        return swap(value, lambda i: i ^ 1)

    def next_chip(value):
        return swap(value, lambda i: i + 1 if i % 2 else i - 1)

    def across_y(value):
        return swap(value, lambda i: i ^ 2)

    def across_z(value):
        return swap(value, lambda i: i + 3 if i % 2 else i - 3)

    x = features.reshape(slots, edge, edge * edge, width)
    flat = [w.reshape(27 * width, width) for w in (enc_fine_w, enc_coarse_w, dec_coarse_w, dec_fine_w)]
    info = jnp.stack([is_odd, position]).astype(jnp.int32).reshape(1, 2)
    parent = fine_parent.reshape(1, slots)
    send = fine_send[0]
    listed = (send == jnp.arange(slots, dtype=jnp.int32)[None, :])[:, :, None, None]
    last = jnp.where(listed[0], x[:, edge - 1], jnp.zeros((), BF16))
    head = jnp.where(listed[1], x[:, 0], jnp.zeros((), BF16))
    far = next_chip(jnp.where(is_odd == 1, last, head))
    near = core(jnp.where(is_odd == 1, head, last))
    codes = encode(coarse_child, coarse_nbr, position, slots, width)
    main, part = inner(x, fine_nbr, flat[0])
    enc, pooled, rim = outer_pool(main, part, near, far, fine_nbr, info, parent, flat[0], codes)

    rim_c = core(rim)
    pooled_c = core(pooled)
    rim_z = across_z(jnp.concatenate([rim, rim_c], axis=0))
    crossed = across_y(jnp.concatenate([pooled, rim_z], axis=0))
    big = jnp.concatenate([rim_z, crossed], axis=0)
    blocks = [pooled, pooled_c, big, core(big)]
    dec_in, near_face, far_face = coarse(
        parent, info, send, blocks, enc, flat[1], flat[2], coarse_slots
    )
    far = next_chip(far_face)
    near = core(near_face)
    main, part = inner(dec_in, fine_nbr, flat[3])
    out = outer(main, part, near, far, fine_nbr, info, flat[3])
    return out.reshape(features.shape)


def solution(mesh):
    placed = (
        P(("groups", "gx"), None, None, None, None),
        P(("groups", "gx"), None),
        P(("groups", "gx"), None, None),
        P(("groups", "gx")),
        P(("groups", "gx"), None),
        P(("groups", "gx"), None),
        P(),
        P(),
        P(),
        P(),
    )
    return jax.shard_map(
        per_device,
        mesh=mesh,
        in_specs=placed,
        out_specs=P(("groups", "gx"), None, None, None, None),
        check_vma=False,
    )
```

```python
import functools

import jax
import jax.numpy as jnp
from jax import lax
from jax.experimental import pallas as pl
from jax.experimental.pallas import tpu as pltpu
from jax.sharding import PartitionSpec as P


LANES = 4
GROUP = 1
CONV_GROUP = 4
TILE = 16
OFFSETS = (-1, 0, 1)
BF16 = jnp.bfloat16
F32 = jnp.float32
VMEM = pl.BlockSpec(memory_space=pltpu.VMEM)
SMEM = pl.BlockSpec(memory_space=pltpu.SMEM)
HBM = pl.BlockSpec(memory_space=pltpu.HBM)
PARAMS = pltpu.CompilerParams(vmem_limit_bytes=16 << 20)


def tap(dx, dy, dz):
    return 9 * (dx + 1) + 3 * (dy + 1) + dz + 1


def z_shifts(center, below, above):
    edge = center.shape[1]
    z = lax.broadcasted_iota(jnp.int32, center.shape, 1)
    down = jnp.where(z == 0, pltpu.roll(below, 1, 1), pltpu.roll(center, 1, 1))
    up = jnp.where(z == edge - 1, pltpu.roll(above, edge - 1, 1), pltpu.roll(center, edge - 1, 1))
    return down, center, up


def columns(fetch, edge):
    parts = []
    for dy in OFFSETS:
        triple = [fetch(dy, dz) for dz in (0, -1, 1)]
        planes, rows, _, width = triple[0].shape
        flat = [v.reshape(planes * rows, edge, width) for v in triple]
        parts.append([s.reshape(planes, rows, edge, width) for s in z_shifts(*flat)])
    return [jnp.concatenate([part[k] for part in parts], axis=1) for k in range(3)]


def y_rows(load, dy, edge):
    if dy == 0:
        value = load(0, edge * edge)
    elif dy < 0:
        value = load(edge * edge - 2 * edge, 2 * edge)[:, edge:]
    else:
        value = load(0, 2 * edge)[:, :edge]
    planes, rows, width = value.shape
    return value.reshape(planes, rows // edge, edge, width)


def pair_weights(w_ref, dxs, width):
    zero = jnp.zeros((3 * width, width), BF16)
    blocks = []
    for dx in dxs:
        for j in range(4):
            sides = []
            for p in range(2):
                dy = j - p
                first = (9 * dx + 3 * dy) * width
                sides.append(w_ref[first : first + 3 * width] if 0 <= dy < 3 else zero)
            blocks.append(jnp.concatenate(sides, axis=1))
    return jnp.concatenate(blocks, axis=0)


def pair_rows(full, j, pairs):
    planes, _, edge, width = full.shape
    picked = jnp.concatenate([full[:, j + 2 * i : j + 2 * i + 1] for i in range(pairs)], axis=1)
    return picked.reshape(planes, pairs * edge, width).astype(BF16)


def unpair(total, planes, pairs, edge, width):
    sides = [
        total[:, p * width : (p + 1) * width].reshape(planes, pairs, 1, edge, width) for p in range(2)
    ]
    return jnp.concatenate(sides, axis=2).reshape(planes, 2 * pairs * edge, width)


def first_kernel(
    info, x_hbm, nbr_hbm, send_hbm, parent_hbm, child_hbm, around_hbm,
    near_ref, far_ref, meta_ref, codes_ref,
    head_v, last_v, nbr_v, send_v, parent_v, child_v, around_v, numbers, sems,
):
    slots, edge, _, _ = x_hbm.shape
    coarse_slots = child_v.shape[0]
    pairs = [(x_hbm.at[:, 0], head_v), (x_hbm.at[:, edge - 1], last_v)]
    pairs += [(nbr_hbm, nbr_v), (send_hbm, send_v), (parent_hbm, parent_v)]
    pairs += [(child_hbm, child_v), (around_hbm, around_v)]
    copies = [pltpu.make_async_copy(*pair, sems.at[i]) for i, pair in enumerate(pairs)]
    for copy in copies:
        copy.start()
    for copy in copies:
        copy.wait()
    position = info[0, 0]
    meta_ref[...] = jnp.full(meta_ref.shape, position, jnp.int32)
    meta_ref[0:slots, 0:27] = nbr_v[...]
    meta_ref[slots : slots + 2, 0:slots] = send_v[...]
    meta_ref[slots + 2 : slots + 3, 0:slots] = parent_v[...]
    numbers[...] = jnp.zeros_like(numbers)
    child = child_v[...]
    numbers[0:coarse_slots, 0:8] = jnp.where(child >= 0, (child & (LANES * slots - 1)) + 1, 0)
    around = around_v[...]
    first = ((position >> 2) - 1) * LANES * coarse_slots
    numbers[coarse_slots : 2 * coarse_slots, 0:27] = jnp.where(around >= 0, around - first + 1, 0)
    codes_ref[...] = numbers[...].astype(F32).astype(BF16)
    is_odd = (position & 1) == 1
    send = send_v[...]
    slot_of = lax.broadcasted_iota(jnp.int32, send.shape, 1)
    listed = jnp.where(send == slot_of, 1.0, 0.0)
    for b in range(slots):
        last = last_v[b].astype(F32) * listed[0:1, b : b + 1]
        head = head_v[b].astype(F32) * listed[1:2, b : b + 1]
        near_ref[b] = jnp.where(is_odd, head, last).astype(BF16)
        far_ref[b] = jnp.where(is_odd, last, head).astype(BF16)


def stay(value):
    return pltpu.with_memory_space_constraint(value, pltpu.HBM)


def first(info, x, nbr, send, parent, child, around):
    slots, _, rows, width = x.shape
    coarse_slots = child.shape[0]
    assert 2 * coarse_slots <= TILE and (LANES * slots) & (LANES * slots - 1) == 0
    face = jax.ShapeDtypeStruct((slots, rows, width), BF16)
    return pl.pallas_call(
        first_kernel,
        out_shape=(
            face,
            face,
            jax.ShapeDtypeStruct((slots + 4, width), jnp.int32),
            jax.ShapeDtypeStruct((TILE, width), BF16),
        ),
        in_specs=[SMEM] + [HBM] * 6,
        out_specs=(VMEM,) * 4,
        scratch_shapes=[pltpu.VMEM((slots, rows, width), BF16)] * 2
        + [pltpu.VMEM(v.shape, jnp.int32) for v in (nbr, send, parent, child, around)]
        + [pltpu.VMEM((TILE, width), jnp.int32), pltpu.SemaphoreType.DMA((7,))],
        compiler_params=PARAMS,
        cost_estimate=pl.CostEstimate(flops=0, bytes_accessed=2097152, transcendentals=0),
        name="first",
    )(info, *[stay(v) for v in (x, nbr, send, parent, child, around)])


def loading_kernel(nbr, x_hbm, w_hbm, out_ref, part_ref, cols, x_ref, w_ref, sems):
    copies = [
        pltpu.make_async_copy(source, target, sems.at[i])
        for i, (source, target) in enumerate(((x_hbm, x_ref), (w_hbm, w_ref)))
    ]
    for copy in copies:
        copy.start()
    copies[0].wait()
    inner_kernel(nbr, x_ref, w_ref, out_ref, part_ref, cols, copies[1])


def inner_kernel(nbr, x_ref, w_ref, out_ref, part_ref, cols, waiting=None):
    slots, edge, _, width = x_ref.shape
    pairs = edge // 2
    empty = jnp.zeros((slots, 4, 3, pairs * edge, width), BF16)
    cols[:, :, :, 0] = empty
    cols[:, :, :, edge + 1] = empty
    for b in range(slots):
        def fetch(dy, dz):
            slot = nbr[b, tap(0, dy, dz)]
            held = jnp.maximum(slot, 0)
            value = y_rows(lambda r, n: x_ref[held, :, r : r + n, :].astype(F32), dy, edge)
            return jnp.where(slot >= 0, value, 0.0)

        for k, full in enumerate(columns(fetch, edge)):
            for j in range(4):
                cols[b, j, k, 1 : edge + 1] = pair_rows(full, j, pairs)
    if waiting is not None:
        waiting.wait()
    weights = pair_weights(w_ref, range(3), width)
    for group in range(0, slots, GROUP):
        bricks = []
        for b in range(group, group + GROUP):
            taps = []
            for dx in range(3):
                for j in range(4):
                    for k in range(3):
                        taps.append(
                            cols[b, j, k, dx : dx + edge].reshape(edge * pairs * edge, width)
                        )
            bricks.append(jnp.concatenate(taps, axis=1))
        totals = jnp.dot(
            jnp.concatenate(bricks, axis=0), weights, preferred_element_type=F32
        )
        count = edge * pairs * edge
        for i in range(GROUP):
            b = group + i
            total = unpair(totals[i * count : (i + 1) * count], edge, pairs, edge, width)
            out_ref[b] = jnp.maximum(total, 0.0).astype(BF16)
            part_ref[b, 0] = total[0]
            part_ref[b, 1] = total[edge - 1]


def inner(x, nbr, weights, load=False):
    slots, edge, rows, width = x.shape
    return pl.pallas_call(
        loading_kernel if load else inner_kernel,
        out_shape=(
            jax.ShapeDtypeStruct(x.shape, BF16),
            jax.ShapeDtypeStruct((slots, 2, rows, width), F32),
        ),
        in_specs=[SMEM] + [HBM if load else VMEM] * 2,
        out_specs=(VMEM, VMEM),
        scratch_shapes=[
            pltpu.VMEM((slots, 4, 3, edge + 2, rows // 2, width), BF16),
        ]
        + load
        * [pltpu.VMEM(x.shape, BF16), pltpu.VMEM(weights.shape, BF16), pltpu.SemaphoreType.DMA((2,))],
        compiler_params=PARAMS,
        cost_estimate=pl.CostEstimate(
            flops=2 * slots * edge * rows * 27 * width * width,
            bytes_accessed=4 << 20,
            transcendentals=0,
        ),
        name="inner",
    )(nbr, *([stay(x), stay(weights)] if load else [x, weights]))


def outer_planes(nbr, near_ref, far_ref, part_ref, w_ref, out_ref):
    slots, _, rows, width = part_ref.shape
    edge = out_ref.shape[1]
    pairs = edge // 2
    is_odd = (nbr[slots + 3, 0] & 1) == 1
    for side, dx in enumerate((-1, 1)):
        use_near = is_odd if side == 0 else jnp.logical_not(is_odd)
        bricks = []
        for b in range(slots):

            def fetch(dy, dz):
                slot = nbr[b, tap(dx, dy, dz)]
                held = jnp.maximum(slot, 0)

                def load(r, n):
                    near = near_ref[held, r : r + n, :].astype(F32)
                    far = far_ref[held, r : r + n, :].astype(F32)
                    return jnp.where(use_near, near, far)[None]

                return jnp.where(slot >= 0, y_rows(load, dy, edge), 0.0)

            shifted = columns(fetch, edge)
            taps = []
            for j in range(4):
                for k in range(3):
                    taps.append(pair_rows(shifted[k], j, pairs).reshape(rows // 2, width))
            bricks.append(jnp.concatenate(taps, axis=1))
        extra = jnp.dot(
            jnp.concatenate(bricks, axis=0),
            pair_weights(w_ref, [dx + 1], width),
            preferred_element_type=F32,
        )
        extra = unpair(extra, slots, pairs, edge, width)
        plane = 0 if side == 0 else out_ref.shape[1] - 1
        for b in range(slots):
            total = part_ref[b, side] + extra[b]
            out_ref[b, plane] = jnp.maximum(total, 0.0).astype(BF16)


def outer_kernel(nbr, near_ref, far_ref, part_ref, w_ref, main_ref, out_ref):
    out_ref[:, 1 : out_ref.shape[1] - 1] = main_ref[:, 1 : out_ref.shape[1] - 1]
    outer_planes(nbr, near_ref, far_ref, part_ref, w_ref, out_ref)


def outer(main, part, near, far, nbr, weights):
    return pl.pallas_call(
        outer_kernel,
        out_shape=jax.ShapeDtypeStruct(main.shape, BF16),
        in_specs=[SMEM, VMEM, VMEM, VMEM, VMEM, VMEM],
        out_specs=VMEM,
        compiler_params=PARAMS,
        cost_estimate=pl.CostEstimate(flops=536870912, bytes_accessed=4194304, transcendentals=0),
        name="outer",
    )(nbr, near, far, part, weights, main)


def outer_pool_kernel(
    nbr, near_ref, far_ref, part_ref, w_ref, main_ref, code_ref, out_ref, pool_ref, rim_ref, sums
):
    slots, edge, _, width = out_ref.shape
    half = edge // 2
    out_ref[:, 1 : edge - 1] = main_ref[:, 1 : edge - 1]
    outer_planes(nbr, near_ref, far_ref, part_ref, w_ref, out_ref)
    cells = half**3
    pool_ref[slots * cells :] = code_ref[...]
    rim_ref[slots * cells // 2 :] = code_ref[...]
    for b in range(slots):
        value = out_ref[b].astype(F32).reshape(half, 2, half, 2, edge, width)
        value = (value[:, 0, :, 0] + value[:, 0, :, 1]) + (value[:, 1, :, 0] + value[:, 1, :, 1])
        sums[b] = value.reshape(half * half * edge, width)
        low = sums[b, pl.ds(0, cells, stride=2), :]
        high = sums[b, pl.ds(1, cells, stride=2), :]
        pooled = (low + high) * 0.125
        pool_ref[b * cells : (b + 1) * cells, :] = pooled.astype(BF16)
        outer_x = (jnp.maximum(nbr[slots + 2, b], 0) >> 2) & 1
        rim = jnp.where(outer_x == 0, pooled[: cells // 2], pooled[cells // 2 :])
        rim_ref[b * cells // 2 : (b + 1) * cells // 2, :] = rim.astype(BF16)


def outer_pool(main, part, near, far, nbr, weights, codes):
    slots, edge, _, width = main.shape
    cells = (edge // 2) ** 3
    return pl.pallas_call(
        outer_pool_kernel,
        out_shape=(
            jax.ShapeDtypeStruct(main.shape, BF16),
            jax.ShapeDtypeStruct((slots * cells + TILE, width), BF16),
            jax.ShapeDtypeStruct((slots * cells // 2 + TILE, width), BF16),
        ),
        in_specs=[SMEM, VMEM, VMEM, VMEM, VMEM, VMEM, VMEM],
        out_specs=(VMEM, VMEM, VMEM),
        scratch_shapes=[pltpu.VMEM((slots, 2 * cells, width), F32)],
        compiler_params=PARAMS,
        cost_estimate=pl.CostEstimate(flops=536870912, bytes_accessed=4194304, transcendentals=0),
        name="outer_pool",
    )(nbr, near, far, part, weights, main, codes)


def source_row(rel, device, lane_y, lane_c):
    c = device & 1
    flip_y = ((device >> 1) & 1) ^ lane_y
    same = flip_y * 2 + (c ^ lane_c)
    below = 4 + 4 * lane_c + flip_y * 2 + (1 - c)
    above = 8 - 4 * lane_c + flip_y * 2 + c
    return jnp.where(rel == 0, same, jnp.where(rel < 0, below, above))


def x_pair_weights(w_ref, width):
    count = 9 * width
    zero = jnp.zeros((count, width), BF16)
    blocks = []
    for j in range(4):
        sides = [w_ref[(j - p) * count : (j - p + 1) * count] if 0 <= j - p < 3 else zero for p in range(2)]
        blocks.append(jnp.concatenate(sides, axis=1))
    return jnp.concatenate(blocks, axis=0)


def valid_conv(values, weights, cols, edge, width):
    size = values[0].shape[0]
    inside = size - 2
    pairs = inside // 2
    even, odd = cols
    bricks = []
    for b, value in enumerate(values):
        flat = value.reshape(size * size, edge, width)
        for k in range(3):
            moved = flat if k == 0 else pltpu.roll(flat, edge - k, 1)
            moved = moved.reshape(size, size, edge, width)
            even[b, k] = moved.reshape(size, size * edge, width).astype(BF16)
            odd[b, k] = moved[:, 1 : size - 1].reshape(size, inside * edge, width).astype(BF16)
        taps = []
        for j in range(4):
            for dy in range(3):
                for k in range(3):
                    if dy == 1:
                        planes = [odd[b, k, j + 2 * i] for i in range(pairs)]
                    else:
                        rows = slice(dy * edge, (dy + inside) * edge)
                        planes = [even[b, k, j + 2 * i, rows] for i in range(pairs)]
                    taps.append(jnp.concatenate(planes, axis=0))
        bricks.append(jnp.concatenate(taps, axis=1))
    rows = inside * edge
    outs = []
    for first in range(0, len(values), CONV_GROUP):
        picked = bricks[first : first + CONV_GROUP]
        total = jnp.dot(jnp.concatenate(picked, axis=0), weights, preferred_element_type=F32)
        total = jnp.maximum(total, 0.0).astype(BF16).astype(F32)
        for i in range(len(picked)):
            one = total[i * pairs * rows : (i + 1) * pairs * rows]
            sides = [one[:, p * width : (p + 1) * width].reshape(pairs, 1, rows, width) for p in range(2)]
            outs.append(jnp.concatenate(sides, axis=1).reshape(inside, inside, edge, width))
    return outs


def coarse_kernel(
    coarse_slots, meta, own_ref, core_ref, y_ref, yc_ref, big_ref, bigc_ref, enc_ref, w1_ref, w2_ref,
    out_ref, near_ref, far_ref, held, codes, even, odd, even2, odd2, spread, table, row_s, there_s, sem,
):
    slots, edge, rows, width = enc_ref.shape
    half = edge // 2
    plane = half * half
    cells = half * plane
    position = meta[slots + 3, 0]
    lane_y = (position >> 1) & 1
    lane_c = position & 1
    whole_rows = slots * cells
    rim_rows = whole_rows // 2
    rim_at = [i * (rim_rows + TILE) for i in range(4)]
    places = [(ref, 0, whole_rows) for ref in (own_ref, core_ref, y_ref, yc_ref)]
    places += [(ref, at, rim_rows) for ref in (big_ref, bigc_ref) for at in rim_at]
    lines = 2 * coarse_slots
    for i, (ref, at, count) in enumerate(places):
        line = ref[at + count : at + count + TILE].astype(F32)[:lines]
        codes[i * lines : (i + 1) * lines] = line.astype(jnp.int32)
    copy = pltpu.make_async_copy(codes, table, sem)
    copy.start()
    first = 0
    for ref, at, count in places:
        held[first : first + count] = ref[at : at + count]
        first += count
    zero_row = first
    held[zero_row:] = jnp.zeros((cells, width), BF16)
    full_rows = LANES * whole_rows
    copy.wait()

    row_of = lax.broadcasted_iota(jnp.int32, (1, edge, width), 1)
    from_above = (row_of & 2) == 0
    center = (row_of >= 2) & (row_of < half + 2)
    regions = []
    masks = []
    for b in range(slots):
        own = meta[slots + 2, b]
        known = own >= 0
        own = jnp.maximum(own, 0)
        octant = own & 7
        brick = own >> 3
        bits = ((octant >> 2) & 1, (octant >> 1) & 1, octant & 1)
        home = source_row(0, brick // coarse_slots, lane_y, lane_c)
        home_slot = brick % coarse_slots
        sign = tuple(2 * bit - 1 for bit in bits)
        for cross in range(8):
            crossed = (cross >> 2, (cross >> 1) & 1, cross & 1)
            number = 13
            for scale, s, c in zip((9, 3, 1), sign, crossed):
                if c:
                    number = number + scale * s
            found = table[home * lines + coarse_slots + home_slot, number] - 1
            there = known & (found >= 0)
            there_s[b, cross] = jnp.where(there, 1, 0)
            found = jnp.maximum(found, 0)
            rel = found // (LANES * coarse_slots) - 1
            lane = found // coarse_slots % LANES
            start = found % coarse_slots
            row = source_row(rel, lane, lane_y, lane_c)
            row_s[b, cross] = jnp.where(there, (rel + 1) * 65536 + row * lines + start, -1)

        def base_of(ex, ey, ez):
            cross = 0
            flip = 0
            for scale, bit, e in zip((4, 2, 1), bits, (ex, ey, ez)):
                if e:
                    cross = cross + scale * (bit if e > 0 else 1 - bit)
                    flip += scale
            entry = row_s[b, cross]
            there = entry >= 0
            entry = jnp.maximum(entry, 0)
            rel = (entry >> 16) - 1
            child = table[entry & 65535, octant ^ flip] - 1
            valid = there & (child >= 0)
            child = jnp.maximum(child, 0)
            source = source_row(rel, child // slots, lane_y, lane_c)
            slot = child % slots
            whole = (source * slots + slot) * cells + (2 * plane if ex < 0 else 0)
            rim = full_rows + ((source - LANES) * slots + slot) * (cells // 2)
            base = jnp.where(rel == 0, whole, rim)
            return pl.multiple_of(jnp.where(valid, base, zero_row), TILE)

        x_parts = []
        for ex in OFFSETS:
            planes = half if ex == 0 else 2
            y_parts = []
            for ey in OFFSETS:
                picked = []
                for ez in OFFSETS:
                    value = held[pl.ds(base_of(ex, ey, ez), planes * plane), :].astype(F32)
                    value = value.reshape(planes, 2, edge, width)
                    if ey < 0:
                        value = value[:, 1:]
                    elif ey > 0:
                        value = value[:, :1]
                    picked.append(value.reshape(-1, edge, width))
                sides = jnp.where(from_above, picked[2], picked[0])
                first_y = jnp.where(center, pltpu.roll(picked[1], 2, 1), pltpu.roll(sides, edge - 2, 1))
                second_y = jnp.where(center, pltpu.roll(picked[1], edge - 2, 1), pltpu.roll(sides, 2, 1))
                shape = (planes, -1, 1, edge, width)
                both = jnp.concatenate([first_y.reshape(shape), second_y.reshape(shape)], axis=2)
                y_parts.append(both.reshape(planes, -1, edge, width))
            x_parts.append(jnp.concatenate(y_parts, axis=1))
        regions.append(jnp.concatenate(x_parts, axis=0))
        at_edge = jnp.where(bits[2] == 1, half + 1, 0)
        kinds = []
        for ex in OFFSETS:
            for ey in OFFSETS:
                cross = 0
                for scale, bit, e in zip((4, 2), bits, (ex, ey)):
                    if e:
                        cross = cross + scale * (bit if e > 0 else 1 - bit)
                kinds.append(jnp.where(row_of == at_edge, there_s[b, cross + 1], there_s[b, cross]) == 1)
        masks.append(kinds)

    mids = []
    for value, kinds in zip(valid_conv(regions, x_pair_weights(w1_ref, width), (even, odd), edge, width), masks):
        spans = ((0, 1), (1, half + 1), (half + 1, half + 2))
        x_parts = []
        for i, (x0, x1) in enumerate(spans):
            y_parts = []
            for n, (y0, y1) in enumerate(spans):
                y_parts.append(jnp.where(kinds[3 * i + n][None], value[x0:x1, y0:y1], 0.0))
            x_parts.append(jnp.concatenate(y_parts, axis=1))
        mids.append(jnp.concatenate(x_parts, axis=0))
    fines = valid_conv(mids, x_pair_weights(w2_ref, width), (even2, odd2), edge, width)
    is_odd = lane_c == 1
    for b in range(slots):
        value = jnp.where(meta[slots + 2, b] >= 0, fines[b], 0.0).reshape(plane * edge, width)
        spread[b, pl.ds(0, plane * edge, stride=2), :] = value
        spread[b, pl.ds(1, plane * edge, stride=2), :] = value
        up = spread[b].reshape(half, half, 2 * edge, width)[:, :, :edge]
        base = enc_ref[b].astype(F32).reshape(half, 2, half, 2, edge, width)
        total = base + up[:, None, :, None]
        total = total.reshape(edge, rows, width).astype(BF16)
        out_ref[b] = total
        last = jnp.where(meta[slots, b] == b, total[edge - 1], 0)
        head = jnp.where(meta[slots + 1, b] == b, total[0], 0)
        near_ref[b] = jnp.where(is_odd, head, last)
        far_ref[b] = jnp.where(is_odd, last, head)


def coarse(meta, blocks, enc, w1, w2, coarse_slots):
    slots, edge, rows, width = enc.shape
    half = edge // 2
    inside = edge - 2
    total = 2 * LANES * slots * half**3 + half**3
    face = jax.ShapeDtypeStruct((slots, rows, width), BF16)
    return pl.pallas_call(
        functools.partial(coarse_kernel, coarse_slots),
        out_shape=(jax.ShapeDtypeStruct(enc.shape, BF16), face, face),
        in_specs=[SMEM] + [VMEM] * 9,
        out_specs=(VMEM, VMEM, VMEM),
        scratch_shapes=[
            pltpu.VMEM((total, width), BF16),
            pltpu.VMEM((3 * LANES * 2 * coarse_slots, width), jnp.int32),
            pltpu.VMEM((slots, 3, edge, edge * edge, width), BF16),
            pltpu.VMEM((slots, 3, edge, inside * edge, width), BF16),
            pltpu.VMEM((slots, 3, inside, inside * edge, width), BF16),
            pltpu.VMEM((slots, 3, inside, half * edge, width), BF16),
            pltpu.VMEM((slots, 2 * half * half * edge, width), F32),
            pltpu.SMEM((3 * LANES * 2 * coarse_slots, width), jnp.int32),
            pltpu.SMEM((slots, 8), jnp.int32),
            pltpu.SMEM((slots, 8), jnp.int32),
            pltpu.SemaphoreType.DMA,
        ],
        compiler_params=PARAMS,
        cost_estimate=pl.CostEstimate(flops=2147483648, bytes_accessed=8388608, transcendentals=0),
        name="coarse",
    )(meta, *blocks, enc, w1, w2)


def per_device(
    features,
    fine_nbr,
    fine_send,
    fine_parent,
    coarse_child,
    coarse_nbr,
    enc_fine_w,
    enc_coarse_w,
    dec_coarse_w,
    dec_fine_w,
):
    slots, edge, _, _, width = features.shape
    coarse_slots = coarse_nbr.shape[0]
    size = lax.axis_size("gx")
    position = lax.axis_index("gx")

    def swap(value, partner):
        pairs = [(i, partner(i)) for i in range(size) if 0 <= partner(i) < size]
        return lax.ppermute(value, "gx", pairs)

    def core(value):
        return swap(value, lambda i: i ^ 1)

    def next_chip(value):
        return swap(value, lambda i: i + 1 if i % 2 else i - 1)

    def across_y(value):
        return swap(value, lambda i: i ^ 2)

    def across_z(value):
        return swap(value, lambda i: i + 3 if i % 2 else i - 3)

    x = features.reshape(slots, edge, edge * edge, width)
    flat = [w.reshape(27 * width, width) for w in (enc_fine_w, enc_coarse_w, dec_coarse_w, dec_fine_w)]
    info = position.astype(jnp.int32).reshape(1, 1)
    near, far, meta, codes = first(
        info, x, fine_nbr, fine_send[0], fine_parent.reshape(1, slots), coarse_child, coarse_nbr
    )
    far = next_chip(far)
    near = core(near)
    main, part = inner(x, meta, flat[0], load=True)
    enc, pooled, rim = outer_pool(main, part, near, far, meta, flat[0], codes)

    rim_c = core(rim)
    rim_z = across_z(jnp.concatenate([rim, rim_c], axis=0))
    pooled_y = across_y(pooled)
    rim_zy = across_y(rim_z)
    big = jnp.concatenate([rim_z, rim_zy], axis=0)
    pooled_c = core(pooled)
    pooled_yc = core(pooled_y)
    big_c = core(big)
    blocks = [pooled, pooled_c, pooled_y, pooled_yc, big, big_c]
    dec_in, near, far = coarse(meta, blocks, enc, flat[1], flat[2], coarse_slots)
    far = next_chip(far)
    near = core(near)
    main, part = inner(dec_in, meta, flat[3])
    out = outer(main, part, near, far, meta, flat[3])
    return out.reshape(features.shape)


def solution(mesh):
    placed = (
        P(("groups", "gx"), None, None, None, None),
        P(("groups", "gx"), None),
        P(("groups", "gx"), None, None),
        P(("groups", "gx")),
        P(("groups", "gx"), None),
        P(("groups", "gx"), None),
        P(),
        P(),
        P(),
        P(),
    )
    return jax.shard_map(
        per_device,
        mesh=mesh,
        in_specs=placed,
        out_specs=P(("groups", "gx"), None, None, None, None),
        check_vma=False,
    )
```

```python
import functools

import jax
import jax.numpy as jnp
from jax import lax
from jax.experimental import pallas as pl
from jax.experimental.pallas import tpu as pltpu
from jax.sharding import PartitionSpec as P


LANES = 4
GROUP = 1
CONV_GROUP = 2
TILE = 16
OFFSETS = (-1, 0, 1)
BF16 = jnp.bfloat16
F32 = jnp.float32
VMEM = pl.BlockSpec(memory_space=pltpu.VMEM)
SMEM = pl.BlockSpec(memory_space=pltpu.SMEM)
HBM = pl.BlockSpec(memory_space=pltpu.HBM)
PARAMS = pltpu.CompilerParams(vmem_limit_bytes=16 << 20)


def tap(dx, dy, dz):
    return 9 * (dx + 1) + 3 * (dy + 1) + dz + 1


def z_shifts(center, below, above):
    edge = center.shape[1]
    z = lax.broadcasted_iota(jnp.int32, center.shape, 1)
    down = jnp.where(z == 0, pltpu.roll(below, 1, 1), pltpu.roll(center, 1, 1))
    up = jnp.where(z == edge - 1, pltpu.roll(above, edge - 1, 1), pltpu.roll(center, edge - 1, 1))
    return down, center, up


def columns(fetch, edge):
    parts = []
    for dy in OFFSETS:
        triple = [fetch(dy, dz) for dz in (0, -1, 1)]
        planes, rows, _, width = triple[0].shape
        flat = [v.reshape(planes * rows, edge, width) for v in triple]
        parts.append([s.reshape(planes, rows, edge, width) for s in z_shifts(*flat)])
    return [jnp.concatenate([part[k] for part in parts], axis=1) for k in range(3)]


def y_rows(load, dy, edge):
    if dy == 0:
        value = load(0, edge * edge)
    elif dy < 0:
        value = load(edge * edge - 2 * edge, 2 * edge)[:, edge:]
    else:
        value = load(0, 2 * edge)[:, :edge]
    planes, rows, width = value.shape
    return value.reshape(planes, rows // edge, edge, width)


def pair_weights(w_ref, dxs, width):
    zero = jnp.zeros((3 * width, width), BF16)
    blocks = []
    for dx in dxs:
        for j in range(4):
            sides = []
            for p in range(2):
                dy = j - p
                first = (9 * dx + 3 * dy) * width
                sides.append(w_ref[first : first + 3 * width] if 0 <= dy < 3 else zero)
            blocks.append(jnp.concatenate(sides, axis=1))
    return jnp.concatenate(blocks, axis=0)


def pair_rows(full, j, pairs):
    planes, _, edge, width = full.shape
    picked = jnp.concatenate([full[:, j + 2 * i : j + 2 * i + 1] for i in range(pairs)], axis=1)
    return picked.reshape(planes, pairs * edge, width).astype(BF16)


def unpair(total, planes, pairs, edge, width):
    sides = [
        total[:, p * width : (p + 1) * width].reshape(planes, pairs, 1, edge, width) for p in range(2)
    ]
    return jnp.concatenate(sides, axis=2).reshape(planes, 2 * pairs * edge, width)


def first_kernel(
    info, x_hbm, w_hbm, nbr_hbm, send_hbm, parent_hbm, child_hbm, around_hbm,
    near_ref, far_ref, meta_ref, codes_ref, x_ref, w_ref,
    head_v, last_v, nbr_v, send_v, parent_v, child_v, around_v, numbers, sems,
):
    slots, edge, _, _ = x_hbm.shape
    coarse_slots = child_v.shape[0]
    pairs = [(x_hbm.at[:, 0], head_v), (x_hbm.at[:, edge - 1], last_v)]
    pairs += [(nbr_hbm, nbr_v), (send_hbm, send_v), (parent_hbm, parent_v)]
    pairs += [(child_hbm, child_v), (around_hbm, around_v)]
    pairs += [(x_hbm, x_ref), (w_hbm, w_ref)]
    copies = [pltpu.make_async_copy(*pair, sems.at[i]) for i, pair in enumerate(pairs)]
    for copy in copies:
        copy.start()
    for copy in copies[:-2]:
        copy.wait()
    position = info[0, 0]
    meta_ref[...] = jnp.full(meta_ref.shape, position, jnp.int32)
    meta_ref[0:slots, 0:27] = nbr_v[...]
    meta_ref[slots : slots + 2, 0:slots] = send_v[...]
    meta_ref[slots + 2 : slots + 3, 0:slots] = parent_v[...]
    numbers[...] = jnp.zeros_like(numbers)
    child = child_v[...]
    numbers[0:coarse_slots, 0:8] = jnp.where(child >= 0, (child & (LANES * slots - 1)) + 1, 0)
    around = around_v[...]
    first = ((position >> 2) - 1) * LANES * coarse_slots
    numbers[coarse_slots : 2 * coarse_slots, 0:27] = jnp.where(around >= 0, around - first + 1, 0)
    codes_ref[...] = numbers[...].astype(F32).astype(BF16)
    is_odd = (position & 1) == 1
    send = send_v[...]
    slot_of = lax.broadcasted_iota(jnp.int32, send.shape, 1)
    listed = jnp.where(send == slot_of, 1.0, 0.0)
    for b in range(slots):
        last = last_v[b].astype(F32) * listed[0:1, b : b + 1]
        head = head_v[b].astype(F32) * listed[1:2, b : b + 1]
        near_ref[b] = jnp.where(is_odd, head, last).astype(BF16)
        far_ref[b] = jnp.where(is_odd, last, head).astype(BF16)
    for copy in copies[-2:]:
        copy.wait()


def stay(value):
    return pltpu.with_memory_space_constraint(value, pltpu.HBM)


def first(info, x, weights, nbr, send, parent, child, around):
    slots, _, rows, width = x.shape
    coarse_slots = child.shape[0]
    assert 2 * coarse_slots <= TILE and (LANES * slots) & (LANES * slots - 1) == 0
    face = jax.ShapeDtypeStruct((slots, rows, width), BF16)
    return pl.pallas_call(
        first_kernel,
        out_shape=(
            face,
            face,
            jax.ShapeDtypeStruct((slots + 4, width), jnp.int32),
            jax.ShapeDtypeStruct((TILE, width), BF16),
            jax.ShapeDtypeStruct(x.shape, BF16),
            jax.ShapeDtypeStruct(weights.shape, BF16),
        ),
        in_specs=[SMEM] + [HBM] * 7,
        out_specs=(VMEM,) * 6,
        scratch_shapes=[pltpu.VMEM((slots, rows, width), BF16)] * 2
        + [pltpu.VMEM(v.shape, jnp.int32) for v in (nbr, send, parent, child, around)]
        + [pltpu.VMEM((TILE, width), jnp.int32), pltpu.SemaphoreType.DMA((9,))],
        compiler_params=PARAMS,
        cost_estimate=pl.CostEstimate(flops=0, bytes_accessed=2097152, transcendentals=0),
        name="first",
    )(info, *[stay(v) for v in (x, weights, nbr, send, parent, child, around)])


def inner_kernel(nbr, x_ref, w_ref, out_ref, part_ref, cols):
    slots, edge, _, width = x_ref.shape
    pairs = edge // 2
    empty = jnp.zeros((slots, 4, 3, pairs * edge, width), BF16)
    cols[:, :, :, 0] = empty
    cols[:, :, :, edge + 1] = empty
    weights = pair_weights(w_ref, range(3), width)
    for group in range(0, slots, GROUP):
        bricks = []
        for b in range(group, group + GROUP):

            def fetch(dy, dz):
                slot = nbr[b, tap(0, dy, dz)]
                held = jnp.maximum(slot, 0)
                value = y_rows(lambda r, n: x_ref[held, :, r : r + n, :].astype(F32), dy, edge)
                return jnp.where(slot >= 0, value, 0.0)

            for k, full in enumerate(columns(fetch, edge)):
                for j in range(4):
                    cols[b, j, k, 1 : edge + 1] = pair_rows(full, j, pairs)
            taps = []
            for dx in range(3):
                for j in range(4):
                    for k in range(3):
                        taps.append(
                            cols[b, j, k, dx : dx + edge].reshape(edge * pairs * edge, width)
                        )
            bricks.append(jnp.concatenate(taps, axis=1))
        totals = jnp.dot(
            jnp.concatenate(bricks, axis=0), weights, preferred_element_type=F32
        )
        count = edge * pairs * edge
        for i in range(GROUP):
            b = group + i
            total = unpair(totals[i * count : (i + 1) * count], edge, pairs, edge, width)
            out_ref[b] = jnp.maximum(total, 0.0).astype(BF16)
            part_ref[b, 0] = total[0]
            part_ref[b, 1] = total[edge - 1]


def inner(x, nbr, weights):
    slots, edge, rows, width = x.shape
    return pl.pallas_call(
        inner_kernel,
        out_shape=(
            jax.ShapeDtypeStruct(x.shape, BF16),
            jax.ShapeDtypeStruct((slots, 2, rows, width), F32),
        ),
        in_specs=[SMEM, VMEM, VMEM],
        out_specs=(VMEM, VMEM),
        scratch_shapes=[
            pltpu.VMEM((slots, 4, 3, edge + 2, rows // 2, width), BF16),
        ],
        compiler_params=PARAMS,
        cost_estimate=pl.CostEstimate(
            flops=2 * slots * edge * rows * 27 * width * width,
            bytes_accessed=4 << 20,
            transcendentals=0,
        ),
        name="inner",
    )(nbr, x, weights)


def outer_planes(nbr, near_ref, far_ref, part_ref, w_ref, out_ref, edge):
    slots, _, rows, width = part_ref.shape
    pairs = edge // 2
    is_odd = (nbr[slots + 3, 0] & 1) == 1
    for side, dx in enumerate((-1, 1)):
        use_near = is_odd if side == 0 else jnp.logical_not(is_odd)
        bricks = []
        for b in range(slots):

            def fetch(dy, dz):
                slot = nbr[b, tap(dx, dy, dz)]
                held = jnp.maximum(slot, 0)

                def load(r, n):
                    near = near_ref[held, r : r + n, :].astype(F32)
                    far = far_ref[held, r : r + n, :].astype(F32)
                    return jnp.where(use_near, near, far)[None]

                return jnp.where(slot >= 0, y_rows(load, dy, edge), 0.0)

            shifted = columns(fetch, edge)
            taps = []
            for j in range(4):
                for k in range(3):
                    taps.append(pair_rows(shifted[k], j, pairs).reshape(rows // 2, width))
            bricks.append(jnp.concatenate(taps, axis=1))
        extra = jnp.dot(
            jnp.concatenate(bricks, axis=0),
            pair_weights(w_ref, [dx + 1], width),
            preferred_element_type=F32,
        )
        extra = unpair(extra, slots, pairs, edge, width)
        plane = 0 if side == 0 else out_ref.shape[1] - 1
        for b in range(slots):
            total = part_ref[b, side] + extra[b]
            out_ref[b, plane] = jnp.maximum(total, 0.0).astype(BF16)


def outer_kernel(nbr, near_ref, far_ref, part_ref, w_ref, main_ref, out_hbm, planes, sems):
    edge = main_ref.shape[1]
    inside = pltpu.make_async_copy(main_ref.at[:, 1 : edge - 1], out_hbm.at[:, 1 : edge - 1], sems.at[0])
    inside.start()
    outer_planes(nbr, near_ref, far_ref, part_ref, w_ref, planes, edge)
    copies = [
        pltpu.make_async_copy(planes.at[:, i], out_hbm.at[:, x], sems.at[i + 1])
        for i, x in enumerate((0, edge - 1))
    ]
    for copy in copies:
        copy.start()
    for copy in copies + [inside]:
        copy.wait()


def outer(main, part, near, far, nbr, weights):
    return pl.pallas_call(
        outer_kernel,
        out_shape=jax.ShapeDtypeStruct(main.shape, BF16),
        in_specs=[SMEM, VMEM, VMEM, VMEM, VMEM, VMEM],
        out_specs=HBM,
        scratch_shapes=[pltpu.VMEM(part.shape, BF16), pltpu.SemaphoreType.DMA((3,))],
        compiler_params=PARAMS,
        cost_estimate=pl.CostEstimate(flops=536870912, bytes_accessed=4194304, transcendentals=0),
        name="outer",
    )(nbr, near, far, part, weights, main)


def outer_pool_kernel(
    nbr, near_ref, far_ref, part_ref, w_ref, main_ref, code_ref, out_ref, pool_ref, rim_ref, sums
):
    slots, edge, _, width = out_ref.shape
    half = edge // 2
    out_ref[:, 1 : edge - 1] = main_ref[:, 1 : edge - 1]
    outer_planes(nbr, near_ref, far_ref, part_ref, w_ref, out_ref, edge)
    cells = half**3
    pool_ref[slots * cells :] = code_ref[...]
    rim_ref[slots * cells // 2 :] = code_ref[...]
    for b in range(slots):
        value = out_ref[b].astype(F32).reshape(half, 2, half, 2, edge, width)
        value = (value[:, 0, :, 0] + value[:, 0, :, 1]) + (value[:, 1, :, 0] + value[:, 1, :, 1])
        sums[b] = value.reshape(half * half * edge, width)
        low = sums[b, pl.ds(0, cells, stride=2), :]
        high = sums[b, pl.ds(1, cells, stride=2), :]
        pooled = (low + high) * 0.125
        pool_ref[b * cells : (b + 1) * cells, :] = pooled.astype(BF16)
        outer_x = (jnp.maximum(nbr[slots + 2, b], 0) >> 2) & 1
        rim = jnp.where(outer_x == 0, pooled[: cells // 2], pooled[cells // 2 :])
        rim_ref[b * cells // 2 : (b + 1) * cells // 2, :] = rim.astype(BF16)


def outer_pool(main, part, near, far, nbr, weights, codes):
    slots, edge, _, width = main.shape
    cells = (edge // 2) ** 3
    return pl.pallas_call(
        outer_pool_kernel,
        out_shape=(
            jax.ShapeDtypeStruct(main.shape, BF16),
            jax.ShapeDtypeStruct((slots * cells + TILE, width), BF16),
            jax.ShapeDtypeStruct((slots * cells // 2 + TILE, width), BF16),
        ),
        in_specs=[SMEM, VMEM, VMEM, VMEM, VMEM, VMEM, VMEM],
        out_specs=(VMEM, VMEM, VMEM),
        scratch_shapes=[pltpu.VMEM((slots, 2 * cells, width), F32)],
        compiler_params=PARAMS,
        cost_estimate=pl.CostEstimate(flops=536870912, bytes_accessed=4194304, transcendentals=0),
        name="outer_pool",
    )(nbr, near, far, part, weights, main, codes)


def x_pair_weights(w_ref, width):
    count = 9 * width
    zero = jnp.zeros((count, width), BF16)
    blocks = []
    for j in range(4):
        sides = [w_ref[(j - p) * count : (j - p + 1) * count] if 0 <= j - p < 3 else zero for p in range(2)]
        blocks.append(jnp.concatenate(sides, axis=1))
    return jnp.concatenate(blocks, axis=0)


def valid_conv(values, weights, cols, edge, width):
    size = values[0].shape[0]
    inside = size - 2
    pairs = inside // 2
    even, odd = cols
    bricks = []
    for b, value in enumerate(values):
        flat = value.reshape(size * size, edge, width)
        for k in range(3):
            moved = flat if k == 0 else pltpu.roll(flat, edge - k, 1)
            moved = moved.reshape(size, size, edge, width)
            even[b, k] = moved.reshape(size, size * edge, width).astype(BF16)
            odd[b, k] = moved[:, 1 : size - 1].reshape(size, inside * edge, width).astype(BF16)
        taps = []
        for j in range(4):
            for dy in range(3):
                for k in range(3):
                    if dy == 1:
                        planes = [odd[b, k, j + 2 * i] for i in range(pairs)]
                    else:
                        rows = slice(dy * edge, (dy + inside) * edge)
                        planes = [even[b, k, j + 2 * i, rows] for i in range(pairs)]
                    taps.append(jnp.concatenate(planes, axis=0))
        bricks.append(jnp.concatenate(taps, axis=1))
    rows = inside * edge
    outs = []
    for first in range(0, len(values), CONV_GROUP):
        picked = bricks[first : first + CONV_GROUP]
        total = jnp.dot(jnp.concatenate(picked, axis=0), weights, preferred_element_type=F32)
        total = jnp.maximum(total, 0.0).astype(BF16).astype(F32)
        for i in range(len(picked)):
            one = total[i * pairs * rows : (i + 1) * pairs * rows]
            sides = [one[:, p * width : (p + 1) * width].reshape(pairs, 1, rows, width) for p in range(2)]
            outs.append(jnp.concatenate(sides, axis=1).reshape(inside, inside, edge, width))
    return outs


def coarse_kernel(
    coarse_slots, meta, own_ref, core_ref, y_ref, yc_ref, big_ref, bigc_ref, enc_ref, w1_ref, w2_ref,
    out_ref, near_ref, far_ref, held, codes, even, odd, even2, odd2, spread, table, code_s, part_s, sem,
):
    slots, edge, rows, width = enc_ref.shape
    half = edge // 2
    plane = half * half
    cells = half * plane
    position = meta[slots + 3, 0]
    lane = position & (LANES - 1)
    group_bits = (LANES * coarse_slots).bit_length() - 1
    lane_c = position & 1
    whole_rows = slots * cells
    rim_rows = whole_rows // 2
    section = (LANES * slots + 1) * cells
    rim_at = [i * (rim_rows + TILE) for i in range(4)]
    places = [(ref, 0, whole_rows) for ref in (own_ref, core_ref, y_ref, yc_ref)]
    places += [(ref, at, rim_rows) for ref in (big_ref, bigc_ref) for at in rim_at]
    origins = [LANES + (lane ^ i) for i in range(LANES)]
    near_rel = jnp.where(lane_c == 1, 2 * LANES, 0)
    far_rel = 2 * LANES - near_rel
    origins += [near_rel + (lane ^ 1 ^ i) for i in range(LANES)]
    origins += [far_rel + (lane ^ i) for i in range(LANES)]
    lines = 3 * LANES * coarse_slots + 1
    codes[...] = jnp.zeros_like(codes)
    for origin, (ref, at, count) in zip(origins, places):
        line = ref[at + count : at + count + TILE].astype(F32).astype(jnp.int32)
        row = 1 + origin * coarse_slots
        codes[pl.ds(row, coarse_slots)] = line[:coarse_slots]
        codes[pl.ds(lines + row, coarse_slots)] = line[coarse_slots : 2 * coarse_slots]
    copy = pltpu.make_async_copy(codes, table, sem)
    copy.start()
    for i in range(4):
        held[i * section : i * section + cells] = jnp.zeros((cells, width), BF16)
    for i, (origin, (ref, at, count)) in enumerate(zip(origins, places)):
        if i < LANES:
            start = section + cells + origin * whole_rows
            start = pl.multiple_of(start + section - LANES * whole_rows, TILE)
            held[pl.ds(start, count)] = ref[at : at + count]
        else:
            group_start = jnp.where(origin >= LANES, 3 * section - 2 * LANES * whole_rows, section)
            start = group_start + cells + origin * whole_rows
            value = ref[at : at + count].reshape(slots, 1, cells // 2, width)
            start = pl.multiple_of(start, TILE)
            held[pl.ds(start, whole_rows)] = jnp.concatenate([value, value], axis=1).reshape(
                whole_rows, width
            )
    group_first = (position >> 2) * LANES * coarse_slots
    copy.wait()

    row_of = lax.broadcasted_iota(jnp.int32, (1, edge, width), 1)
    from_above = (row_of & 2) == 0
    center = (row_of >= 2) & (row_of < half + 2)
    regions = []
    masks = []
    for b in range(slots):
        own = jnp.where(meta[slots + 2, b] >= 0, meta[slots + 2, b], group_first * 8)
        octant = own & 7
        bits = ((octant >> 2) & 1, (octant >> 1) & 1, octant & 1)
        home = lines + 1 + LANES * coarse_slots + (own >> 3) - group_first
        steps = [scale * (2 * bit - 1) for scale, bit in zip((9, 3, 1), bits)]
        numbers = [13, 13 + steps[2]]
        numbers += [number + steps[1] for number in numbers]
        numbers += [number + steps[0] for number in numbers]
        for cross, number in enumerate(numbers):
            found = table[home, number]
            code_s[b, cross] = found
            part_s[b, cross] = ((found + LANES * coarse_slots - 1) >> group_bits) * section
        turns = [octant ^ flip for flip in range(8)]
        across = [{0: 0, 1: scale * bit, -1: scale * (1 - bit)} for scale, bit in zip((4, 2, 1), bits)]

        def base_of(ex, ey, ez):
            flip = 4 * abs(ex) + 2 * abs(ey) + abs(ez)
            cross = across[0][ex] + across[1][ey] + across[2][ez]
            child = table[code_s[b, cross], turns[flip]]
            base = part_s[b, cross] + child * cells
            return pl.multiple_of(base + (2 * plane if ex < 0 else 0), TILE)

        x_parts = []
        for ex in OFFSETS:
            planes = half if ex == 0 else 2
            y_parts = []
            for ey in OFFSETS:
                picked = []
                for ez in OFFSETS:
                    value = held[pl.ds(base_of(ex, ey, ez), planes * plane), :].astype(F32)
                    value = value.reshape(planes, 2, edge, width)
                    if ey < 0:
                        value = value[:, 1:]
                    elif ey > 0:
                        value = value[:, :1]
                    picked.append(value.reshape(-1, edge, width))
                sides = jnp.where(from_above, picked[2], picked[0])
                first_y = jnp.where(center, pltpu.roll(picked[1], 2, 1), pltpu.roll(sides, edge - 2, 1))
                second_y = jnp.where(center, pltpu.roll(picked[1], edge - 2, 1), pltpu.roll(sides, 2, 1))
                shape = (planes, -1, 1, edge, width)
                both = jnp.concatenate([first_y.reshape(shape), second_y.reshape(shape)], axis=2)
                y_parts.append(both.reshape(planes, -1, edge, width))
            x_parts.append(jnp.concatenate(y_parts, axis=1))
        regions.append(jnp.concatenate(x_parts, axis=0))
        at_edge = jnp.where(bits[2] == 1, half + 1, 0)
        kinds = []
        for ex in OFFSETS:
            for ey in OFFSETS:
                cross = across[0][ex] + across[1][ey]
                there = jnp.where(row_of == at_edge, code_s[b, cross + 1], code_s[b, cross])
                kinds.append(there > 0)
        masks.append(kinds)

    mids = []
    for value, kinds in zip(valid_conv(regions, x_pair_weights(w1_ref, width), (even, odd), edge, width), masks):
        spans = ((0, 1), (1, half + 1), (half + 1, half + 2))
        x_parts = []
        for i, (x0, x1) in enumerate(spans):
            y_parts = []
            for n, (y0, y1) in enumerate(spans):
                y_parts.append(jnp.where(kinds[3 * i + n][None], value[x0:x1, y0:y1], 0.0))
            x_parts.append(jnp.concatenate(y_parts, axis=1))
        mids.append(jnp.concatenate(x_parts, axis=0))
    fines = valid_conv(mids, x_pair_weights(w2_ref, width), (even2, odd2), edge, width)
    is_odd = lane_c == 1
    for b in range(slots):
        value = jnp.where(meta[slots + 2, b] >= 0, fines[b], 0.0).reshape(plane * edge, width)
        spread[b, pl.ds(0, plane * edge, stride=2), :] = value
        spread[b, pl.ds(1, plane * edge, stride=2), :] = value
        up = spread[b].reshape(half, half, 2 * edge, width)[:, :, :edge]
        base = enc_ref[b].astype(F32).reshape(half, 2, half, 2, edge, width)
        total = base + up[:, None, :, None]
        total = total.reshape(edge, rows, width).astype(BF16)
        out_ref[b] = total
        last = jnp.where(meta[slots, b] == b, total[edge - 1], 0)
        head = jnp.where(meta[slots + 1, b] == b, total[0], 0)
        near_ref[b] = jnp.where(is_odd, head, last)
        far_ref[b] = jnp.where(is_odd, last, head)


def coarse(meta, blocks, enc, w1, w2, coarse_slots):
    slots, edge, rows, width = enc.shape
    half = edge // 2
    inside = edge - 2
    total = 4 * (LANES * slots + 1) * half**3
    assert LANES * coarse_slots & (LANES * coarse_slots - 1) == 0
    lines = 2 * (3 * LANES * coarse_slots + 1)
    face = jax.ShapeDtypeStruct((slots, rows, width), BF16)
    return pl.pallas_call(
        functools.partial(coarse_kernel, coarse_slots),
        out_shape=(jax.ShapeDtypeStruct(enc.shape, BF16), face, face),
        in_specs=[SMEM] + [VMEM] * 9,
        out_specs=(VMEM, VMEM, VMEM),
        scratch_shapes=[
            pltpu.VMEM((total, width), BF16),
            pltpu.VMEM((lines, width), jnp.int32),
            pltpu.VMEM((slots, 3, edge, edge * edge, width), BF16),
            pltpu.VMEM((slots, 3, edge, inside * edge, width), BF16),
            pltpu.VMEM((slots, 3, inside, inside * edge, width), BF16),
            pltpu.VMEM((slots, 3, inside, half * edge, width), BF16),
            pltpu.VMEM((slots, 2 * half * half * edge, width), F32),
            pltpu.SMEM((lines, width), jnp.int32),
            pltpu.SMEM((slots, 8), jnp.int32),
            pltpu.SMEM((slots, 8), jnp.int32),
            pltpu.SemaphoreType.DMA,
        ],
        compiler_params=PARAMS,
        cost_estimate=pl.CostEstimate(flops=2147483648, bytes_accessed=8388608, transcendentals=0),
        name="coarse",
    )(meta, *blocks, enc, w1, w2)


def per_device(
    features,
    fine_nbr,
    fine_send,
    fine_parent,
    coarse_child,
    coarse_nbr,
    enc_fine_w,
    enc_coarse_w,
    dec_coarse_w,
    dec_fine_w,
):
    slots, edge, _, _, width = features.shape
    coarse_slots = coarse_nbr.shape[0]
    size = lax.axis_size("gx")
    position = lax.axis_index("gx")

    def swap(value, partner):
        pairs = [(i, partner(i)) for i in range(size) if 0 <= partner(i) < size]
        return lax.ppermute(value, "gx", pairs)

    def core(value):
        return swap(value, lambda i: i ^ 1)

    def next_chip(value):
        return swap(value, lambda i: i + 1 if i % 2 else i - 1)

    def across_y(value):
        return swap(value, lambda i: i ^ 2)

    def across_z(value):
        return swap(value, lambda i: i + 3 if i % 2 else i - 3)

    x = features.reshape(slots, edge, edge * edge, width)
    flat = [w.reshape(27 * width, width) for w in (enc_fine_w, enc_coarse_w, dec_coarse_w, dec_fine_w)]
    info = position.astype(jnp.int32).reshape(1, 1)
    near, far, meta, codes, x, first_w = first(
        info, x, flat[0], fine_nbr, fine_send[0], fine_parent.reshape(1, slots), coarse_child, coarse_nbr
    )
    far = next_chip(far)
    near = core(near)
    main, part = inner(x, meta, first_w)
    enc, pooled, rim = outer_pool(main, part, near, far, meta, first_w, codes)

    rim_c = core(rim)
    rim_z = across_z(jnp.concatenate([rim, rim_c], axis=0))
    pooled_y = across_y(pooled)
    rim_zy = across_y(rim_z)
    big = jnp.concatenate([rim_z, rim_zy], axis=0)
    pooled_c = core(pooled)
    pooled_yc = core(pooled_y)
    big_c = core(big)
    blocks = [pooled, pooled_c, pooled_y, pooled_yc, big, big_c]
    dec_in, near, far = coarse(meta, blocks, enc, flat[1], flat[2], coarse_slots)
    far = next_chip(far)
    near = core(near)
    main, part = inner(dec_in, meta, flat[3])
    out = outer(main, part, near, far, meta, flat[3])
    return out.reshape(features.shape)


def solution(mesh):
    placed = (
        P(("groups", "gx"), None, None, None, None),
        P(("groups", "gx"), None),
        P(("groups", "gx"), None, None),
        P(("groups", "gx")),
        P(("groups", "gx"), None),
        P(("groups", "gx"), None),
        P(),
        P(),
        P(),
        P(),
    )
    return jax.shard_map(
        per_device,
        mesh=mesh,
        in_specs=placed,
        out_specs=P(("groups", "gx"), None, None, None, None),
        check_vma=False,
    )
```

```python
import functools

import jax
import jax.numpy as jnp
from jax import lax
from jax.experimental import pallas as pl
from jax.experimental.pallas import tpu as pltpu
from jax.sharding import PartitionSpec as P


LANES = 4
GROUP = 2
ENC_GROUP = 1
DEC_GROUP = 4
TILE = 16
OFFSETS = (-1, 0, 1)
BF16 = jnp.bfloat16
F32 = jnp.float32
VMEM = pl.BlockSpec(memory_space=pltpu.VMEM)
SMEM = pl.BlockSpec(memory_space=pltpu.SMEM)
HBM = pl.BlockSpec(memory_space=pltpu.HBM)
PARAMS = pltpu.CompilerParams(vmem_limit_bytes=16 << 20)


def tap(dx, dy, dz):
    return 9 * (dx + 1) + 3 * (dy + 1) + dz + 1


def z_shifts(center, below, above):
    edge = center.shape[1]
    z = lax.broadcasted_iota(jnp.int32, center.shape, 1)
    down = jnp.where(z == 0, pltpu.roll(below, 1, 1), pltpu.roll(center, 1, 1))
    up = jnp.where(z == edge - 1, pltpu.roll(above, edge - 1, 1), pltpu.roll(center, edge - 1, 1))
    return down, center, up


def columns(fetch, edge):
    parts = []
    for dy in OFFSETS:
        triple = [fetch(dy, dz) for dz in (0, -1, 1)]
        planes, rows, _, width = triple[0].shape
        flat = [v.reshape(planes * rows, edge, width) for v in triple]
        parts.append([s.reshape(planes, rows, edge, width) for s in z_shifts(*flat)])
    return [jnp.concatenate([part[k] for part in parts], axis=1) for k in range(3)]


def y_rows(load, dy, edge):
    if dy == 0:
        value = load(0, edge * edge)
    elif dy < 0:
        value = load(edge * edge - 2 * edge, 2 * edge)[:, edge:]
    else:
        value = load(0, 2 * edge)[:, :edge]
    planes, rows, width = value.shape
    return value.reshape(planes, rows // edge, edge, width)


def pair_weights(w_ref, dxs, width):
    zero = jnp.zeros((3 * width, width), BF16)
    blocks = []
    for dx in dxs:
        for j in range(4):
            sides = []
            for p in range(2):
                dy = j - p
                first = (9 * dx + 3 * dy) * width
                sides.append(w_ref[first : first + 3 * width] if 0 <= dy < 3 else zero)
            blocks.append(jnp.concatenate(sides, axis=1))
    return jnp.concatenate(blocks, axis=0)


def pair_rows(full, j, pairs):
    planes, _, edge, width = full.shape
    picked = jnp.concatenate([full[:, j + 2 * i : j + 2 * i + 1] for i in range(pairs)], axis=1)
    return picked.reshape(planes, pairs * edge, width).astype(BF16)


def unpair(total, planes, pairs, edge, width):
    sides = [
        total[:, p * width : (p + 1) * width].reshape(planes, pairs, 1, edge, width) for p in range(2)
    ]
    return jnp.concatenate(sides, axis=2).reshape(planes, 2 * pairs * edge, width)


def first_kernel(
    info, x_hbm, w_hbm, nbr_hbm, send_hbm, parent_hbm, child_hbm, around_hbm,
    near_ref, far_ref, meta_ref, codes_ref, x_ref, w_ref,
    head_v, last_v, nbr_v, send_v, parent_v, child_v, around_v, numbers, sems,
):
    slots, edge, _, _ = x_hbm.shape
    coarse_slots = child_v.shape[0]
    pairs = [(x_hbm.at[:, 0], head_v), (x_hbm.at[:, edge - 1], last_v)]
    pairs += [(nbr_hbm, nbr_v), (send_hbm, send_v), (parent_hbm, parent_v)]
    pairs += [(child_hbm, child_v), (around_hbm, around_v)]
    pairs += [(x_hbm, x_ref), (w_hbm, w_ref)]
    copies = [pltpu.make_async_copy(*pair, sems.at[i]) for i, pair in enumerate(pairs)]
    for copy in copies:
        copy.start()
    for copy in copies[:-2]:
        copy.wait()
    position = info[0, 0]
    meta_ref[...] = jnp.full(meta_ref.shape, position, jnp.int32)
    meta_ref[0:slots, 0:27] = nbr_v[...]
    meta_ref[slots : slots + 2, 0:slots] = send_v[...]
    meta_ref[slots + 2 : slots + 3, 0:slots] = parent_v[...]
    numbers[...] = jnp.zeros_like(numbers)
    child = child_v[...]
    numbers[0:coarse_slots, 0:8] = jnp.where(child >= 0, (child & (LANES * slots - 1)) + 1, 0)
    around = around_v[...]
    first = ((position >> 2) - 1) * LANES * coarse_slots
    place = around - first
    inside = (around >= 0) & (place >= 0) & (place < 3 * LANES * coarse_slots)
    numbers[coarse_slots : 2 * coarse_slots, 0:27] = jnp.where(inside, place + 1, 0)
    codes_ref[...] = numbers[...].astype(F32).astype(BF16)
    is_odd = (position & 1) == 1
    send = send_v[...]
    slot_of = lax.broadcasted_iota(jnp.int32, send.shape, 1)
    listed = jnp.where(send == slot_of, 1.0, 0.0)
    for b in range(slots):
        last = last_v[b].astype(F32) * listed[0:1, b : b + 1]
        head = head_v[b].astype(F32) * listed[1:2, b : b + 1]
        near_ref[b] = jnp.where(is_odd, head, last).astype(BF16)
        far_ref[b] = jnp.where(is_odd, last, head).astype(BF16)
    for copy in copies[-2:]:
        copy.wait()


def stay(value):
    return pltpu.with_memory_space_constraint(value, pltpu.HBM)


def first(info, x, weights, nbr, send, parent, child, around):
    slots, _, rows, width = x.shape
    coarse_slots = child.shape[0]
    assert 2 * coarse_slots <= TILE and (LANES * slots) & (LANES * slots - 1) == 0
    face = jax.ShapeDtypeStruct((slots, rows, width), BF16)
    return pl.pallas_call(
        first_kernel,
        out_shape=(
            face,
            face,
            jax.ShapeDtypeStruct((slots + 4, width), jnp.int32),
            jax.ShapeDtypeStruct((TILE, width), BF16),
            jax.ShapeDtypeStruct(x.shape, BF16),
            jax.ShapeDtypeStruct(weights.shape, BF16),
        ),
        in_specs=[SMEM] + [HBM] * 7,
        out_specs=(VMEM,) * 6,
        scratch_shapes=[pltpu.VMEM((slots, rows, width), BF16)] * 2
        + [pltpu.VMEM(v.shape, jnp.int32) for v in (nbr, send, parent, child, around)]
        + [pltpu.VMEM((TILE, width), jnp.int32), pltpu.SemaphoreType.DMA((9,))],
        compiler_params=PARAMS,
        cost_estimate=pl.CostEstimate(flops=0, bytes_accessed=2097152, transcendentals=0),
        name="first",
    )(info, *[stay(v) for v in (x, weights, nbr, send, parent, child, around)])


def inner_kernel(nbr, x_ref, w_ref, out_ref, part_ref, cols):
    slots, edge, _, width = x_ref.shape
    pairs = edge // 2
    empty = jnp.zeros((slots, 4, 3, pairs * edge, width), BF16)
    cols[:, :, :, 0] = empty
    cols[:, :, :, edge + 1] = empty
    weights = pair_weights(w_ref, range(3), width)
    for group in range(0, slots, GROUP):
        bricks = []
        for b in range(group, group + GROUP):

            def fetch(dy, dz):
                slot = nbr[b, tap(0, dy, dz)]
                held = jnp.maximum(slot, 0)
                value = y_rows(lambda r, n: x_ref[held, :, r : r + n, :].astype(F32), dy, edge)
                return jnp.where(slot >= 0, value, 0.0)

            for k, full in enumerate(columns(fetch, edge)):
                for j in range(4):
                    cols[b, j, k, 1 : edge + 1] = pair_rows(full, j, pairs)
            taps = []
            for dx in range(3):
                for j in range(4):
                    for k in range(3):
                        taps.append(
                            cols[b, j, k, dx : dx + edge].reshape(edge * pairs * edge, width)
                        )
            bricks.append(jnp.concatenate(taps, axis=1))
        totals = jnp.dot(
            jnp.concatenate(bricks, axis=0), weights, preferred_element_type=F32
        )
        count = edge * pairs * edge
        for i in range(GROUP):
            b = group + i
            total = unpair(totals[i * count : (i + 1) * count], edge, pairs, edge, width)
            out_ref[b] = jnp.maximum(total, 0.0).astype(BF16)
            part_ref[b, 0] = total[0]
            part_ref[b, 1] = total[edge - 1]


def inner(x, nbr, weights):
    slots, edge, rows, width = x.shape
    return pl.pallas_call(
        inner_kernel,
        out_shape=(
            jax.ShapeDtypeStruct(x.shape, BF16),
            jax.ShapeDtypeStruct((slots, 2, rows, width), F32),
        ),
        in_specs=[SMEM, VMEM, VMEM],
        out_specs=(VMEM, VMEM),
        scratch_shapes=[
            pltpu.VMEM((slots, 4, 3, edge + 2, rows // 2, width), BF16),
        ],
        compiler_params=PARAMS,
        cost_estimate=pl.CostEstimate(
            flops=2 * slots * edge * rows * 27 * width * width,
            bytes_accessed=4 << 20,
            transcendentals=0,
        ),
        name="inner",
    )(nbr, x, weights)


def outer_planes(nbr, near_ref, far_ref, part_ref, w_ref, out_ref, stack, edge):
    slots, _, rows, width = part_ref.shape
    pairs = edge // 2
    is_odd = nbr[slots + 3, 0] & 1
    stack[:slots] = near_ref[...].astype(F32)
    stack[slots : 2 * slots] = far_ref[...].astype(F32)
    stack[2 * slots] = jnp.zeros((rows, width), F32)
    for side, dx in enumerate((-1, 1)):
        offset = slots * (1 - is_odd if side == 0 else is_odd)
        bricks = []
        for b in range(slots):

            def fetch(dy, dz):
                slot = nbr[b, tap(dx, dy, dz)]
                held = jnp.where(slot >= 0, slot + offset, 2 * slots)
                first, count = {-1: (edge - 1, 1), 0: (0, edge), 1: (0, 1)}[dy]
                value = stack[held, first * edge : (first + count) * edge]
                return value.reshape(1, count, edge, width)

            shifted = columns(fetch, edge)
            taps = []
            for j in range(4):
                for k in range(3):
                    taps.append(pair_rows(shifted[k], j, pairs).reshape(rows // 2, width))
            bricks.append(jnp.concatenate(taps, axis=1))
        extra = jnp.dot(
            jnp.concatenate(bricks, axis=0),
            pair_weights(w_ref, [dx + 1], width),
            preferred_element_type=F32,
        )
        extra = unpair(extra, slots, pairs, edge, width)
        plane = 0 if side == 0 else out_ref.shape[1] - 1
        for b in range(slots):
            total = part_ref[b, side] + extra[b]
            out_ref[b, plane] = jnp.maximum(total, 0.0).astype(BF16)


def outer_kernel(nbr, near_ref, far_ref, part_ref, w_ref, main_ref, out_hbm, planes, stack, sems):
    edge = main_ref.shape[1]
    inside = pltpu.make_async_copy(main_ref.at[:, 1 : edge - 1], out_hbm.at[:, 1 : edge - 1], sems.at[0])
    inside.start()
    outer_planes(nbr, near_ref, far_ref, part_ref, w_ref, planes, stack, edge)
    copies = [
        pltpu.make_async_copy(planes.at[:, i], out_hbm.at[:, x], sems.at[i + 1])
        for i, x in enumerate((0, edge - 1))
    ]
    for copy in copies:
        copy.start()
    for copy in copies + [inside]:
        copy.wait()


def outer(main, part, near, far, nbr, weights):
    return pl.pallas_call(
        outer_kernel,
        out_shape=jax.ShapeDtypeStruct(main.shape, BF16),
        in_specs=[SMEM, VMEM, VMEM, VMEM, VMEM, VMEM],
        out_specs=HBM,
        scratch_shapes=[
            pltpu.VMEM(part.shape, BF16),
            pltpu.VMEM((2 * main.shape[0] + 1,) + main.shape[2:], F32),
            pltpu.SemaphoreType.DMA((3,)),
        ],
        compiler_params=PARAMS,
        cost_estimate=pl.CostEstimate(flops=536870912, bytes_accessed=4194304, transcendentals=0),
        name="outer",
    )(nbr, near, far, part, weights, main)


def outer_pool_kernel(
    nbr, near_ref, far_ref, part_ref, w_ref, main_ref, code_ref, out_ref, pool_ref, rim_ref, sums, stack
):
    slots, edge, _, width = out_ref.shape
    half = edge // 2
    out_ref[:, 1 : edge - 1] = main_ref[:, 1 : edge - 1]
    outer_planes(nbr, near_ref, far_ref, part_ref, w_ref, out_ref, stack, edge)
    cells = half**3
    pool_ref[slots * cells :] = code_ref[...]
    rim_ref[slots * cells // 2 :] = code_ref[...]
    for b in range(slots):
        value = out_ref[b].astype(F32).reshape(half, 2, half, 2, edge, width)
        value = (value[:, 0, :, 0] + value[:, 0, :, 1]) + (value[:, 1, :, 0] + value[:, 1, :, 1])
        sums[b] = value.reshape(half * half * edge, width)
        low = sums[b, pl.ds(0, cells, stride=2), :]
        high = sums[b, pl.ds(1, cells, stride=2), :]
        pooled = (low + high) * 0.125
        pool_ref[b * cells : (b + 1) * cells, :] = pooled.astype(BF16)
        outer_x = (jnp.maximum(nbr[slots + 2, b], 0) >> 2) & 1
        rim = jnp.where(outer_x == 0, pooled[: cells // 2], pooled[cells // 2 :])
        rim_ref[b * cells // 2 : (b + 1) * cells // 2, :] = rim.astype(BF16)


def outer_pool(main, part, near, far, nbr, weights, codes):
    slots, edge, rows, width = main.shape
    cells = (edge // 2) ** 3
    return pl.pallas_call(
        outer_pool_kernel,
        out_shape=(
            jax.ShapeDtypeStruct(main.shape, BF16),
            jax.ShapeDtypeStruct((slots * cells + TILE, width), BF16),
            jax.ShapeDtypeStruct((slots * cells // 2 + TILE, width), BF16),
        ),
        in_specs=[SMEM, VMEM, VMEM, VMEM, VMEM, VMEM, VMEM],
        out_specs=(VMEM, VMEM, VMEM),
        scratch_shapes=[
            pltpu.VMEM((slots, 2 * cells, width), F32),
            pltpu.VMEM((2 * slots + 1, rows, width), F32),
        ],
        compiler_params=PARAMS,
        cost_estimate=pl.CostEstimate(flops=536870912, bytes_accessed=4194304, transcendentals=0),
        name="outer_pool",
    )(nbr, near, far, part, weights, main, codes)


def x_pair_weights(w_ref, width):
    count = 9 * width
    zero = jnp.zeros((count, width), BF16)
    blocks = []
    for j in range(4):
        sides = [w_ref[(j - p) * count : (j - p + 1) * count] if 0 <= j - p < 3 else zero for p in range(2)]
        blocks.append(jnp.concatenate(sides, axis=1))
    return jnp.concatenate(blocks, axis=0)


def valid_conv(values, weights, cols, edge, width, group):
    size = values[0].shape[0]
    inside = size - 2
    pairs = inside // 2
    even, odd = cols
    bricks = []
    for b, value in enumerate(values):
        flat = value.reshape(size * size, edge, width)
        for k in range(3):
            moved = flat if k == 0 else pltpu.roll(flat, edge - k, 1)
            moved = moved.reshape(size, size, edge, width)
            even[b, k] = moved.reshape(size, size * edge, width).astype(BF16)
            odd[b, k] = moved[:, 1 : size - 1].reshape(size, inside * edge, width).astype(BF16)
        taps = []
        for j in range(4):
            for dy in range(3):
                for k in range(3):
                    if dy == 1:
                        planes = [odd[b, k, j + 2 * i] for i in range(pairs)]
                    else:
                        rows = slice(dy * edge, (dy + inside) * edge)
                        planes = [even[b, k, j + 2 * i, rows] for i in range(pairs)]
                    taps.append(jnp.concatenate(planes, axis=0))
        bricks.append(jnp.concatenate(taps, axis=1))
    rows = inside * edge
    outs = []
    for first in range(0, len(values), group):
        picked = bricks[first : first + group]
        total = jnp.dot(jnp.concatenate(picked, axis=0), weights, preferred_element_type=F32)
        total = jnp.maximum(total, 0.0).astype(BF16).astype(F32)
        for i in range(len(picked)):
            one = total[i * pairs * rows : (i + 1) * pairs * rows]
            sides = [one[:, p * width : (p + 1) * width].reshape(pairs, 1, rows, width) for p in range(2)]
            outs.append(jnp.concatenate(sides, axis=1).reshape(inside, inside, edge, width))
    return outs


def coarse_kernel(
    coarse_slots, meta, own_ref, core_ref, y_ref, yc_ref, z_ref, zy_ref, zc_ref, zyc_ref, enc_ref, w1_ref, w2_ref,
    out_ref, near_ref, far_ref, held, codes, even, odd, even2, odd2, spread, table, code_s, sem,
):
    slots, edge, rows, width = enc_ref.shape
    half = edge // 2
    plane = half * half
    cells = half * plane
    position = meta[slots + 3, 0]
    lane = position & (LANES - 1)
    lane_c = position & 1
    whole_rows = slots * cells
    rim_rows = whole_rows // 2
    section = (LANES * slots + 1) * cells
    places = [(ref, 0, whole_rows) for ref in (own_ref, core_ref, y_ref, yc_ref)]
    for ref in (z_ref, zy_ref, zc_ref, zyc_ref):
        places += [(ref, at, rim_rows) for at in (0, rim_rows + TILE)]
    origins = [LANES + (lane ^ i) for i in range(LANES)]
    near_rel = jnp.where(lane_c == 1, 2 * LANES, 0)
    far_rel = 2 * LANES - near_rel
    origins += [near_rel + (lane ^ 1 ^ i) for i in range(LANES)]
    origins += [far_rel + (lane ^ i) for i in range(LANES)]
    lines = 3 * LANES * coarse_slots + 1
    codes[...] = jnp.zeros_like(codes)
    for i, (origin, (ref, at, count)) in enumerate(zip(origins, places)):
        line = ref[at + count : at + count + TILE].astype(F32).astype(jnp.int32)
        row = 1 + origin * coarse_slots
        start = 2 * section if i < LANES else jnp.where(origin >= LANES, 3 * section, section)
        codes[pl.ds(row, coarse_slots)] = line[:coarse_slots] * cells + start
        codes[pl.ds(lines + row, coarse_slots)] = line[coarse_slots : 2 * coarse_slots]
    copy = pltpu.make_async_copy(codes, table, sem)
    copy.start()
    for i in range(4):
        held[i * section : i * section + cells] = jnp.zeros((cells, width), BF16)
    for i, (origin, (ref, at, count)) in enumerate(zip(origins, places)):
        if i < LANES:
            start = section + cells + origin * whole_rows
            start = pl.multiple_of(start + section - LANES * whole_rows, TILE)
            held[pl.ds(start, count)] = ref[at : at + count]
        else:
            group_start = jnp.where(origin >= LANES, 3 * section - 2 * LANES * whole_rows, section)
            start = group_start + cells + origin * whole_rows
            value = ref[at : at + count].reshape(slots, 1, cells // 2, width)
            start = pl.multiple_of(start, TILE)
            held[pl.ds(start, whole_rows)] = jnp.concatenate([value, value], axis=1).reshape(
                whole_rows, width
            )
    group_first = (position >> 2) * LANES * coarse_slots
    copy.wait()

    row_of = lax.broadcasted_iota(jnp.int32, (1, edge, width), 1)
    from_above = (row_of & 2) == 0
    center = (row_of >= 2) & (row_of < half + 2)
    regions = []
    masks = []
    for b in range(slots):
        own = jnp.where(meta[slots + 2, b] >= 0, meta[slots + 2, b], group_first * 8)
        octant = own & 7
        bits = ((octant >> 2) & 1, (octant >> 1) & 1, octant & 1)
        brick = jnp.clip((own >> 3) - group_first, 0, LANES * coarse_slots - 1)
        home = lines + 1 + LANES * coarse_slots + brick
        steps = [scale * (2 * bit - 1) for scale, bit in zip((9, 3, 1), bits)]
        numbers = [13, 13 + steps[2]]
        numbers += [number + steps[1] for number in numbers]
        numbers += [number + steps[0] for number in numbers]
        for cross, number in enumerate(numbers):
            code_s[b, cross] = table[home, number]
        turns = [octant ^ flip for flip in range(8)]
        across = [{0: 0, 1: scale * bit, -1: scale * (1 - bit)} for scale, bit in zip((4, 2, 1), bits)]

        def base_of(ex, ey, ez):
            flip = 4 * abs(ex) + 2 * abs(ey) + abs(ez)
            cross = across[0][ex] + across[1][ey] + across[2][ez]
            base = table[code_s[b, cross], turns[flip]]
            return pl.multiple_of(base + (2 * plane if ex < 0 else 0), TILE)

        x_parts = []
        for ex in OFFSETS:
            planes = half if ex == 0 else 2
            y_parts = []
            for ey in OFFSETS:
                picked = []
                for ez in OFFSETS:
                    value = held[pl.ds(base_of(ex, ey, ez), planes * plane), :].astype(F32)
                    value = value.reshape(planes, 2, edge, width)
                    if ey < 0:
                        value = value[:, 1:]
                    elif ey > 0:
                        value = value[:, :1]
                    picked.append(value.reshape(-1, edge, width))
                sides = jnp.where(from_above, picked[2], picked[0])
                first_y = jnp.where(center, pltpu.roll(picked[1], 2, 1), pltpu.roll(sides, edge - 2, 1))
                second_y = jnp.where(center, pltpu.roll(picked[1], edge - 2, 1), pltpu.roll(sides, 2, 1))
                shape = (planes, -1, 1, edge, width)
                both = jnp.concatenate([first_y.reshape(shape), second_y.reshape(shape)], axis=2)
                y_parts.append(both.reshape(planes, -1, edge, width))
            x_parts.append(jnp.concatenate(y_parts, axis=1))
        regions.append(jnp.concatenate(x_parts, axis=0))
        at_edge = jnp.where(bits[2] == 1, half + 1, 0)
        kinds = []
        for ex in OFFSETS:
            for ey in OFFSETS:
                cross = across[0][ex] + across[1][ey]
                there = jnp.where(row_of == at_edge, code_s[b, cross + 1], code_s[b, cross])
                kinds.append(there > 0)
        masks.append(kinds)

    mids = []
    for value, kinds in zip(valid_conv(regions, x_pair_weights(w1_ref, width), (even, odd), edge, width, ENC_GROUP), masks):
        spans = ((0, 1), (1, half + 1), (half + 1, half + 2))
        x_parts = []
        for i, (x0, x1) in enumerate(spans):
            y_parts = []
            for n, (y0, y1) in enumerate(spans):
                y_parts.append(jnp.where(kinds[3 * i + n][None], value[x0:x1, y0:y1], 0.0))
            x_parts.append(jnp.concatenate(y_parts, axis=1))
        mids.append(jnp.concatenate(x_parts, axis=0))
    fines = valid_conv(mids, x_pair_weights(w2_ref, width), (even2, odd2), edge, width, DEC_GROUP)
    is_odd = lane_c == 1
    for b in range(slots):
        value = jnp.where(meta[slots + 2, b] >= 0, fines[b], 0.0).reshape(plane * edge, width)
        spread[b, pl.ds(0, plane * edge, stride=2), :] = value
        spread[b, pl.ds(1, plane * edge, stride=2), :] = value
        up = spread[b].reshape(half, half, 2 * edge, width)[:, :, :edge]
        base = enc_ref[b].astype(F32).reshape(half, 2, half, 2, edge, width)
        total = base + up[:, None, :, None]
        total = total.reshape(edge, rows, width).astype(BF16)
        out_ref[b] = total
        last = jnp.where(meta[slots, b] == b, total[edge - 1], 0)
        head = jnp.where(meta[slots + 1, b] == b, total[0], 0)
        near_ref[b] = jnp.where(is_odd, head, last)
        far_ref[b] = jnp.where(is_odd, last, head)


def coarse(meta, blocks, enc, w1, w2, coarse_slots):
    slots, edge, rows, width = enc.shape
    half = edge // 2
    inside = edge - 2
    total = 4 * (LANES * slots + 1) * half**3
    lines = 2 * (3 * LANES * coarse_slots + 1)
    face = jax.ShapeDtypeStruct((slots, rows, width), BF16)
    return pl.pallas_call(
        functools.partial(coarse_kernel, coarse_slots),
        out_shape=(jax.ShapeDtypeStruct(enc.shape, BF16), face, face),
        in_specs=[SMEM] + [VMEM] * 11,
        out_specs=(VMEM, VMEM, VMEM),
        scratch_shapes=[
            pltpu.VMEM((total, width), BF16),
            pltpu.VMEM((lines, width), jnp.int32),
            pltpu.VMEM((slots, 3, edge, edge * edge, width), BF16),
            pltpu.VMEM((slots, 3, edge, inside * edge, width), BF16),
            pltpu.VMEM((slots, 3, inside, inside * edge, width), BF16),
            pltpu.VMEM((slots, 3, inside, half * edge, width), BF16),
            pltpu.VMEM((slots, 2 * half * half * edge, width), F32),
            pltpu.SMEM((lines, width), jnp.int32),
            pltpu.SMEM((slots, 8), jnp.int32),
            pltpu.SemaphoreType.DMA,
        ],
        compiler_params=PARAMS,
        cost_estimate=pl.CostEstimate(flops=2147483648, bytes_accessed=8388608, transcendentals=0),
        name="coarse",
    )(meta, *blocks, enc, w1, w2)


def per_device(
    features,
    fine_nbr,
    fine_send,
    fine_parent,
    coarse_child,
    coarse_nbr,
    enc_fine_w,
    enc_coarse_w,
    dec_coarse_w,
    dec_fine_w,
):
    slots, edge, _, _, width = features.shape
    coarse_slots = coarse_nbr.shape[0]
    size = lax.axis_size("gx")
    position = lax.axis_index("gx")

    def swap(value, partner):
        pairs = [(i, partner(i)) for i in range(size) if 0 <= partner(i) < size]
        return lax.ppermute(value, "gx", pairs)

    def core(value):
        return swap(value, lambda i: i ^ 1)

    def next_chip(value):
        return swap(value, lambda i: i + 1 if i % 2 else i - 1)

    def across_y(value):
        return swap(value, lambda i: i ^ 2)

    def across_z(value):
        return swap(value, lambda i: i + 3 if i % 2 else i - 3)

    x = features.reshape(slots, edge, edge * edge, width)
    flat = [w.reshape(27 * width, width) for w in (enc_fine_w, enc_coarse_w, dec_coarse_w, dec_fine_w)]
    info = position.astype(jnp.int32).reshape(1, 1)
    near, far, meta, codes, x, first_w = first(
        info, x, flat[0], fine_nbr, fine_send[0], fine_parent.reshape(1, slots), coarse_child, coarse_nbr
    )
    far = next_chip(far)
    near = core(near)
    main, part = inner(x, meta, first_w)
    enc, pooled, rim = outer_pool(main, part, near, far, meta, first_w, codes)

    rim_c = core(rim)
    rim_z = across_z(jnp.concatenate([rim, rim_c], axis=0))
    pooled_y = across_y(pooled)
    rim_zy = across_y(rim_z)
    pooled_c = core(pooled)
    pooled_yc = core(pooled_y)
    rim_zc = core(rim_z)
    rim_zyc = core(rim_zy)
    blocks = [pooled, pooled_c, pooled_y, pooled_yc, rim_z, rim_zy, rim_zc, rim_zyc]
    dec_in, near, far = coarse(meta, blocks, enc, flat[1], flat[2], coarse_slots)
    far = next_chip(far)
    near = core(near)
    main, part = inner(dec_in, meta, flat[3])
    out = outer(main, part, near, far, meta, flat[3])
    return out.reshape(features.shape)


def solution(mesh):
    placed = (
        P(("groups", "gx"), None, None, None, None),
        P(("groups", "gx"), None),
        P(("groups", "gx"), None, None),
        P(("groups", "gx")),
        P(("groups", "gx"), None),
        P(("groups", "gx"), None),
        P(),
        P(),
        P(),
        P(),
    )
    return jax.shard_map(
        per_device,
        mesh=mesh,
        in_specs=placed,
        out_specs=P(("groups", "gx"), None, None, None, None),
        check_vma=False,
    )
```

```python
import functools

import jax
import jax.numpy as jnp
from jax import lax
from jax.experimental import pallas as pl
from jax.experimental.pallas import tpu as pltpu
from jax.sharding import PartitionSpec as P


LANES = 4
GROUP = 2
ENC_GROUP = 1
DEC_GROUP = 4
TILE = 16
OFFSETS = (-1, 0, 1)
BF16 = jnp.bfloat16
F32 = jnp.float32
VMEM = pl.BlockSpec(memory_space=pltpu.VMEM)
SMEM = pl.BlockSpec(memory_space=pltpu.SMEM)
HBM = pl.BlockSpec(memory_space=pltpu.HBM)
PARAMS = pltpu.CompilerParams(vmem_limit_bytes=16 << 20)


def tap(dx, dy, dz):
    return 9 * (dx + 1) + 3 * (dy + 1) + dz + 1


def z_shifts(center, below, above):
    edge = center.shape[1]
    z = lax.broadcasted_iota(jnp.int32, center.shape, 1)
    down = jnp.where(z == 0, pltpu.roll(below, 1, 1), pltpu.roll(center, 1, 1))
    up = jnp.where(z == edge - 1, pltpu.roll(above, edge - 1, 1), pltpu.roll(center, edge - 1, 1))
    return down, center, up


def columns(fetch, edge):
    parts = []
    for dy in OFFSETS:
        triple = [fetch(dy, dz) for dz in (0, -1, 1)]
        planes, rows, _, width = triple[0].shape
        flat = [v.reshape(planes * rows, edge, width) for v in triple]
        parts.append([s.reshape(planes, rows, edge, width) for s in z_shifts(*flat)])
    return [jnp.concatenate([part[k] for part in parts], axis=1) for k in range(3)]


def y_rows(load, dy, edge):
    if dy == 0:
        value = load(0, edge * edge)
    elif dy < 0:
        value = load(edge * edge - 2 * edge, 2 * edge)[:, edge:]
    else:
        value = load(0, 2 * edge)[:, :edge]
    planes, rows, width = value.shape
    return value.reshape(planes, rows // edge, edge, width)


def pair_weights(w_ref, dxs, width):
    zero = jnp.zeros((3 * width, width), BF16)
    blocks = []
    for dx in dxs:
        for j in range(4):
            sides = []
            for p in range(2):
                dy = j - p
                first = (9 * dx + 3 * dy) * width
                sides.append(w_ref[first : first + 3 * width] if 0 <= dy < 3 else zero)
            blocks.append(jnp.concatenate(sides, axis=1))
    return jnp.concatenate(blocks, axis=0)


def pair_rows(full, j, pairs):
    planes, _, edge, width = full.shape
    picked = jnp.concatenate([full[:, j + 2 * i : j + 2 * i + 1] for i in range(pairs)], axis=1)
    return picked.reshape(planes, pairs * edge, width).astype(BF16)


def unpair(total, planes, pairs, edge, width):
    sides = [
        total[:, p * width : (p + 1) * width].reshape(planes, pairs, 1, edge, width) for p in range(2)
    ]
    return jnp.concatenate(sides, axis=2).reshape(planes, 2 * pairs * edge, width)


def first_kernel(
    x_hbm, w_hbm, nbr_hbm, send_hbm, parent_hbm, child_hbm, around_hbm,
    near_ref, far_ref, meta_ref, codes_ref, x_ref, w_ref, ids_ref, low_ref,
    head_v, last_v, nbr_v, send_v, parent_v, child_v, around_v, numbers, sems,
):
    slots, edge, _, width = x_hbm.shape
    coarse_slots = child_v.shape[0]
    pairs = [(x_hbm.at[:, 0], head_v), (x_hbm.at[:, edge - 1], last_v)]
    pairs += [(nbr_hbm, nbr_v), (send_hbm, send_v), (parent_hbm, parent_v)]
    pairs += [(child_hbm, child_v), (around_hbm, around_v)]
    pairs += [(x_hbm, x_ref), (w_hbm, w_ref)]
    copies = [pltpu.make_async_copy(*pair, sems.at[i]) for i, pair in enumerate(pairs)]
    for copy in copies:
        copy.start()
    for copy in copies[:-2]:
        copy.wait()
    position = lax.axis_index("gx")
    meta_ref[...] = jnp.full(meta_ref.shape, position, jnp.int32)
    meta_ref[0:slots, 0:27] = nbr_v[...]
    meta_ref[slots : slots + 2, 0:slots] = send_v[...]
    meta_ref[slots + 2 : slots + 3, 0:slots] = parent_v[...]
    numbers[...] = jnp.zeros_like(numbers)
    child = child_v[...]
    numbers[0:coarse_slots, 0:8] = jnp.where(child >= 0, (child & (LANES * slots - 1)) + 1, 0)
    around = around_v[...]
    first = ((position >> 2) - 1) * LANES * coarse_slots
    place = around - first
    inside = (around >= 0) & (place >= 0) & (place < 3 * LANES * coarse_slots)
    numbers[coarse_slots : 2 * coarse_slots, 0:27] = jnp.where(inside, place + 1, 0)
    codes_ref[...] = numbers[...].astype(F32).astype(BF16)
    is_odd = (position & 1) == 1
    send = send_v[...]
    slot_of = lax.broadcasted_iota(jnp.int32, send.shape, 1)
    listed = jnp.where(send == slot_of, 1.0, 0.0)
    for b in range(slots):
        last = last_v[b].astype(F32) * listed[0:1, b : b + 1]
        head = head_v[b].astype(F32) * listed[1:2, b : b + 1]
        near_ref[b] = jnp.where(is_odd, head, last).astype(BF16)
        far_ref[b] = jnp.where(is_odd, last, head).astype(BF16)
    for b in range(slots):
        parent = jnp.broadcast_to(parent_v[0:1, b : b + 1], (1, width))
        low_ref[b : b + 1] = jnp.where((parent & 4) == 0, 1, 0)
    z = lax.broadcasted_iota(jnp.int32, (edge, width), 0)
    line = 0
    for dx in (-1, 1):
        for b in range(slots):
            for dy in OFFSETS:
                wide = [
                    jnp.broadcast_to(nbr_v[b : b + 1, tap(dx, dy, dz) : tap(dx, dy, dz) + 1], (edge, width))
                    for dz in OFFSETS
                ]
                ends = (jnp.where(z == 0, wide[0], wide[1]), wide[1], jnp.where(z == edge - 1, wide[2], wide[1]))
                for value in ends:
                    ids_ref[line : line + edge] = value
                    line += edge
    for copy in copies[-2:]:
        copy.wait()


def stay(value):
    return pltpu.with_memory_space_constraint(value, pltpu.HBM)


def first(x, weights, nbr, send, parent, child, around):
    slots, edge, rows, width = x.shape
    coarse_slots = child.shape[0]
    assert 2 * coarse_slots <= TILE and (LANES * slots) & (LANES * slots - 1) == 0
    face = jax.ShapeDtypeStruct((slots, rows, width), BF16)
    return pl.pallas_call(
        first_kernel,
        out_shape=(
            face,
            face,
            jax.ShapeDtypeStruct((slots + 4, width), jnp.int32),
            jax.ShapeDtypeStruct((TILE, width), BF16),
            jax.ShapeDtypeStruct(x.shape, BF16),
            jax.ShapeDtypeStruct(weights.shape, BF16),
            jax.ShapeDtypeStruct((2 * slots * 9 * edge, width), jnp.int32),
            jax.ShapeDtypeStruct((slots, width), jnp.int32),
        ),
        in_specs=[HBM] * 7,
        out_specs=(VMEM,) * 8,
        scratch_shapes=[pltpu.VMEM((slots, rows, width), BF16)] * 2
        + [pltpu.VMEM(v.shape, jnp.int32) for v in (nbr, send, parent, child, around)]
        + [pltpu.VMEM((TILE, width), jnp.int32), pltpu.SemaphoreType.DMA((9,))],
        compiler_params=PARAMS,
        cost_estimate=pl.CostEstimate(flops=0, bytes_accessed=2097152, transcendentals=0),
        name="first",
    )(*[stay(v) for v in (x, weights, nbr, send, parent, child, around)])


def inner_kernel(nbr, x_ref, w_ref, out_ref, part_ref, cols):
    slots, edge, _, width = x_ref.shape
    pairs = edge // 2
    empty = jnp.zeros((slots, 4, 3, pairs * edge, width), BF16)
    cols[:, :, :, 0] = empty
    cols[:, :, :, edge + 1] = empty
    weights = pair_weights(w_ref, range(3), width)
    for group in range(0, slots, GROUP):
        bricks = []
        for b in range(group, group + GROUP):

            def fetch(dy, dz):
                slot = nbr[b, tap(0, dy, dz)]
                held = jnp.maximum(slot, 0)
                value = y_rows(lambda r, n: x_ref[held, :, r : r + n, :].astype(F32), dy, edge)
                return jnp.where(slot >= 0, value, 0.0)

            for k, full in enumerate(columns(fetch, edge)):
                for j in range(4):
                    cols[b, j, k, 1 : edge + 1] = pair_rows(full, j, pairs)
            taps = []
            for dx in range(3):
                for j in range(4):
                    for k in range(3):
                        taps.append(
                            cols[b, j, k, dx : dx + edge].reshape(edge * pairs * edge, width)
                        )
            bricks.append(jnp.concatenate(taps, axis=1))
        totals = jnp.dot(
            jnp.concatenate(bricks, axis=0), weights, preferred_element_type=F32
        )
        count = edge * pairs * edge
        for i in range(GROUP):
            b = group + i
            total = unpair(totals[i * count : (i + 1) * count], edge, pairs, edge, width)
            out_ref[b] = jnp.maximum(total, 0.0).astype(BF16)
            part_ref[b, 0] = total[0]
            part_ref[b, 1] = total[edge - 1]


def inner(x, nbr, weights):
    slots, edge, rows, width = x.shape
    return pl.pallas_call(
        inner_kernel,
        out_shape=(
            jax.ShapeDtypeStruct(x.shape, BF16),
            jax.ShapeDtypeStruct((slots, 2, rows, width), F32),
        ),
        in_specs=[SMEM, VMEM, VMEM],
        out_specs=(VMEM, VMEM),
        scratch_shapes=[
            pltpu.VMEM((slots, 4, 3, edge + 2, rows // 2, width), BF16),
        ],
        compiler_params=PARAMS,
        cost_estimate=pl.CostEstimate(
            flops=2 * slots * edge * rows * 27 * width * width,
            bytes_accessed=4 << 20,
            transcendentals=0,
        ),
        name="inner",
    )(nbr, x, weights)


def outer_planes(ids_ref, near_ref, far_ref, part_ref, w_ref, out_ref, stack, edge):
    slots, _, rows, width = part_ref.shape
    pairs = edge // 2
    is_odd = lax.axis_index("gx") & 1
    for first, ref in ((0, near_ref), (slots, far_ref)):
        value = ref[...].astype(F32).reshape(slots * edge, edge, width)
        for k, turn in enumerate((1, 0, edge - 1)):
            moved = pltpu.roll(value, turn, 1) if turn else value
            stack[k, first : first + slots] = moved.reshape(slots, rows, width)
    for side, dx in enumerate((-1, 1)):
        offset = slots * (1 - is_odd if side == 0 else is_odd)
        bricks = []
        for b in range(slots):
            shifted = []
            for k in range(3):
                parts = []
                for dy in OFFSETS:
                    line = (((side * slots + b) * 3 + dy + 1) * 3 + k) * edge
                    ids = ids_ref[line : line + edge][None]
                    first, count = {-1: (edge - 1, 1), 0: (0, edge), 1: (0, 1)}[dy]
                    value = jnp.zeros((count, edge, width), F32)
                    for slot in range(slots):
                        held = stack[k, offset + slot, first * edge : (first + count) * edge]
                        value = jnp.where(ids == slot, held.reshape(count, edge, width), value)
                    parts.append(value)
                shifted.append(jnp.concatenate(parts, axis=0)[None])
            taps = []
            for j in range(4):
                for k in range(3):
                    taps.append(pair_rows(shifted[k], j, pairs).reshape(rows // 2, width))
            bricks.append(jnp.concatenate(taps, axis=1))
        extra = jnp.dot(
            jnp.concatenate(bricks, axis=0),
            pair_weights(w_ref, [dx + 1], width),
            preferred_element_type=F32,
        )
        extra = unpair(extra, slots, pairs, edge, width)
        plane = 0 if side == 0 else out_ref.shape[1] - 1
        for b in range(slots):
            total = part_ref[b, side] + extra[b]
            out_ref[b, plane] = jnp.maximum(total, 0.0).astype(BF16)


def outer_kernel(ids_ref, near_ref, far_ref, part_ref, w_ref, main_ref, out_hbm, planes, stack, sems):
    edge = main_ref.shape[1]
    inside = pltpu.make_async_copy(main_ref.at[:, 1 : edge - 1], out_hbm.at[:, 1 : edge - 1], sems.at[0])
    inside.start()
    outer_planes(ids_ref, near_ref, far_ref, part_ref, w_ref, planes, stack, edge)
    copies = [
        pltpu.make_async_copy(planes.at[:, i], out_hbm.at[:, x], sems.at[i + 1])
        for i, x in enumerate((0, edge - 1))
    ]
    for copy in copies:
        copy.start()
    for copy in copies + [inside]:
        copy.wait()


def outer(main, part, near, far, ids, weights):
    return pl.pallas_call(
        outer_kernel,
        out_shape=jax.ShapeDtypeStruct(main.shape, BF16),
        in_specs=[VMEM] * 6,
        out_specs=HBM,
        scratch_shapes=[
            pltpu.VMEM(part.shape, BF16),
            pltpu.VMEM((3, 2 * main.shape[0]) + main.shape[2:], F32),
            pltpu.SemaphoreType.DMA((3,)),
        ],
        compiler_params=PARAMS,
        cost_estimate=pl.CostEstimate(flops=536870912, bytes_accessed=4194304, transcendentals=0),
        name="outer",
    )(ids, near, far, part, weights, main)


def outer_pool_kernel(
    ids_ref, low_ref, near_ref, far_ref, part_ref, w_ref, main_ref, code_ref, out_ref, pool_ref, rim_ref, sums, stack
):
    slots, edge, _, width = out_ref.shape
    half = edge // 2
    out_ref[:, 1 : edge - 1] = main_ref[:, 1 : edge - 1]
    outer_planes(ids_ref, near_ref, far_ref, part_ref, w_ref, out_ref, stack, edge)
    cells = half**3
    pool_ref[slots * cells :] = code_ref[...]
    rim_ref[slots * cells // 2 :] = code_ref[...]
    for b in range(slots):
        value = out_ref[b].astype(F32).reshape(half, 2, half, 2, edge, width)
        value = (value[:, 0, :, 0] + value[:, 0, :, 1]) + (value[:, 1, :, 0] + value[:, 1, :, 1])
        sums[b] = value.reshape(half * half * edge, width)
        low = sums[b, pl.ds(0, cells, stride=2), :]
        high = sums[b, pl.ds(1, cells, stride=2), :]
        pooled = (low + high) * 0.125
        pool_ref[b * cells : (b + 1) * cells, :] = pooled.astype(BF16)
        rim = jnp.where(low_ref[b : b + 1] == 1, pooled[: cells // 2], pooled[cells // 2 :])
        rim_ref[b * cells // 2 : (b + 1) * cells // 2, :] = rim.astype(BF16)


def outer_pool(main, part, near, far, ids, low, weights, codes):
    slots, edge, rows, width = main.shape
    cells = (edge // 2) ** 3
    return pl.pallas_call(
        outer_pool_kernel,
        out_shape=(
            jax.ShapeDtypeStruct(main.shape, BF16),
            jax.ShapeDtypeStruct((slots * cells + TILE, width), BF16),
            jax.ShapeDtypeStruct((slots * cells // 2 + TILE, width), BF16),
        ),
        in_specs=[VMEM] * 8,
        out_specs=(VMEM, VMEM, VMEM),
        scratch_shapes=[
            pltpu.VMEM((slots, 2 * cells, width), F32),
            pltpu.VMEM((3, 2 * slots, rows, width), F32),
        ],
        compiler_params=PARAMS,
        cost_estimate=pl.CostEstimate(flops=536870912, bytes_accessed=4194304, transcendentals=0),
        name="outer_pool",
    )(ids, low, near, far, part, weights, main, codes)


def x_pair_weights(w_ref, width):
    count = 9 * width
    zero = jnp.zeros((count, width), BF16)
    blocks = []
    for j in range(4):
        sides = [w_ref[(j - p) * count : (j - p + 1) * count] if 0 <= j - p < 3 else zero for p in range(2)]
        blocks.append(jnp.concatenate(sides, axis=1))
    return jnp.concatenate(blocks, axis=0)


def valid_conv(values, weights, cols, edge, width, group):
    size = values[0].shape[0]
    inside = size - 2
    pairs = inside // 2
    even, odd = cols
    bricks = []
    for b, value in enumerate(values):
        flat = value.reshape(size * size, edge, width)
        for k in range(3):
            moved = flat if k == 0 else pltpu.roll(flat, edge - k, 1)
            moved = moved.reshape(size, size, edge, width)
            even[b, k] = moved.reshape(size, size * edge, width).astype(BF16)
            odd[b, k] = moved[:, 1 : size - 1].reshape(size, inside * edge, width).astype(BF16)
        taps = []
        for j in range(4):
            for dy in range(3):
                for k in range(3):
                    if dy == 1:
                        planes = [odd[b, k, j + 2 * i] for i in range(pairs)]
                    else:
                        rows = slice(dy * edge, (dy + inside) * edge)
                        planes = [even[b, k, j + 2 * i, rows] for i in range(pairs)]
                    taps.append(jnp.concatenate(planes, axis=0))
        bricks.append(jnp.concatenate(taps, axis=1))
    rows = inside * edge
    outs = []
    for first in range(0, len(values), group):
        picked = bricks[first : first + group]
        total = jnp.dot(jnp.concatenate(picked, axis=0), weights, preferred_element_type=F32)
        total = jnp.maximum(total, 0.0).astype(BF16).astype(F32)
        for i in range(len(picked)):
            one = total[i * pairs * rows : (i + 1) * pairs * rows]
            sides = [one[:, p * width : (p + 1) * width].reshape(pairs, 1, rows, width) for p in range(2)]
            outs.append(jnp.concatenate(sides, axis=1).reshape(inside, inside, edge, width))
    return outs


def coarse_kernel(
    coarse_slots, meta_ref, own_ref, core_ref, y_ref, yc_ref, z_ref, zy_ref, zc_ref, zyc_ref, enc_ref, w1_ref, w2_ref,
    out_ref, near_ref, far_ref, held, codes, even, odd, even2, odd2, spread, table, code_s, sem,
):
    slots, edge, rows, width = enc_ref.shape
    half = edge // 2
    plane = half * half
    cells = half * plane
    position = lax.axis_index("gx")
    lane = position & (LANES - 1)
    lane_c = position & 1
    whole_rows = slots * cells
    rim_rows = whole_rows // 2
    section = (LANES * slots + 1) * cells
    places = [(ref, 0, whole_rows) for ref in (own_ref, core_ref, y_ref, yc_ref)]
    for ref in (z_ref, zy_ref, zc_ref, zyc_ref):
        places += [(ref, at, rim_rows) for at in (0, rim_rows + TILE)]
    origins = [LANES + (lane ^ i) for i in range(LANES)]
    near_rel = jnp.where(lane_c == 1, 2 * LANES, 0)
    far_rel = 2 * LANES - near_rel
    origins += [near_rel + (lane ^ 1 ^ i) for i in range(LANES)]
    origins += [far_rel + (lane ^ i) for i in range(LANES)]
    lines = 3 * LANES * coarse_slots + 1
    codes[...] = jnp.zeros_like(codes)
    codes[2 * lines : 2 * lines + slots + 4] = meta_ref[...]
    for i, (origin, (ref, at, count)) in enumerate(zip(origins, places)):
        line = ref[at + count : at + count + TILE].astype(F32).astype(jnp.int32)
        row = 1 + origin * coarse_slots
        start = 2 * section if i < LANES else jnp.where(origin >= LANES, 3 * section, section)
        codes[pl.ds(row, coarse_slots)] = line[:coarse_slots] * cells + start
        codes[pl.ds(lines + row, coarse_slots)] = line[coarse_slots : 2 * coarse_slots]
    copy = pltpu.make_async_copy(codes, table, sem)
    copy.start()
    for i in range(4):
        held[i * section : i * section + cells] = jnp.zeros((cells, width), BF16)
    for i, (origin, (ref, at, count)) in enumerate(zip(origins, places)):
        if i < LANES:
            start = section + cells + origin * whole_rows
            start = pl.multiple_of(start + section - LANES * whole_rows, TILE)
            held[pl.ds(start, count)] = ref[at : at + count]
        else:
            group_start = jnp.where(origin >= LANES, 3 * section - 2 * LANES * whole_rows, section)
            start = group_start + cells + origin * whole_rows
            value = ref[at : at + count].reshape(slots, 1, cells // 2, width)
            start = pl.multiple_of(start, TILE)
            held[pl.ds(start, whole_rows)] = jnp.concatenate([value, value], axis=1).reshape(
                whole_rows, width
            )
    group_first = (position >> 2) * LANES * coarse_slots
    copy.wait()

    row_of = lax.broadcasted_iota(jnp.int32, (1, edge, width), 1)
    from_above = (row_of & 2) == 0
    center = (row_of >= 2) & (row_of < half + 2)
    regions = []
    masks = []
    for b in range(slots):
        own = jnp.where(table[2 * lines + slots + 2, b] >= 0, table[2 * lines + slots + 2, b], group_first * 8)
        octant = own & 7
        bits = ((octant >> 2) & 1, (octant >> 1) & 1, octant & 1)
        brick = jnp.clip((own >> 3) - group_first, 0, LANES * coarse_slots - 1)
        home = lines + 1 + LANES * coarse_slots + brick
        steps = [scale * (2 * bit - 1) for scale, bit in zip((9, 3, 1), bits)]
        numbers = [13, 13 + steps[2]]
        numbers += [number + steps[1] for number in numbers]
        numbers += [number + steps[0] for number in numbers]
        for cross, number in enumerate(numbers):
            code_s[b, cross] = table[home, number]
        turns = [octant ^ flip for flip in range(8)]
        across = [{0: 0, 1: scale * bit, -1: scale * (1 - bit)} for scale, bit in zip((4, 2, 1), bits)]

        def base_of(ex, ey, ez):
            flip = 4 * abs(ex) + 2 * abs(ey) + abs(ez)
            cross = across[0][ex] + across[1][ey] + across[2][ez]
            base = table[code_s[b, cross], turns[flip]]
            return pl.multiple_of(base + (2 * plane if ex < 0 else 0), TILE)

        x_parts = []
        for ex in OFFSETS:
            planes = half if ex == 0 else 2
            y_parts = []
            for ey in OFFSETS:
                picked = []
                for ez in OFFSETS:
                    value = held[pl.ds(base_of(ex, ey, ez), planes * plane), :].astype(F32)
                    value = value.reshape(planes, 2, edge, width)
                    if ey < 0:
                        value = value[:, 1:]
                    elif ey > 0:
                        value = value[:, :1]
                    picked.append(value.reshape(-1, edge, width))
                sides = jnp.where(from_above, picked[2], picked[0])
                first_y = jnp.where(center, pltpu.roll(picked[1], 2, 1), pltpu.roll(sides, edge - 2, 1))
                second_y = jnp.where(center, pltpu.roll(picked[1], edge - 2, 1), pltpu.roll(sides, 2, 1))
                shape = (planes, -1, 1, edge, width)
                both = jnp.concatenate([first_y.reshape(shape), second_y.reshape(shape)], axis=2)
                y_parts.append(both.reshape(planes, -1, edge, width))
            x_parts.append(jnp.concatenate(y_parts, axis=1))
        regions.append(jnp.concatenate(x_parts, axis=0))
        at_edge = jnp.where(bits[2] == 1, half + 1, 0)
        kinds = []
        for ex in OFFSETS:
            for ey in OFFSETS:
                cross = across[0][ex] + across[1][ey]
                there = jnp.where(row_of == at_edge, code_s[b, cross + 1], code_s[b, cross])
                kinds.append(there > 0)
        masks.append(kinds)

    mids = []
    for value, kinds in zip(valid_conv(regions, x_pair_weights(w1_ref, width), (even, odd), edge, width, ENC_GROUP), masks):
        spans = ((0, 1), (1, half + 1), (half + 1, half + 2))
        x_parts = []
        for i, (x0, x1) in enumerate(spans):
            y_parts = []
            for n, (y0, y1) in enumerate(spans):
                y_parts.append(jnp.where(kinds[3 * i + n][None], value[x0:x1, y0:y1], 0.0))
            x_parts.append(jnp.concatenate(y_parts, axis=1))
        mids.append(jnp.concatenate(x_parts, axis=0))
    fines = valid_conv(mids, x_pair_weights(w2_ref, width), (even2, odd2), edge, width, DEC_GROUP)
    is_odd = lane_c == 1
    for b in range(slots):
        value = jnp.where(table[2 * lines + slots + 2, b] >= 0, fines[b], 0.0).reshape(plane * edge, width)
        spread[b, pl.ds(0, plane * edge, stride=2), :] = value
        spread[b, pl.ds(1, plane * edge, stride=2), :] = value
        up = spread[b].reshape(half, half, 2 * edge, width)[:, :, :edge]
        base = enc_ref[b].astype(F32).reshape(half, 2, half, 2, edge, width)
        total = base + up[:, None, :, None]
        total = total.reshape(edge, rows, width).astype(BF16)
        out_ref[b] = total
        last = jnp.where(table[2 * lines + slots, b] == b, total[edge - 1], 0)
        head = jnp.where(table[2 * lines + slots + 1, b] == b, total[0], 0)
        near_ref[b] = jnp.where(is_odd, head, last)
        far_ref[b] = jnp.where(is_odd, last, head)


def coarse(meta, blocks, enc, w1, w2, coarse_slots):
    slots, edge, rows, width = enc.shape
    half = edge // 2
    inside = edge - 2
    total = 4 * (LANES * slots + 1) * half**3
    lines = 2 * (3 * LANES * coarse_slots + 1) + slots + 4
    face = jax.ShapeDtypeStruct((slots, rows, width), BF16)
    return pl.pallas_call(
        functools.partial(coarse_kernel, coarse_slots),
        out_shape=(jax.ShapeDtypeStruct(enc.shape, BF16), face, face),
        in_specs=[VMEM] * 12,
        out_specs=(VMEM, VMEM, VMEM),
        scratch_shapes=[
            pltpu.VMEM((total, width), BF16),
            pltpu.VMEM((lines, width), jnp.int32),
            pltpu.VMEM((slots, 3, edge, edge * edge, width), BF16),
            pltpu.VMEM((slots, 3, edge, inside * edge, width), BF16),
            pltpu.VMEM((slots, 3, inside, inside * edge, width), BF16),
            pltpu.VMEM((slots, 3, inside, half * edge, width), BF16),
            pltpu.VMEM((slots, 2 * half * half * edge, width), F32),
            pltpu.SMEM((lines, width), jnp.int32),
            pltpu.SMEM((slots, 8), jnp.int32),
            pltpu.SemaphoreType.DMA,
        ],
        compiler_params=PARAMS,
        cost_estimate=pl.CostEstimate(flops=2147483648, bytes_accessed=8388608, transcendentals=0),
        name="coarse",
    )(meta, *blocks, enc, w1, w2)


def per_device(
    features,
    fine_nbr,
    fine_send,
    fine_parent,
    coarse_child,
    coarse_nbr,
    enc_fine_w,
    enc_coarse_w,
    dec_coarse_w,
    dec_fine_w,
):
    slots, edge, _, _, width = features.shape
    coarse_slots = coarse_nbr.shape[0]
    size = lax.axis_size("gx")

    def swap(value, partner):
        pairs = [(i, partner(i)) for i in range(size) if 0 <= partner(i) < size]
        return lax.ppermute(value, "gx", pairs)

    def core(value):
        return swap(value, lambda i: i ^ 1)

    def next_chip(value):
        return swap(value, lambda i: i + 1 if i % 2 else i - 1)

    def across_y(value):
        return swap(value, lambda i: i ^ 2)

    def across_z(value):
        return swap(value, lambda i: i + 3 if i % 2 else i - 3)

    x = features.reshape(slots, edge, edge * edge, width)
    flat = [w.reshape(27 * width, width) for w in (enc_fine_w, enc_coarse_w, dec_coarse_w, dec_fine_w)]
    near, far, meta, codes, x, first_w, ids, low = first(
        x, flat[0], fine_nbr, fine_send[0], fine_parent.reshape(1, slots), coarse_child, coarse_nbr
    )
    far = next_chip(far)
    near = core(near)
    main, part = inner(x, meta, first_w)
    enc, pooled, rim = outer_pool(main, part, near, far, ids, low, first_w, codes)

    rim_c = core(rim)
    rim_z = across_z(jnp.concatenate([rim, rim_c], axis=0))
    pooled_y = across_y(pooled)
    rim_zy = across_y(rim_z)
    pooled_c = core(pooled)
    pooled_yc = core(pooled_y)
    rim_zc = core(rim_z)
    rim_zyc = core(rim_zy)
    blocks = [pooled, pooled_c, pooled_y, pooled_yc, rim_z, rim_zy, rim_zc, rim_zyc]
    dec_in, near, far = coarse(meta, blocks, enc, flat[1], flat[2], coarse_slots)
    far = next_chip(far)
    near = core(near)
    main, part = inner(dec_in, meta, flat[3])
    out = outer(main, part, near, far, ids, flat[3])
    return out.reshape(features.shape)


def solution(mesh):
    placed = (
        P(("groups", "gx"), None, None, None, None),
        P(("groups", "gx"), None),
        P(("groups", "gx"), None, None),
        P(("groups", "gx")),
        P(("groups", "gx"), None),
        P(("groups", "gx"), None),
        P(),
        P(),
        P(),
        P(),
    )
    return jax.shard_map(
        per_device,
        mesh=mesh,
        in_specs=placed,
        out_specs=P(("groups", "gx"), None, None, None, None),
        check_vma=False,
    )
```

```python
import functools

import jax
import jax.numpy as jnp
from jax import lax
from jax.experimental import pallas as pl
from jax.experimental.pallas import tpu as pltpu
from jax.sharding import PartitionSpec as P


LANES = 4
GROUP = 2
ENC_GROUP = 1
DEC_GROUP = 4
TILE = 16
OFFSETS = (-1, 0, 1)
BF16 = jnp.bfloat16
F32 = jnp.float32
VMEM = pl.BlockSpec(memory_space=pltpu.VMEM)
HBM = pl.BlockSpec(memory_space=pltpu.HBM)
PARAMS = pltpu.CompilerParams(vmem_limit_bytes=16 << 20)


def tap(dx, dy, dz):
    return 9 * (dx + 1) + 3 * (dy + 1) + dz + 1


def pair_weights(w_ref, dxs, width):
    zero = jnp.zeros((3 * width, width), BF16)
    blocks = []
    for dx in dxs:
        for j in range(4):
            sides = []
            for p in range(2):
                dy = j - p
                first = (9 * dx + 3 * dy) * width
                sides.append(w_ref[first : first + 3 * width] if 0 <= dy < 3 else zero)
            blocks.append(jnp.concatenate(sides, axis=1))
    return jnp.concatenate(blocks, axis=0)


def pair_rows(full, j, pairs):
    planes, _, edge, width = full.shape
    picked = jnp.concatenate([full[:, j + 2 * i : j + 2 * i + 1] for i in range(pairs)], axis=1)
    return picked.reshape(planes, pairs * edge, width).astype(BF16)


def unpair(total, planes, pairs, edge, width):
    sides = [
        total[:, p * width : (p + 1) * width].reshape(planes, pairs, 1, edge, width) for p in range(2)
    ]
    return jnp.concatenate(sides, axis=2).reshape(planes, 2 * pairs * edge, width)


def first_kernel(
    x_hbm, w_hbm, nbr_hbm, send_hbm, parent_hbm, child_hbm, around_hbm,
    near_ref, far_ref, meta_ref, codes_ref, x_ref, w_ref, ids_ref, low_ref,
    head_v, last_v, nbr_v, send_v, parent_v, child_v, around_v, numbers, sems,
):
    slots, edge, _, width = x_hbm.shape
    coarse_slots = child_v.shape[0]
    pairs = [(x_hbm.at[:, 0], head_v), (x_hbm.at[:, edge - 1], last_v)]
    pairs += [(nbr_hbm, nbr_v), (send_hbm, send_v), (parent_hbm, parent_v)]
    pairs += [(child_hbm, child_v), (around_hbm, around_v)]
    pairs += [(x_hbm, x_ref), (w_hbm, w_ref)]
    copies = [pltpu.make_async_copy(*pair, sems.at[i]) for i, pair in enumerate(pairs)]
    for copy in copies:
        copy.start()
    for copy in copies[:-2]:
        copy.wait()
    position = lax.axis_index("gx")
    meta_ref[...] = jnp.full(meta_ref.shape, position, jnp.int32)
    meta_ref[0:slots, 0:27] = nbr_v[...]
    meta_ref[slots : slots + 2, 0:slots] = send_v[...]
    meta_ref[slots + 2 : slots + 3, 0:slots] = parent_v[...]
    numbers[...] = jnp.zeros_like(numbers)
    child = child_v[...]
    numbers[0:coarse_slots, 0:8] = jnp.where(child >= 0, (child & (LANES * slots - 1)) + 1, 0)
    around = around_v[...]
    first = ((position >> 2) - 1) * LANES * coarse_slots
    place = around - first
    inside = (around >= 0) & (place >= 0) & (place < 3 * LANES * coarse_slots)
    numbers[coarse_slots : 2 * coarse_slots, 0:27] = jnp.where(inside, place + 1, 0)
    codes_ref[...] = numbers[...].astype(F32).astype(BF16)
    is_odd = (position & 1) == 1
    send = send_v[...]
    slot_of = lax.broadcasted_iota(jnp.int32, send.shape, 1)
    listed = jnp.where(send == slot_of, 1.0, 0.0)
    for b in range(slots):
        last = last_v[b].astype(F32) * listed[0:1, b : b + 1]
        head = head_v[b].astype(F32) * listed[1:2, b : b + 1]
        near_ref[b] = jnp.where(is_odd, head, last).astype(BF16)
        far_ref[b] = jnp.where(is_odd, last, head).astype(BF16)
    for b in range(slots):
        parent = jnp.broadcast_to(parent_v[0:1, b : b + 1], (1, width))
        low_ref[b : b + 1] = jnp.where((parent & 4) == 0, 1, 0)
    z = lax.broadcasted_iota(jnp.int32, (edge, width), 0)
    line = 0
    for dx in (-1, 1, 0):
        for b in range(slots):
            for dy in OFFSETS:
                wide = [
                    jnp.broadcast_to(nbr_v[b : b + 1, tap(dx, dy, dz) : tap(dx, dy, dz) + 1], (edge, width))
                    for dz in OFFSETS
                ]
                ends = (jnp.where(z == 0, wide[0], wide[1]), wide[1], jnp.where(z == edge - 1, wide[2], wide[1]))
                for value in ends:
                    ids_ref[line : line + edge] = value
                    line += edge
    for copy in copies[-2:]:
        copy.wait()


def stay(value):
    return pltpu.with_memory_space_constraint(value, pltpu.HBM)


def first(x, weights, nbr, send, parent, child, around):
    slots, edge, rows, width = x.shape
    coarse_slots = child.shape[0]
    assert 2 * coarse_slots <= TILE and (LANES * slots) & (LANES * slots - 1) == 0
    face = jax.ShapeDtypeStruct((slots, rows, width), BF16)
    return pl.pallas_call(
        first_kernel,
        out_shape=(
            face,
            face,
            jax.ShapeDtypeStruct((slots + 4, width), jnp.int32),
            jax.ShapeDtypeStruct((TILE, width), BF16),
            jax.ShapeDtypeStruct(x.shape, BF16),
            jax.ShapeDtypeStruct(weights.shape, BF16),
            jax.ShapeDtypeStruct((3 * slots * 9 * edge, width), jnp.int32),
            jax.ShapeDtypeStruct((slots, width), jnp.int32),
        ),
        in_specs=[HBM] * 7,
        out_specs=(VMEM,) * 8,
        scratch_shapes=[pltpu.VMEM((slots, rows, width), BF16)] * 2
        + [pltpu.VMEM(v.shape, jnp.int32) for v in (nbr, send, parent, child, around)]
        + [pltpu.VMEM((TILE, width), jnp.int32), pltpu.SemaphoreType.DMA((9,))],
        compiler_params=PARAMS,
        cost_estimate=pl.CostEstimate(flops=0, bytes_accessed=2097152, transcendentals=0),
        name="first",
    )(*[stay(v) for v in (x, weights, nbr, send, parent, child, around)])


def inner_kernel(ids_ref, x_ref, w_ref, out_ref, part_ref, cols, stack):
    slots, edge, _, width = x_ref.shape
    pairs = edge // 2
    empty = jnp.zeros((slots, 4, 3, pairs * edge, width), BF16)
    cols[:, :, :, 0] = empty
    cols[:, :, :, edge + 1] = empty
    for b in range(slots):
        value = x_ref[b].astype(F32).reshape(edge * edge, edge, width)
        for k, turn in enumerate((1, 0, edge - 1)):
            moved = pltpu.roll(value, turn, 1) if turn else value
            stack[k, b] = moved.reshape(edge, edge, edge, width)
    weights = pair_weights(w_ref, range(3), width)
    for group in range(0, slots, GROUP):
        bricks = []
        for b in range(group, group + GROUP):
            for k in range(3):
                parts = []
                for dy in OFFSETS:
                    line = (((2 * slots + b) * 3 + dy + 1) * 3 + k) * edge
                    ids = ids_ref[line : line + edge][None, None]
                    first, count = {-1: (edge - 1, 1), 0: (0, edge), 1: (0, 1)}[dy]
                    if dy == 0 and k == 1:
                        value = jnp.where(ids == b, stack[k, b], 0.0)
                    else:
                        value = jnp.zeros((edge, count, edge, width), F32)
                        for slot in range(slots):
                            held = stack[k, slot, :, first : first + count]
                            value = jnp.where(ids == slot, held, value)
                    parts.append(value)
                full = jnp.concatenate(parts, axis=1)
                for j in range(4):
                    cols[b, j, k, 1 : edge + 1] = pair_rows(full, j, pairs)
            taps = []
            for dx in range(3):
                for j in range(4):
                    for k in range(3):
                        taps.append(
                            cols[b, j, k, dx : dx + edge].reshape(edge * pairs * edge, width)
                        )
            bricks.append(jnp.concatenate(taps, axis=1))
        totals = jnp.dot(
            jnp.concatenate(bricks, axis=0), weights, preferred_element_type=F32
        )
        count = edge * pairs * edge
        for i in range(GROUP):
            b = group + i
            total = unpair(totals[i * count : (i + 1) * count], edge, pairs, edge, width)
            out_ref[b] = jnp.maximum(total, 0.0).astype(BF16)
            part_ref[b, 0] = total[0]
            part_ref[b, 1] = total[edge - 1]


def inner(x, ids, weights):
    slots, edge, rows, width = x.shape
    return pl.pallas_call(
        inner_kernel,
        out_shape=(
            jax.ShapeDtypeStruct(x.shape, BF16),
            jax.ShapeDtypeStruct((slots, 2, rows, width), F32),
        ),
        in_specs=[VMEM, VMEM, VMEM],
        out_specs=(VMEM, VMEM),
        scratch_shapes=[
            pltpu.VMEM((slots, 4, 3, edge + 2, rows // 2, width), BF16),
            pltpu.VMEM((3, slots, edge, edge, edge, width), F32),
        ],
        compiler_params=PARAMS,
        cost_estimate=pl.CostEstimate(
            flops=2 * slots * edge * rows * 27 * width * width,
            bytes_accessed=4 << 20,
            transcendentals=0,
        ),
        name="inner",
    )(ids, x, weights)


def outer_planes(ids_ref, near_ref, far_ref, part_ref, w_ref, out_ref, stack, edge):
    slots, _, rows, width = part_ref.shape
    pairs = edge // 2
    is_odd = lax.axis_index("gx") & 1
    for first, ref in ((0, near_ref), (slots, far_ref)):
        value = ref[...].astype(F32).reshape(slots * edge, edge, width)
        for k, turn in enumerate((1, 0, edge - 1)):
            moved = pltpu.roll(value, turn, 1) if turn else value
            stack[k, first : first + slots] = moved.reshape(slots, rows, width)
    for side, dx in enumerate((-1, 1)):
        offset = slots * (1 - is_odd if side == 0 else is_odd)
        bricks = []
        for b in range(slots):
            shifted = []
            for k in range(3):
                parts = []
                for dy in OFFSETS:
                    line = (((side * slots + b) * 3 + dy + 1) * 3 + k) * edge
                    ids = ids_ref[line : line + edge][None]
                    first, count = {-1: (edge - 1, 1), 0: (0, edge), 1: (0, 1)}[dy]
                    value = jnp.zeros((count, edge, width), F32)
                    for slot in range(slots):
                        held = stack[k, offset + slot, first * edge : (first + count) * edge]
                        value = jnp.where(ids == slot, held.reshape(count, edge, width), value)
                    parts.append(value)
                shifted.append(jnp.concatenate(parts, axis=0)[None])
            taps = []
            for j in range(4):
                for k in range(3):
                    taps.append(pair_rows(shifted[k], j, pairs).reshape(rows // 2, width))
            bricks.append(jnp.concatenate(taps, axis=1))
        extra = jnp.dot(
            jnp.concatenate(bricks, axis=0),
            pair_weights(w_ref, [dx + 1], width),
            preferred_element_type=F32,
        )
        extra = unpair(extra, slots, pairs, edge, width)
        plane = 0 if side == 0 else out_ref.shape[1] - 1
        for b in range(slots):
            total = part_ref[b, side] + extra[b]
            out_ref[b, plane] = jnp.maximum(total, 0.0).astype(BF16)


def outer_kernel(ids_ref, near_ref, far_ref, part_ref, w_ref, main_ref, out_hbm, planes, stack, sems):
    edge = main_ref.shape[1]
    inside = pltpu.make_async_copy(main_ref.at[:, 1 : edge - 1], out_hbm.at[:, 1 : edge - 1], sems.at[0])
    inside.start()
    outer_planes(ids_ref, near_ref, far_ref, part_ref, w_ref, planes, stack, edge)
    copies = [
        pltpu.make_async_copy(planes.at[:, i], out_hbm.at[:, x], sems.at[i + 1])
        for i, x in enumerate((0, edge - 1))
    ]
    for copy in copies:
        copy.start()
    for copy in copies + [inside]:
        copy.wait()


def outer(main, part, near, far, ids, weights):
    return pl.pallas_call(
        outer_kernel,
        out_shape=jax.ShapeDtypeStruct(main.shape, BF16),
        in_specs=[VMEM] * 6,
        out_specs=HBM,
        scratch_shapes=[
            pltpu.VMEM(part.shape, BF16),
            pltpu.VMEM((3, 2 * main.shape[0]) + main.shape[2:], F32),
            pltpu.SemaphoreType.DMA((3,)),
        ],
        compiler_params=PARAMS,
        cost_estimate=pl.CostEstimate(flops=536870912, bytes_accessed=4194304, transcendentals=0),
        name="outer",
    )(ids, near, far, part, weights, main)


def outer_pool_kernel(
    ids_ref, low_ref, near_ref, far_ref, part_ref, w_ref, main_ref, code_ref, out_ref, pool_ref, rim_ref, sums, stack
):
    slots, edge, _, width = out_ref.shape
    half = edge // 2
    out_ref[:, 1 : edge - 1] = main_ref[:, 1 : edge - 1]
    outer_planes(ids_ref, near_ref, far_ref, part_ref, w_ref, out_ref, stack, edge)
    cells = half**3
    pool_ref[slots * cells :] = code_ref[...]
    rim_ref[slots * cells // 2 :] = code_ref[...]
    for b in range(slots):
        value = out_ref[b].astype(F32).reshape(half, 2, half, 2, edge, width)
        value = (value[:, 0, :, 0] + value[:, 0, :, 1]) + (value[:, 1, :, 0] + value[:, 1, :, 1])
        sums[b] = value.reshape(half * half * edge, width)
        low = sums[b, pl.ds(0, cells, stride=2), :]
        high = sums[b, pl.ds(1, cells, stride=2), :]
        pooled = (low + high) * 0.125
        pool_ref[b * cells : (b + 1) * cells, :] = pooled.astype(BF16)
        rim = jnp.where(low_ref[b : b + 1] == 1, pooled[: cells // 2], pooled[cells // 2 :])
        rim_ref[b * cells // 2 : (b + 1) * cells // 2, :] = rim.astype(BF16)


def outer_pool(main, part, near, far, ids, low, weights, codes):
    slots, edge, rows, width = main.shape
    cells = (edge // 2) ** 3
    return pl.pallas_call(
        outer_pool_kernel,
        out_shape=(
            jax.ShapeDtypeStruct(main.shape, BF16),
            jax.ShapeDtypeStruct((slots * cells + TILE, width), BF16),
            jax.ShapeDtypeStruct((slots * cells // 2 + TILE, width), BF16),
        ),
        in_specs=[VMEM] * 8,
        out_specs=(VMEM, VMEM, VMEM),
        scratch_shapes=[
            pltpu.VMEM((slots, 2 * cells, width), F32),
            pltpu.VMEM((3, 2 * slots, rows, width), F32),
        ],
        compiler_params=PARAMS,
        cost_estimate=pl.CostEstimate(flops=536870912, bytes_accessed=4194304, transcendentals=0),
        name="outer_pool",
    )(ids, low, near, far, part, weights, main, codes)


def x_pair_weights(w_ref, width):
    count = 9 * width
    zero = jnp.zeros((count, width), BF16)
    blocks = []
    for j in range(4):
        sides = [w_ref[(j - p) * count : (j - p + 1) * count] if 0 <= j - p < 3 else zero for p in range(2)]
        blocks.append(jnp.concatenate(sides, axis=1))
    return jnp.concatenate(blocks, axis=0)


def valid_conv(values, weights, cols, edge, width, group):
    size = values[0].shape[0]
    inside = size - 2
    pairs = inside // 2
    even, odd = cols
    bricks = []
    for b, value in enumerate(values):
        flat = value.reshape(size * size, edge, width)
        for k in range(3):
            moved = flat if k == 0 else pltpu.roll(flat, edge - k, 1)
            moved = moved.reshape(size, size, edge, width)
            even[b, k] = moved.reshape(size, size * edge, width).astype(BF16)
            odd[b, k] = moved[:, 1 : size - 1].reshape(size, inside * edge, width).astype(BF16)
        taps = []
        for j in range(4):
            for dy in range(3):
                for k in range(3):
                    if dy == 1:
                        planes = [odd[b, k, j + 2 * i] for i in range(pairs)]
                    else:
                        rows = slice(dy * edge, (dy + inside) * edge)
                        planes = [even[b, k, j + 2 * i, rows] for i in range(pairs)]
                    taps.append(jnp.concatenate(planes, axis=0))
        bricks.append(jnp.concatenate(taps, axis=1))
    rows = inside * edge
    outs = []
    for first in range(0, len(values), group):
        picked = bricks[first : first + group]
        total = jnp.dot(jnp.concatenate(picked, axis=0), weights, preferred_element_type=F32)
        total = jnp.maximum(total, 0.0).astype(BF16).astype(F32)
        for i in range(len(picked)):
            one = total[i * pairs * rows : (i + 1) * pairs * rows]
            sides = [one[:, p * width : (p + 1) * width].reshape(pairs, 1, rows, width) for p in range(2)]
            outs.append(jnp.concatenate(sides, axis=1).reshape(inside, inside, edge, width))
    return outs


def coarse_kernel(
    coarse_slots, meta_ref, own_ref, core_ref, y_ref, yc_ref, z_ref, zy_ref, zc_ref, zyc_ref, enc_ref, w1_ref, w2_ref,
    out_ref, near_ref, far_ref, held, codes, even, odd, even2, odd2, spread, table, code_s, sem,
):
    slots, edge, rows, width = enc_ref.shape
    half = edge // 2
    plane = half * half
    cells = half * plane
    position = lax.axis_index("gx")
    lane = position & (LANES - 1)
    lane_c = position & 1
    whole_rows = slots * cells
    rim_rows = whole_rows // 2
    section = (LANES * slots + 1) * cells
    places = [(ref, 0, whole_rows) for ref in (own_ref, core_ref, y_ref, yc_ref)]
    for ref in (z_ref, zy_ref, zc_ref, zyc_ref):
        places += [(ref, at, rim_rows) for at in (0, rim_rows + TILE)]
    origins = [LANES + (lane ^ i) for i in range(LANES)]
    near_rel = jnp.where(lane_c == 1, 2 * LANES, 0)
    far_rel = 2 * LANES - near_rel
    origins += [near_rel + (lane ^ 1 ^ i) for i in range(LANES)]
    origins += [far_rel + (lane ^ i) for i in range(LANES)]
    lines = 3 * LANES * coarse_slots + 1
    codes[...] = jnp.zeros_like(codes)
    codes[2 * lines : 2 * lines + slots + 4] = meta_ref[...]
    for i, (origin, (ref, at, count)) in enumerate(zip(origins, places)):
        line = ref[at + count : at + count + TILE].astype(F32).astype(jnp.int32)
        row = 1 + origin * coarse_slots
        start = 2 * section if i < LANES else jnp.where(origin >= LANES, 3 * section, section)
        codes[pl.ds(row, coarse_slots)] = line[:coarse_slots] * cells + start
        codes[pl.ds(lines + row, coarse_slots)] = line[coarse_slots : 2 * coarse_slots]
    copy = pltpu.make_async_copy(codes, table, sem)
    copy.start()
    for i in range(4):
        held[i * section : i * section + cells] = jnp.zeros((cells, width), BF16)
    for i, (origin, (ref, at, count)) in enumerate(zip(origins, places)):
        if i < LANES:
            start = section + cells + origin * whole_rows
            start = pl.multiple_of(start + section - LANES * whole_rows, TILE)
            held[pl.ds(start, count)] = ref[at : at + count]
        else:
            group_start = jnp.where(origin >= LANES, 3 * section - 2 * LANES * whole_rows, section)
            start = group_start + cells + origin * whole_rows
            value = ref[at : at + count].reshape(slots, 1, cells // 2, width)
            start = pl.multiple_of(start, TILE)
            held[pl.ds(start, whole_rows)] = jnp.concatenate([value, value], axis=1).reshape(
                whole_rows, width
            )
    group_first = (position >> 2) * LANES * coarse_slots
    copy.wait()

    row_of = lax.broadcasted_iota(jnp.int32, (1, edge, width), 1)
    from_above = (row_of & 2) == 0
    center = (row_of >= 2) & (row_of < half + 2)
    regions = []
    masks = []
    for b in range(slots):
        own = jnp.where(table[2 * lines + slots + 2, b] >= 0, table[2 * lines + slots + 2, b], group_first * 8)
        octant = own & 7
        bits = ((octant >> 2) & 1, (octant >> 1) & 1, octant & 1)
        brick = jnp.clip((own >> 3) - group_first, 0, LANES * coarse_slots - 1)
        home = lines + 1 + LANES * coarse_slots + brick
        steps = [scale * (2 * bit - 1) for scale, bit in zip((9, 3, 1), bits)]
        numbers = [13, 13 + steps[2]]
        numbers += [number + steps[1] for number in numbers]
        numbers += [number + steps[0] for number in numbers]
        for cross, number in enumerate(numbers):
            code_s[b, cross] = table[home, number]
        turns = [octant ^ flip for flip in range(8)]
        across = [{0: 0, 1: scale * bit, -1: scale * (1 - bit)} for scale, bit in zip((4, 2, 1), bits)]

        def base_of(ex, ey, ez):
            flip = 4 * abs(ex) + 2 * abs(ey) + abs(ez)
            cross = across[0][ex] + across[1][ey] + across[2][ez]
            base = table[code_s[b, cross], turns[flip]]
            return pl.multiple_of(base + (2 * plane if ex < 0 else 0), TILE)

        x_parts = []
        for ex in OFFSETS:
            planes = half if ex == 0 else 2
            y_parts = []
            for ey in OFFSETS:
                picked = []
                for ez in OFFSETS:
                    value = held[pl.ds(base_of(ex, ey, ez), planes * plane), :].astype(F32)
                    value = value.reshape(planes, 2, edge, width)
                    if ey < 0:
                        value = value[:, 1:]
                    elif ey > 0:
                        value = value[:, :1]
                    picked.append(value.reshape(-1, edge, width))
                sides = jnp.where(from_above, picked[2], picked[0])
                first_y = jnp.where(center, pltpu.roll(picked[1], 2, 1), pltpu.roll(sides, edge - 2, 1))
                second_y = jnp.where(center, pltpu.roll(picked[1], edge - 2, 1), pltpu.roll(sides, 2, 1))
                shape = (planes, -1, 1, edge, width)
                both = jnp.concatenate([first_y.reshape(shape), second_y.reshape(shape)], axis=2)
                y_parts.append(both.reshape(planes, -1, edge, width))
            x_parts.append(jnp.concatenate(y_parts, axis=1))
        regions.append(jnp.concatenate(x_parts, axis=0))
        at_edge = jnp.where(bits[2] == 1, half + 1, 0)
        kinds = []
        for ex in OFFSETS:
            for ey in OFFSETS:
                cross = across[0][ex] + across[1][ey]
                there = jnp.where(row_of == at_edge, code_s[b, cross + 1], code_s[b, cross])
                kinds.append(there > 0)
        masks.append(kinds)

    mids = []
    for value, kinds in zip(valid_conv(regions, x_pair_weights(w1_ref, width), (even, odd), edge, width, ENC_GROUP), masks):
        spans = ((0, 1), (1, half + 1), (half + 1, half + 2))
        x_parts = []
        for i, (x0, x1) in enumerate(spans):
            y_parts = []
            for n, (y0, y1) in enumerate(spans):
                y_parts.append(jnp.where(kinds[3 * i + n][None], value[x0:x1, y0:y1], 0.0))
            x_parts.append(jnp.concatenate(y_parts, axis=1))
        mids.append(jnp.concatenate(x_parts, axis=0))
    fines = valid_conv(mids, x_pair_weights(w2_ref, width), (even2, odd2), edge, width, DEC_GROUP)
    is_odd = lane_c == 1
    for b in range(slots):
        value = jnp.where(table[2 * lines + slots + 2, b] >= 0, fines[b], 0.0).reshape(plane * edge, width)
        spread[b, pl.ds(0, plane * edge, stride=2), :] = value
        spread[b, pl.ds(1, plane * edge, stride=2), :] = value
        up = spread[b].reshape(half, half, 2 * edge, width)[:, :, :edge]
        base = enc_ref[b].astype(F32).reshape(half, 2, half, 2, edge, width)
        total = base + up[:, None, :, None]
        total = total.reshape(edge, rows, width).astype(BF16)
        out_ref[b] = total
        last = jnp.where(table[2 * lines + slots, b] == b, total[edge - 1], 0)
        head = jnp.where(table[2 * lines + slots + 1, b] == b, total[0], 0)
        near_ref[b] = jnp.where(is_odd, head, last)
        far_ref[b] = jnp.where(is_odd, last, head)


def coarse(meta, blocks, enc, w1, w2, coarse_slots):
    slots, edge, rows, width = enc.shape
    half = edge // 2
    inside = edge - 2
    total = 4 * (LANES * slots + 1) * half**3
    lines = 2 * (3 * LANES * coarse_slots + 1) + slots + 4
    face = jax.ShapeDtypeStruct((slots, rows, width), BF16)
    return pl.pallas_call(
        functools.partial(coarse_kernel, coarse_slots),
        out_shape=(jax.ShapeDtypeStruct(enc.shape, BF16), face, face),
        in_specs=[VMEM] * 12,
        out_specs=(VMEM, VMEM, VMEM),
        scratch_shapes=[
            pltpu.VMEM((total, width), BF16),
            pltpu.VMEM((lines, width), jnp.int32),
            pltpu.VMEM((slots, 3, edge, edge * edge, width), BF16),
            pltpu.VMEM((slots, 3, edge, inside * edge, width), BF16),
            pltpu.VMEM((slots, 3, inside, inside * edge, width), BF16),
            pltpu.VMEM((slots, 3, inside, half * edge, width), BF16),
            pltpu.VMEM((slots, 2 * half * half * edge, width), F32),
            pltpu.SMEM((lines, width), jnp.int32),
            pltpu.SMEM((slots, 8), jnp.int32),
            pltpu.SemaphoreType.DMA,
        ],
        compiler_params=PARAMS,
        cost_estimate=pl.CostEstimate(flops=2147483648, bytes_accessed=8388608, transcendentals=0),
        name="coarse",
    )(meta, *blocks, enc, w1, w2)


def per_device(
    features,
    fine_nbr,
    fine_send,
    fine_parent,
    coarse_child,
    coarse_nbr,
    enc_fine_w,
    enc_coarse_w,
    dec_coarse_w,
    dec_fine_w,
):
    slots, edge, _, _, width = features.shape
    coarse_slots = coarse_nbr.shape[0]
    size = lax.axis_size("gx")

    def swap(value, partner):
        pairs = [(i, partner(i)) for i in range(size) if 0 <= partner(i) < size]
        return lax.ppermute(value, "gx", pairs)

    def core(value):
        return swap(value, lambda i: i ^ 1)

    def next_chip(value):
        return swap(value, lambda i: i + 1 if i % 2 else i - 1)

    def across_y(value):
        return swap(value, lambda i: i ^ 2)

    def across_z(value):
        return swap(value, lambda i: i + 3 if i % 2 else i - 3)

    x = features.reshape(slots, edge, edge * edge, width)
    flat = [w.reshape(27 * width, width) for w in (enc_fine_w, enc_coarse_w, dec_coarse_w, dec_fine_w)]
    near, far, meta, codes, x, first_w, ids, low = first(
        x, flat[0], fine_nbr, fine_send[0], fine_parent.reshape(1, slots), coarse_child, coarse_nbr
    )
    far = next_chip(far)
    near = core(near)
    main, part = inner(x, ids, first_w)
    enc, pooled, rim = outer_pool(main, part, near, far, ids, low, first_w, codes)

    rim_c = core(rim)
    rim_z = across_z(jnp.concatenate([rim, rim_c], axis=0))
    pooled_y = across_y(pooled)
    rim_zy = across_y(rim_z)
    pooled_c = core(pooled)
    pooled_yc = core(pooled_y)
    rim_zc = core(rim_z)
    rim_zyc = core(rim_zy)
    blocks = [pooled, pooled_c, pooled_y, pooled_yc, rim_z, rim_zy, rim_zc, rim_zyc]
    dec_in, near, far = coarse(meta, blocks, enc, flat[1], flat[2], coarse_slots)
    far = next_chip(far)
    near = core(near)
    main, part = inner(dec_in, ids, flat[3])
    out = outer(main, part, near, far, ids, flat[3])
    return out.reshape(features.shape)


def solution(mesh):
    placed = (
        P(("groups", "gx"), None, None, None, None),
        P(("groups", "gx"), None),
        P(("groups", "gx"), None, None),
        P(("groups", "gx")),
        P(("groups", "gx"), None),
        P(("groups", "gx"), None),
        P(),
        P(),
        P(),
        P(),
    )
    return jax.shard_map(
        per_device,
        mesh=mesh,
        in_specs=placed,
        out_specs=P(("groups", "gx"), None, None, None, None),
        check_vma=False,
    )
```

```python
import functools

import jax
import jax.numpy as jnp
from jax import lax
from jax.experimental import pallas as pl
from jax.experimental.pallas import tpu as pltpu
from jax.sharding import PartitionSpec as P


LANES = 4
GROUP = 4
ENC_GROUP = 1
DEC_GROUP = 4
TILE = 16
OFFSETS = (-1, 0, 1)
BF16 = jnp.bfloat16
F32 = jnp.float32
VMEM = pl.BlockSpec(memory_space=pltpu.VMEM)
HBM = pl.BlockSpec(memory_space=pltpu.HBM)
PARAMS = pltpu.CompilerParams(vmem_limit_bytes=16 << 20)


def tap(dx, dy, dz):
    return 9 * (dx + 1) + 3 * (dy + 1) + dz + 1


def pair_weights(w_ref, dxs, width):
    zero = jnp.zeros((3 * width, width), BF16)
    blocks = []
    for dx in dxs:
        for j in range(4):
            sides = []
            for p in range(2):
                dy = j - p
                first = (9 * dx + 3 * dy) * width
                sides.append(w_ref[first : first + 3 * width] if 0 <= dy < 3 else zero)
            blocks.append(jnp.concatenate(sides, axis=1))
    return jnp.concatenate(blocks, axis=0)


def pair_rows(full, j, pairs):
    planes, _, edge, width = full.shape
    picked = jnp.concatenate([full[:, j + 2 * i : j + 2 * i + 1] for i in range(pairs)], axis=1)
    return picked.reshape(planes, pairs * edge, width).astype(BF16)


def unpair(total, planes, pairs, edge, width):
    sides = [
        total[:, p * width : (p + 1) * width].reshape(planes, pairs, 1, edge, width) for p in range(2)
    ]
    return jnp.concatenate(sides, axis=2).reshape(planes, 2 * pairs * edge, width)


def first_kernel(
    x_hbm, w_hbm, nbr_hbm, send_hbm, parent_hbm, child_hbm, around_hbm,
    near_ref, far_ref, meta_ref, codes_ref, x_ref, w_ref, ids_ref, low_ref,
    head_v, last_v, nbr_v, send_v, parent_v, child_v, around_v, numbers, sems,
):
    slots, edge, _, width = x_hbm.shape
    coarse_slots = child_v.shape[0]
    pairs = [(x_hbm.at[:, 0], head_v), (x_hbm.at[:, edge - 1], last_v)]
    pairs += [(nbr_hbm, nbr_v), (send_hbm, send_v), (parent_hbm, parent_v)]
    pairs += [(child_hbm, child_v), (around_hbm, around_v)]
    pairs += [(x_hbm, x_ref), (w_hbm, w_ref)]
    copies = [pltpu.make_async_copy(*pair, sems.at[i]) for i, pair in enumerate(pairs)]
    for copy in copies:
        copy.start()
    for copy in copies[:-2]:
        copy.wait()
    position = lax.axis_index("gx")
    meta_ref[...] = jnp.full(meta_ref.shape, position, jnp.int32)
    meta_ref[0:slots, 0:27] = nbr_v[...]
    meta_ref[slots : slots + 2, 0:slots] = send_v[...]
    meta_ref[slots + 2 : slots + 3, 0:slots] = parent_v[...]
    numbers[...] = jnp.zeros_like(numbers)
    child = child_v[...]
    numbers[0:coarse_slots, 0:8] = jnp.where(child >= 0, (child & (LANES * slots - 1)) + 1, 0)
    around = around_v[...]
    first = ((position >> 2) - 1) * LANES * coarse_slots
    place = around - first
    inside = (around >= 0) & (place >= 0) & (place < 3 * LANES * coarse_slots)
    numbers[coarse_slots : 2 * coarse_slots, 0:27] = jnp.where(inside, place + 1, 0)
    codes_ref[...] = numbers[...].astype(F32).astype(BF16)
    is_odd = (position & 1) == 1
    send = send_v[...]
    slot_of = lax.broadcasted_iota(jnp.int32, send.shape, 1)
    listed = jnp.where(send == slot_of, 1.0, 0.0)
    for b in range(slots):
        last = last_v[b].astype(F32) * listed[0:1, b : b + 1]
        head = head_v[b].astype(F32) * listed[1:2, b : b + 1]
        near_ref[b] = jnp.where(is_odd, head, last).astype(BF16)
        far_ref[b] = jnp.where(is_odd, last, head).astype(BF16)
    for b in range(slots):
        parent = jnp.broadcast_to(parent_v[0:1, b : b + 1], (1, width))
        low_ref[b : b + 1] = jnp.where((parent & 4) == 0, 1, 0)
    z = lax.broadcasted_iota(jnp.int32, (edge, width), 0)
    line = 0
    for dx in (-1, 1, 0):
        for b in range(slots):
            for dy in OFFSETS:
                wide = [
                    jnp.broadcast_to(nbr_v[b : b + 1, tap(dx, dy, dz) : tap(dx, dy, dz) + 1], (edge, width))
                    for dz in OFFSETS
                ]
                ends = (jnp.where(z == 0, wide[0], wide[1]), wide[1], jnp.where(z == edge - 1, wide[2], wide[1]))
                for value in ends:
                    ids_ref[line : line + edge] = value
                    line += edge
    for copy in copies[-2:]:
        copy.wait()


def stay(value):
    return pltpu.with_memory_space_constraint(value, pltpu.HBM)


def first(x, weights, nbr, send, parent, child, around):
    slots, edge, rows, width = x.shape
    coarse_slots = child.shape[0]
    assert 2 * coarse_slots <= TILE and (LANES * slots) & (LANES * slots - 1) == 0
    face = jax.ShapeDtypeStruct((slots, rows, width), BF16)
    return pl.pallas_call(
        first_kernel,
        out_shape=(
            face,
            face,
            jax.ShapeDtypeStruct((slots + 4, width), jnp.int32),
            jax.ShapeDtypeStruct((TILE, width), BF16),
            jax.ShapeDtypeStruct(x.shape, BF16),
            jax.ShapeDtypeStruct(weights.shape, BF16),
            jax.ShapeDtypeStruct((3 * slots * 9 * edge, width), jnp.int32),
            jax.ShapeDtypeStruct((slots, width), jnp.int32),
        ),
        in_specs=[HBM] * 7,
        out_specs=(VMEM,) * 8,
        scratch_shapes=[pltpu.VMEM((slots, rows, width), BF16)] * 2
        + [pltpu.VMEM(v.shape, jnp.int32) for v in (nbr, send, parent, child, around)]
        + [pltpu.VMEM((TILE, width), jnp.int32), pltpu.SemaphoreType.DMA((9,))],
        compiler_params=PARAMS,
        cost_estimate=pl.CostEstimate(flops=0, bytes_accessed=2097152, transcendentals=0),
        name="first",
    )(*[stay(v) for v in (x, weights, nbr, send, parent, child, around)])


def inner_kernel(ids_ref, x_ref, w_ref, out_ref, part_ref, cols, stack):
    slots, edge, _, width = x_ref.shape
    pairs = edge // 2
    empty = jnp.zeros((slots, 4, 3, pairs * edge, width), BF16)
    cols[:, :, :, 0] = empty
    cols[:, :, :, edge + 1] = empty
    for b in range(slots):
        value = x_ref[b].astype(F32).reshape(edge * edge, edge, width)
        for k, turn in enumerate((1, 0, edge - 1)):
            moved = pltpu.roll(value, turn, 1) if turn else value
            stack[k, b] = moved.reshape(edge, edge, edge, width)
    weights = pair_weights(w_ref, range(3), width)
    for group in range(0, slots, GROUP):
        bricks = []
        for b in range(group, group + GROUP):
            for k in range(3):
                parts = []
                for dy in OFFSETS:
                    line = (((2 * slots + b) * 3 + dy + 1) * 3 + k) * edge
                    ids = ids_ref[line : line + edge][None, None]
                    first, count = {-1: (edge - 1, 1), 0: (0, edge), 1: (0, 1)}[dy]
                    if dy == 0 and k == 1:
                        value = jnp.where(ids == b, stack[k, b], 0.0)
                    else:
                        value = jnp.zeros((edge, count, edge, width), F32)
                        for slot in range(slots):
                            held = stack[k, slot, :, first : first + count]
                            value = jnp.where(ids == slot, held, value)
                    parts.append(value)
                full = jnp.concatenate(parts, axis=1)
                for j in range(4):
                    cols[b, j, k, 1 : edge + 1] = pair_rows(full, j, pairs)
            taps = []
            for dx in range(3):
                for j in range(4):
                    for k in range(3):
                        taps.append(
                            cols[b, j, k, dx : dx + edge].reshape(edge * pairs * edge, width)
                        )
            bricks.append(jnp.concatenate(taps, axis=1))
        totals = jnp.dot(
            jnp.concatenate(bricks, axis=0), weights, preferred_element_type=F32
        )
        count = edge * pairs * edge
        for i in range(GROUP):
            b = group + i
            total = unpair(totals[i * count : (i + 1) * count], edge, pairs, edge, width)
            out_ref[b] = jnp.maximum(total, 0.0).astype(BF16)
            part_ref[b, 0] = total[0]
            part_ref[b, 1] = total[edge - 1]


def inner(x, ids, weights):
    slots, edge, rows, width = x.shape
    return pl.pallas_call(
        inner_kernel,
        out_shape=(
            jax.ShapeDtypeStruct(x.shape, BF16),
            jax.ShapeDtypeStruct((slots, 2, rows, width), F32),
        ),
        in_specs=[VMEM, VMEM, VMEM],
        out_specs=(VMEM, VMEM),
        scratch_shapes=[
            pltpu.VMEM((slots, 4, 3, edge + 2, rows // 2, width), BF16),
            pltpu.VMEM((3, slots, edge, edge, edge, width), F32),
        ],
        compiler_params=PARAMS,
        cost_estimate=pl.CostEstimate(
            flops=2 * slots * edge * rows * 27 * width * width,
            bytes_accessed=4 << 20,
            transcendentals=0,
        ),
        name="inner",
    )(ids, x, weights)


def outer_planes(ids_ref, near_ref, far_ref, part_ref, w_ref, out_ref, stack, edge, copies=None):
    slots, _, rows, width = part_ref.shape
    pairs = edge // 2
    is_odd = lax.axis_index("gx") & 1
    for first, ref in ((0, near_ref), (slots, far_ref)):
        value = ref[...].astype(F32).reshape(slots * edge, edge, width)
        for k, turn in enumerate((1, 0, edge - 1)):
            moved = pltpu.roll(value, turn, 1) if turn else value
            stack[k, first : first + slots] = moved.reshape(slots, rows, width)
    for side, dx in enumerate((-1, 1)):
        offset = slots * (1 - is_odd if side == 0 else is_odd)
        bricks = []
        for b in range(slots):
            shifted = []
            for k in range(3):
                parts = []
                for dy in OFFSETS:
                    line = (((side * slots + b) * 3 + dy + 1) * 3 + k) * edge
                    ids = ids_ref[line : line + edge][None]
                    first, count = {-1: (edge - 1, 1), 0: (0, edge), 1: (0, 1)}[dy]
                    value = jnp.zeros((count, edge, width), F32)
                    for slot in range(slots):
                        held = stack[k, offset + slot, first * edge : (first + count) * edge]
                        value = jnp.where(ids == slot, held.reshape(count, edge, width), value)
                    parts.append(value)
                shifted.append(jnp.concatenate(parts, axis=0)[None])
            taps = []
            for j in range(4):
                for k in range(3):
                    taps.append(pair_rows(shifted[k], j, pairs).reshape(rows // 2, width))
            bricks.append(jnp.concatenate(taps, axis=1))
        extra = jnp.dot(
            jnp.concatenate(bricks, axis=0),
            pair_weights(w_ref, [dx + 1], width),
            preferred_element_type=F32,
        )
        extra = unpair(extra, slots, pairs, edge, width)
        plane = 0 if side == 0 else out_ref.shape[1] - 1
        for b in range(slots):
            total = part_ref[b, side] + extra[b]
            out_ref[b, plane] = jnp.maximum(total, 0.0).astype(BF16)
        if copies is not None:
            copies[side].start()


def outer_kernel(ids_ref, near_ref, far_ref, part_ref, w_ref, main_ref, out_hbm, planes, stack, sems):
    edge = main_ref.shape[1]
    inside = pltpu.make_async_copy(main_ref.at[:, 1 : edge - 1], out_hbm.at[:, 1 : edge - 1], sems.at[0])
    inside.start()
    copies = [
        pltpu.make_async_copy(planes.at[:, i], out_hbm.at[:, x], sems.at[i + 1])
        for i, x in enumerate((0, edge - 1))
    ]
    outer_planes(ids_ref, near_ref, far_ref, part_ref, w_ref, planes, stack, edge, copies)
    for copy in copies + [inside]:
        copy.wait()


def outer(main, part, near, far, ids, weights):
    return pl.pallas_call(
        outer_kernel,
        out_shape=jax.ShapeDtypeStruct(main.shape, BF16),
        in_specs=[VMEM] * 6,
        out_specs=HBM,
        scratch_shapes=[
            pltpu.VMEM(part.shape, BF16),
            pltpu.VMEM((3, 2 * main.shape[0]) + main.shape[2:], F32),
            pltpu.SemaphoreType.DMA((3,)),
        ],
        compiler_params=PARAMS,
        cost_estimate=pl.CostEstimate(flops=536870912, bytes_accessed=4194304, transcendentals=0),
        name="outer",
    )(ids, near, far, part, weights, main)


def outer_pool_kernel(
    ids_ref, low_ref, near_ref, far_ref, part_ref, w_ref, main_ref, code_ref, out_ref, pool_ref, rim_ref, sums, stack
):
    slots, edge, _, width = out_ref.shape
    half = edge // 2
    out_ref[:, 1 : edge - 1] = main_ref[:, 1 : edge - 1]
    outer_planes(ids_ref, near_ref, far_ref, part_ref, w_ref, out_ref, stack, edge)
    cells = half**3
    pool_ref[slots * cells :] = code_ref[...]
    rim_ref[slots * cells // 2 :] = code_ref[...]
    for b in range(slots):
        value = out_ref[b].astype(F32).reshape(half, 2, half, 2, edge, width)
        value = (value[:, 0, :, 0] + value[:, 0, :, 1]) + (value[:, 1, :, 0] + value[:, 1, :, 1])
        sums[b] = value.reshape(half * half * edge, width)
        low = sums[b, pl.ds(0, cells, stride=2), :]
        high = sums[b, pl.ds(1, cells, stride=2), :]
        pooled = (low + high) * 0.125
        pool_ref[b * cells : (b + 1) * cells, :] = pooled.astype(BF16)
        rim = jnp.where(low_ref[b : b + 1] == 1, pooled[: cells // 2], pooled[cells // 2 :])
        rim_ref[b * cells // 2 : (b + 1) * cells // 2, :] = rim.astype(BF16)


def outer_pool(main, part, near, far, ids, low, weights, codes):
    slots, edge, rows, width = main.shape
    cells = (edge // 2) ** 3
    return pl.pallas_call(
        outer_pool_kernel,
        out_shape=(
            jax.ShapeDtypeStruct(main.shape, BF16),
            jax.ShapeDtypeStruct((slots * cells + TILE, width), BF16),
            jax.ShapeDtypeStruct((slots * cells // 2 + TILE, width), BF16),
        ),
        in_specs=[VMEM] * 8,
        out_specs=(VMEM, VMEM, VMEM),
        scratch_shapes=[
            pltpu.VMEM((slots, 2 * cells, width), F32),
            pltpu.VMEM((3, 2 * slots, rows, width), F32),
        ],
        compiler_params=PARAMS,
        cost_estimate=pl.CostEstimate(flops=536870912, bytes_accessed=4194304, transcendentals=0),
        name="outer_pool",
    )(ids, low, near, far, part, weights, main, codes)


def x_pair_weights(w_ref, width):
    count = 9 * width
    zero = jnp.zeros((count, width), BF16)
    blocks = []
    for j in range(4):
        sides = [w_ref[(j - p) * count : (j - p + 1) * count] if 0 <= j - p < 3 else zero for p in range(2)]
        blocks.append(jnp.concatenate(sides, axis=1))
    return jnp.concatenate(blocks, axis=0)


def valid_conv(values, weights, cols, edge, width, group):
    size = values[0].shape[0]
    inside = size - 2
    pairs = inside // 2
    even, odd = cols
    bricks = []
    for b, value in enumerate(values):
        flat = value.reshape(size * size, edge, width)
        for k in range(3):
            moved = flat if k == 0 else pltpu.roll(flat, edge - k, 1)
            moved = moved.reshape(size, size, edge, width)
            even[b, k] = moved.reshape(size, size * edge, width).astype(BF16)
            odd[b, k] = moved[:, 1 : size - 1].reshape(size, inside * edge, width).astype(BF16)
        taps = []
        for j in range(4):
            for dy in range(3):
                for k in range(3):
                    if dy == 1:
                        planes = [odd[b, k, j + 2 * i] for i in range(pairs)]
                    else:
                        rows = slice(dy * edge, (dy + inside) * edge)
                        planes = [even[b, k, j + 2 * i, rows] for i in range(pairs)]
                    taps.append(jnp.concatenate(planes, axis=0))
        bricks.append(jnp.concatenate(taps, axis=1))
    rows = inside * edge
    outs = []
    for first in range(0, len(values), group):
        picked = bricks[first : first + group]
        total = jnp.dot(jnp.concatenate(picked, axis=0), weights, preferred_element_type=F32)
        total = jnp.maximum(total, 0.0).astype(BF16).astype(F32)
        for i in range(len(picked)):
            one = total[i * pairs * rows : (i + 1) * pairs * rows]
            sides = [one[:, p * width : (p + 1) * width].reshape(pairs, 1, rows, width) for p in range(2)]
            outs.append(jnp.concatenate(sides, axis=1).reshape(inside, inside, edge, width))
    return outs


def coarse_kernel(
    coarse_slots, meta_ref, own_ref, core_ref, y_ref, yc_ref, z_ref, zy_ref, zc_ref, zyc_ref, enc_ref, w1_ref, w2_ref,
    out_ref, near_ref, far_ref, held, codes, even, odd, even2, odd2, spread, table, code_s, sem,
):
    slots, edge, rows, width = enc_ref.shape
    half = edge // 2
    plane = half * half
    cells = half * plane
    position = lax.axis_index("gx")
    lane = position & (LANES - 1)
    lane_c = position & 1
    whole_rows = slots * cells
    rim_rows = whole_rows // 2
    section = (LANES * slots + 1) * cells
    places = [(ref, 0, whole_rows) for ref in (own_ref, core_ref, y_ref, yc_ref)]
    for ref in (z_ref, zy_ref, zc_ref, zyc_ref):
        places += [(ref, at, rim_rows) for at in (0, rim_rows + TILE)]
    origins = [LANES + (lane ^ i) for i in range(LANES)]
    near_rel = jnp.where(lane_c == 1, 2 * LANES, 0)
    far_rel = 2 * LANES - near_rel
    origins += [near_rel + (lane ^ 1 ^ i) for i in range(LANES)]
    origins += [far_rel + (lane ^ i) for i in range(LANES)]
    lines = 3 * LANES * coarse_slots + 1
    codes[...] = jnp.zeros_like(codes)
    after = lines + LANES * coarse_slots
    codes[after : after + 3] = meta_ref[slots : slots + 3]
    for i, (origin, (ref, at, count)) in enumerate(zip(origins, places)):
        line = ref[at + count : at + count + TILE].astype(F32).astype(jnp.int32)
        row = 1 + origin * coarse_slots
        start = 2 * section if i < LANES else jnp.where(origin >= LANES, 3 * section, section)
        codes[pl.ds(row, coarse_slots)] = line[:coarse_slots] * cells + start
        if i < LANES:
            row = lines + (origin - LANES) * coarse_slots
            codes[pl.ds(row, coarse_slots)] = line[coarse_slots : 2 * coarse_slots]
    copy = pltpu.make_async_copy(codes, table, sem)
    copy.start()
    for i in range(4):
        held[i * section : i * section + cells] = jnp.zeros((cells, width), BF16)
    for i, (origin, (ref, at, count)) in enumerate(zip(origins, places)):
        if i < LANES:
            start = section + cells + origin * whole_rows
            start = pl.multiple_of(start + section - LANES * whole_rows, TILE)
            held[pl.ds(start, count)] = ref[at : at + count]
        else:
            group_start = jnp.where(origin >= LANES, 3 * section - 2 * LANES * whole_rows, section)
            start = group_start + cells + origin * whole_rows
            value = ref[at : at + count].reshape(slots, 1, cells // 2, width)
            start = pl.multiple_of(start, TILE)
            held[pl.ds(start, whole_rows)] = jnp.concatenate([value, value], axis=1).reshape(
                whole_rows, width
            )
    group_first = (position >> 2) * LANES * coarse_slots
    copy.wait()

    row_of = lax.broadcasted_iota(jnp.int32, (1, edge, width), 1)
    from_above = (row_of & 2) == 0
    center = (row_of >= 2) & (row_of < half + 2)
    regions = []
    masks = []
    for b in range(slots):
        own = jnp.where(table[after + 2, b] >= 0, table[after + 2, b], group_first * 8)
        octant = own & 7
        bits = ((octant >> 2) & 1, (octant >> 1) & 1, octant & 1)
        brick = jnp.clip((own >> 3) - group_first, 0, LANES * coarse_slots - 1)
        home = lines + brick
        steps = [scale * (2 * bit - 1) for scale, bit in zip((9, 3, 1), bits)]
        numbers = [13, 13 + steps[2]]
        numbers += [number + steps[1] for number in numbers]
        numbers += [number + steps[0] for number in numbers]
        for cross, number in enumerate(numbers):
            code_s[b, cross] = table[home, number]
        turns = [octant ^ flip for flip in range(8)]
        across = [{0: 0, 1: scale * bit, -1: scale * (1 - bit)} for scale, bit in zip((4, 2, 1), bits)]

        def base_of(ex, ey, ez):
            flip = 4 * abs(ex) + 2 * abs(ey) + abs(ez)
            cross = across[0][ex] + across[1][ey] + across[2][ez]
            base = table[code_s[b, cross], turns[flip]]
            return pl.multiple_of(base + (2 * plane if ex < 0 else 0), TILE)

        x_parts = []
        for ex in OFFSETS:
            planes = half if ex == 0 else 2
            y_parts = []
            for ey in OFFSETS:
                picked = []
                for ez in OFFSETS:
                    value = held[pl.ds(base_of(ex, ey, ez), planes * plane), :].astype(F32)
                    value = value.reshape(planes, 2, edge, width)
                    if ey < 0:
                        value = value[:, 1:]
                    elif ey > 0:
                        value = value[:, :1]
                    picked.append(value.reshape(-1, edge, width))
                sides = jnp.where(from_above, picked[2], picked[0])
                first_y = jnp.where(center, pltpu.roll(picked[1], 2, 1), pltpu.roll(sides, edge - 2, 1))
                second_y = jnp.where(center, pltpu.roll(picked[1], edge - 2, 1), pltpu.roll(sides, 2, 1))
                shape = (planes, -1, 1, edge, width)
                both = jnp.concatenate([first_y.reshape(shape), second_y.reshape(shape)], axis=2)
                y_parts.append(both.reshape(planes, -1, edge, width))
            x_parts.append(jnp.concatenate(y_parts, axis=1))
        regions.append(jnp.concatenate(x_parts, axis=0))
        at_edge = jnp.where(bits[2] == 1, half + 1, 0)
        kinds = []
        for ex in OFFSETS:
            for ey in OFFSETS:
                cross = across[0][ex] + across[1][ey]
                there = jnp.where(row_of == at_edge, code_s[b, cross + 1], code_s[b, cross])
                kinds.append(there > 0)
        masks.append(kinds)

    mids = []
    for value, kinds in zip(valid_conv(regions, x_pair_weights(w1_ref, width), (even, odd), edge, width, ENC_GROUP), masks):
        spans = ((0, 1), (1, half + 1), (half + 1, half + 2))
        x_parts = []
        for i, (x0, x1) in enumerate(spans):
            y_parts = []
            for n, (y0, y1) in enumerate(spans):
                y_parts.append(jnp.where(kinds[3 * i + n][None], value[x0:x1, y0:y1], 0.0))
            x_parts.append(jnp.concatenate(y_parts, axis=1))
        mids.append(jnp.concatenate(x_parts, axis=0))
    fines = valid_conv(mids, x_pair_weights(w2_ref, width), (even2, odd2), edge, width, DEC_GROUP)
    is_odd = lane_c == 1
    for b in range(slots):
        value = jnp.where(table[after + 2, b] >= 0, fines[b], 0.0).reshape(plane * edge, width)
        spread[b, pl.ds(0, plane * edge, stride=2), :] = value
        spread[b, pl.ds(1, plane * edge, stride=2), :] = value
        up = spread[b].reshape(half, half, 2 * edge, width)[:, :, :edge]
        base = enc_ref[b].astype(F32).reshape(half, 2, half, 2, edge, width)
        total = base + up[:, None, :, None]
        total = total.reshape(edge, rows, width).astype(BF16)
        out_ref[b] = total
        last = jnp.where(table[after, b] == b, total[edge - 1], 0)
        head = jnp.where(table[after + 1, b] == b, total[0], 0)
        near_ref[b] = jnp.where(is_odd, head, last)
        far_ref[b] = jnp.where(is_odd, last, head)


def coarse(meta, blocks, enc, w1, w2, coarse_slots):
    slots, edge, rows, width = enc.shape
    half = edge // 2
    inside = edge - 2
    total = 4 * (LANES * slots + 1) * half**3
    lines = 4 * LANES * coarse_slots + 4
    face = jax.ShapeDtypeStruct((slots, rows, width), BF16)
    return pl.pallas_call(
        functools.partial(coarse_kernel, coarse_slots),
        out_shape=(jax.ShapeDtypeStruct(enc.shape, BF16), face, face),
        in_specs=[VMEM] * 12,
        out_specs=(VMEM, VMEM, VMEM),
        scratch_shapes=[
            pltpu.VMEM((total, width), BF16),
            pltpu.VMEM((lines, width), jnp.int32),
            pltpu.VMEM((slots, 3, edge, edge * edge, width), BF16),
            pltpu.VMEM((slots, 3, edge, inside * edge, width), BF16),
            pltpu.VMEM((slots, 3, inside, inside * edge, width), BF16),
            pltpu.VMEM((slots, 3, inside, half * edge, width), BF16),
            pltpu.VMEM((slots, 2 * half * half * edge, width), F32),
            pltpu.SMEM((lines, width), jnp.int32),
            pltpu.SMEM((slots, 8), jnp.int32),
            pltpu.SemaphoreType.DMA,
        ],
        compiler_params=PARAMS,
        cost_estimate=pl.CostEstimate(flops=2147483648, bytes_accessed=8388608, transcendentals=0),
        name="coarse",
    )(meta, *blocks, enc, w1, w2)


def per_device(
    features,
    fine_nbr,
    fine_send,
    fine_parent,
    coarse_child,
    coarse_nbr,
    enc_fine_w,
    enc_coarse_w,
    dec_coarse_w,
    dec_fine_w,
):
    slots, edge, _, _, width = features.shape
    coarse_slots = coarse_nbr.shape[0]
    size = lax.axis_size("gx")

    def swap(value, partner):
        pairs = [(i, partner(i)) for i in range(size) if 0 <= partner(i) < size]
        return lax.ppermute(value, "gx", pairs)

    def core(value):
        return swap(value, lambda i: i ^ 1)

    def next_chip(value):
        return swap(value, lambda i: i + 1 if i % 2 else i - 1)

    def across_y(value):
        return swap(value, lambda i: i ^ 2)

    def across_z(value):
        return swap(value, lambda i: i + 3 if i % 2 else i - 3)

    x = features.reshape(slots, edge, edge * edge, width)
    flat = [w.reshape(27 * width, width) for w in (enc_fine_w, enc_coarse_w, dec_coarse_w, dec_fine_w)]
    near, far, meta, codes, x, first_w, ids, low = first(
        x, flat[0], fine_nbr, fine_send[0], fine_parent.reshape(1, slots), coarse_child, coarse_nbr
    )
    far = next_chip(far)
    near = core(near)
    main, part = inner(x, ids, first_w)
    enc, pooled, rim = outer_pool(main, part, near, far, ids, low, first_w, codes)

    rim_c = core(rim)
    rim_z = across_z(jnp.concatenate([rim, rim_c], axis=0))
    pooled_y = across_y(pooled)
    rim_zy = across_y(rim_z)
    pooled_c = core(pooled)
    pooled_yc = core(pooled_y)
    rim_zc = core(rim_z)
    rim_zyc = core(rim_zy)
    blocks = [pooled, pooled_c, pooled_y, pooled_yc, rim_z, rim_zy, rim_zc, rim_zyc]
    dec_in, near, far = coarse(meta, blocks, enc, flat[1], flat[2], coarse_slots)
    far = next_chip(far)
    near = core(near)
    main, part = inner(dec_in, ids, flat[3])
    out = outer(main, part, near, far, ids, flat[3])
    return out.reshape(features.shape)


def solution(mesh):
    placed = (
        P(("groups", "gx"), None, None, None, None),
        P(("groups", "gx"), None),
        P(("groups", "gx"), None, None),
        P(("groups", "gx")),
        P(("groups", "gx"), None),
        P(("groups", "gx"), None),
        P(),
        P(),
        P(),
        P(),
    )
    return jax.shard_map(
        per_device,
        mesh=mesh,
        in_specs=placed,
        out_specs=P(("groups", "gx"), None, None, None, None),
        check_vma=False,
    )
```

```python
import functools

import jax
import jax.numpy as jnp
from jax import lax
from jax.experimental import pallas as pl
from jax.experimental.pallas import tpu as pltpu
from jax.sharding import PartitionSpec as P


LANES = 4
GROUP = 4
ENC_GROUP = 1
DEC_GROUP = 2
TILE = 16
OFFSETS = (-1, 0, 1)
BF16 = jnp.bfloat16
F32 = jnp.float32
VMEM = pl.BlockSpec(memory_space=pltpu.VMEM)
HBM = pl.BlockSpec(memory_space=pltpu.HBM)
PARAMS = pltpu.CompilerParams(vmem_limit_bytes=16 << 20)


def tap(dx, dy, dz):
    return 9 * (dx + 1) + 3 * (dy + 1) + dz + 1


def pair_weights(w_ref, dxs, width):
    zero = jnp.zeros((3 * width, width), BF16)
    blocks = []
    for dx in dxs:
        for j in range(4):
            sides = []
            for p in range(2):
                dy = j - p
                first = (9 * dx + 3 * dy) * width
                sides.append(w_ref[first : first + 3 * width] if 0 <= dy < 3 else zero)
            blocks.append(jnp.concatenate(sides, axis=1))
    return jnp.concatenate(blocks, axis=0)


def pair_rows(full, j, pairs):
    planes, _, edge, width = full.shape
    picked = jnp.concatenate([full[:, j + 2 * i : j + 2 * i + 1] for i in range(pairs)], axis=1)
    return picked.reshape(planes, pairs * edge, width).astype(BF16)


def unpair(total, planes, pairs, edge, width):
    sides = [
        total[:, p * width : (p + 1) * width].reshape(planes, pairs, 1, edge, width) for p in range(2)
    ]
    return jnp.concatenate(sides, axis=2).reshape(planes, 2 * pairs * edge, width)


def first_kernel(
    x_hbm, w_hbm, nbr_hbm, send_hbm, parent_hbm, child_hbm, around_hbm,
    near_ref, far_ref, meta_ref, codes_ref, x_ref, w_ref, ids_ref, low_ref,
    head_v, last_v, nbr_v, send_v, parent_v, child_v, around_v, numbers, sems,
):
    slots, edge, _, width = x_hbm.shape
    coarse_slots = child_v.shape[0]
    pairs = [(x_hbm.at[:, 0], head_v), (x_hbm.at[:, edge - 1], last_v)]
    pairs += [(nbr_hbm, nbr_v), (send_hbm, send_v), (parent_hbm, parent_v)]
    pairs += [(child_hbm, child_v), (around_hbm, around_v)]
    pairs += [(x_hbm, x_ref), (w_hbm, w_ref)]
    copies = [pltpu.make_async_copy(*pair, sems.at[i]) for i, pair in enumerate(pairs)]
    for copy in copies:
        copy.start()
    for copy in copies[:-2]:
        copy.wait()
    position = lax.axis_index("gx")
    meta_ref[...] = jnp.full(meta_ref.shape, position, jnp.int32)
    meta_ref[0:slots, 0:27] = nbr_v[...]
    meta_ref[slots : slots + 2, 0:slots] = send_v[...]
    meta_ref[slots + 2 : slots + 3, 0:slots] = parent_v[...]
    numbers[...] = jnp.zeros_like(numbers)
    child = child_v[...]
    numbers[0:coarse_slots, 0:8] = jnp.where(child >= 0, (child & (LANES * slots - 1)) + 1, 0)
    around = around_v[...]
    first = ((position >> 2) - 1) * LANES * coarse_slots
    place = around - first
    inside = (around >= 0) & (place >= 0) & (place < 3 * LANES * coarse_slots)
    numbers[coarse_slots : 2 * coarse_slots, 0:27] = jnp.where(inside, place + 1, 0)
    codes_ref[...] = numbers[...].astype(F32).astype(BF16)
    is_odd = (position & 1) == 1
    send = send_v[...]
    slot_of = lax.broadcasted_iota(jnp.int32, send.shape, 1)
    listed = jnp.where(send == slot_of, 1.0, 0.0)
    for b in range(slots):
        last = last_v[b].astype(F32) * listed[0:1, b : b + 1]
        head = head_v[b].astype(F32) * listed[1:2, b : b + 1]
        near_ref[b] = jnp.where(is_odd, head, last).astype(BF16)
        far_ref[b] = jnp.where(is_odd, last, head).astype(BF16)
    for b in range(slots):
        parent = jnp.broadcast_to(parent_v[0:1, b : b + 1], (1, width))
        low_ref[b : b + 1] = jnp.where((parent & 4) == 0, 1, 0)
    z = lax.broadcasted_iota(jnp.int32, (edge, width), 0)
    line = 0
    for dx in (-1, 1, 0):
        for b in range(slots):
            for dy in OFFSETS:
                wide = [
                    jnp.broadcast_to(nbr_v[b : b + 1, tap(dx, dy, dz) : tap(dx, dy, dz) + 1], (edge, width))
                    for dz in OFFSETS
                ]
                ends = (jnp.where(z == 0, wide[0], wide[1]), wide[1], jnp.where(z == edge - 1, wide[2], wide[1]))
                for value in ends:
                    ids_ref[line : line + edge] = value
                    line += edge
    for copy in copies[-2:]:
        copy.wait()


def stay(value):
    return pltpu.with_memory_space_constraint(value, pltpu.HBM)


def first(x, weights, nbr, send, parent, child, around):
    slots, edge, rows, width = x.shape
    coarse_slots = child.shape[0]
    assert 2 * coarse_slots <= TILE and (LANES * slots) & (LANES * slots - 1) == 0
    face = jax.ShapeDtypeStruct((slots, rows, width), BF16)
    return pl.pallas_call(
        first_kernel,
        out_shape=(
            face,
            face,
            jax.ShapeDtypeStruct((slots + 4, width), jnp.int32),
            jax.ShapeDtypeStruct((TILE, width), BF16),
            jax.ShapeDtypeStruct(x.shape, BF16),
            jax.ShapeDtypeStruct(weights.shape, BF16),
            jax.ShapeDtypeStruct((3 * slots * 9 * edge, width), jnp.int32),
            jax.ShapeDtypeStruct((slots, width), jnp.int32),
        ),
        in_specs=[HBM] * 7,
        out_specs=(VMEM,) * 8,
        scratch_shapes=[pltpu.VMEM((slots, rows, width), BF16)] * 2
        + [pltpu.VMEM(v.shape, jnp.int32) for v in (nbr, send, parent, child, around)]
        + [pltpu.VMEM((TILE, width), jnp.int32), pltpu.SemaphoreType.DMA((9,))],
        compiler_params=PARAMS,
        cost_estimate=pl.CostEstimate(flops=0, bytes_accessed=2097152, transcendentals=0),
        name="first",
    )(*[stay(v) for v in (x, weights, nbr, send, parent, child, around)])


def inner_kernel(ids_ref, x_ref, w_ref, out_ref, part_ref, cols, stack):
    slots, edge, _, width = x_ref.shape
    pairs = edge // 2
    empty = jnp.zeros((slots, 4, 3, pairs * edge, width), BF16)
    cols[:, :, :, 0] = empty
    cols[:, :, :, edge + 1] = empty
    for b in range(slots):
        value = x_ref[b].astype(F32).reshape(edge * edge, edge, width)
        for k, turn in enumerate((1, edge - 1)):
            stack[k, b] = pltpu.roll(value, turn, 1).reshape(edge, edge, edge, width)
    weights = pair_weights(w_ref, range(3), width)
    for group in range(0, slots, GROUP):
        bricks = []
        for b in range(group, group + GROUP):
            for k in range(3):
                parts = []
                for dy in OFFSETS:
                    line = (((2 * slots + b) * 3 + dy + 1) * 3 + k) * edge
                    ids = ids_ref[line : line + edge][None, None]
                    first, count = {-1: (edge - 1, 1), 0: (0, edge), 1: (0, 1)}[dy]
                    if dy == 0 and k == 1:
                        held = x_ref[b].astype(F32).reshape(edge, edge, edge, width)
                        value = jnp.where(ids == b, held, 0.0)
                    else:
                        value = jnp.zeros((edge, count, edge, width), F32)
                        for slot in range(slots):
                            if k == 1:
                                row = first // 2 * 2 * edge
                                held = x_ref[slot, :, row : row + 2 * edge].astype(F32)
                                held = held.reshape(edge, 2, edge, width)[:, first % 2 : first % 2 + 1]
                            else:
                                held = stack[k // 2, slot, :, first : first + count]
                            value = jnp.where(ids == slot, held, value)
                    parts.append(value)
                full = jnp.concatenate(parts, axis=1)
                for j in range(4):
                    cols[b, j, k, 1 : edge + 1] = pair_rows(full, j, pairs)
            taps = []
            for dx in range(3):
                for j in range(4):
                    for k in range(3):
                        taps.append(
                            cols[b, j, k, dx : dx + edge].reshape(edge * pairs * edge, width)
                        )
            bricks.append(jnp.concatenate(taps, axis=1))
        totals = jnp.dot(
            jnp.concatenate(bricks, axis=0), weights, preferred_element_type=F32
        )
        count = edge * pairs * edge
        for i in range(GROUP):
            b = group + i
            total = unpair(totals[i * count : (i + 1) * count], edge, pairs, edge, width)
            out_ref[b] = jnp.maximum(total, 0.0).astype(BF16)
            part_ref[b, 0] = total[0]
            part_ref[b, 1] = total[edge - 1]


def inner(x, ids, weights):
    slots, edge, rows, width = x.shape
    return pl.pallas_call(
        inner_kernel,
        out_shape=(
            jax.ShapeDtypeStruct(x.shape, BF16),
            jax.ShapeDtypeStruct((slots, 2, rows, width), F32),
        ),
        in_specs=[VMEM, VMEM, VMEM],
        out_specs=(VMEM, VMEM),
        scratch_shapes=[
            pltpu.VMEM((slots, 4, 3, edge + 2, rows // 2, width), BF16),
            pltpu.VMEM((2, slots, edge, edge, edge, width), F32),
        ],
        compiler_params=PARAMS,
        cost_estimate=pl.CostEstimate(
            flops=2 * slots * edge * rows * 27 * width * width,
            bytes_accessed=4 << 20,
            transcendentals=0,
        ),
        name="inner",
    )(ids, x, weights)


def outer_planes(ids_ref, near_ref, far_ref, part_ref, w_ref, out_ref, stack, edge, copies=None):
    slots, _, rows, width = part_ref.shape
    pairs = edge // 2
    is_odd = lax.axis_index("gx") & 1
    for first, ref in ((0, near_ref), (slots, far_ref)):
        value = ref[...].astype(F32).reshape(slots * edge, edge, width)
        for k, turn in enumerate((1, 0, edge - 1)):
            moved = pltpu.roll(value, turn, 1) if turn else value
            stack[k, first : first + slots] = moved.reshape(slots, rows, width)
    for side, dx in enumerate((-1, 1)):
        offset = slots * (1 - is_odd if side == 0 else is_odd)
        bricks = []
        for b in range(slots):
            shifted = []
            for k in range(3):
                parts = []
                for dy in OFFSETS:
                    line = (((side * slots + b) * 3 + dy + 1) * 3 + k) * edge
                    ids = ids_ref[line : line + edge][None]
                    first, count = {-1: (edge - 1, 1), 0: (0, edge), 1: (0, 1)}[dy]
                    value = jnp.zeros((count, edge, width), F32)
                    for slot in range(slots):
                        held = stack[k, offset + slot, first * edge : (first + count) * edge]
                        value = jnp.where(ids == slot, held.reshape(count, edge, width), value)
                    parts.append(value)
                shifted.append(jnp.concatenate(parts, axis=0)[None])
            taps = []
            for j in range(4):
                for k in range(3):
                    taps.append(pair_rows(shifted[k], j, pairs).reshape(rows // 2, width))
            bricks.append(jnp.concatenate(taps, axis=1))
        extra = jnp.dot(
            jnp.concatenate(bricks, axis=0),
            pair_weights(w_ref, [dx + 1], width),
            preferred_element_type=F32,
        )
        extra = unpair(extra, slots, pairs, edge, width)
        plane = 0 if side == 0 else out_ref.shape[1] - 1
        for b in range(slots):
            total = part_ref[b, side] + extra[b]
            out_ref[b, plane] = jnp.maximum(total, 0.0).astype(BF16)
        if copies is not None:
            copies[side].start()


def outer_kernel(ids_ref, near_ref, far_ref, part_ref, w_ref, main_ref, out_hbm, planes, stack, sems):
    edge = main_ref.shape[1]
    inside = pltpu.make_async_copy(main_ref.at[:, 1 : edge - 1], out_hbm.at[:, 1 : edge - 1], sems.at[0])
    inside.start()
    copies = [
        pltpu.make_async_copy(planes.at[:, i], out_hbm.at[:, x], sems.at[i + 1])
        for i, x in enumerate((0, edge - 1))
    ]
    outer_planes(ids_ref, near_ref, far_ref, part_ref, w_ref, planes, stack, edge, copies)
    for copy in copies + [inside]:
        copy.wait()


def outer(main, part, near, far, ids, weights):
    return pl.pallas_call(
        outer_kernel,
        out_shape=jax.ShapeDtypeStruct(main.shape, BF16),
        in_specs=[VMEM] * 6,
        out_specs=HBM,
        scratch_shapes=[
            pltpu.VMEM(part.shape, BF16),
            pltpu.VMEM((3, 2 * main.shape[0]) + main.shape[2:], F32),
            pltpu.SemaphoreType.DMA((3,)),
        ],
        compiler_params=PARAMS,
        cost_estimate=pl.CostEstimate(flops=536870912, bytes_accessed=4194304, transcendentals=0),
        name="outer",
    )(ids, near, far, part, weights, main)


def outer_pool_kernel(
    ids_ref, low_ref, near_ref, far_ref, part_ref, w_ref, main_ref, code_ref, out_ref, pool_ref, rim_ref, sums, stack
):
    slots, edge, _, width = out_ref.shape
    half = edge // 2
    out_ref[:, 1 : edge - 1] = main_ref[:, 1 : edge - 1]
    outer_planes(ids_ref, near_ref, far_ref, part_ref, w_ref, out_ref, stack, edge)
    cells = half**3
    pool_ref[slots * cells :] = code_ref[...]
    rim_ref[slots * cells // 2 :] = code_ref[...]
    for b in range(slots):
        value = out_ref[b].astype(F32).reshape(half, 2, half, 2, edge, width)
        value = (value[:, 0, :, 0] + value[:, 0, :, 1]) + (value[:, 1, :, 0] + value[:, 1, :, 1])
        sums[b] = value.reshape(half * half * edge, width)
        low = sums[b, pl.ds(0, cells, stride=2), :]
        high = sums[b, pl.ds(1, cells, stride=2), :]
        pooled = (low + high) * 0.125
        pool_ref[b * cells : (b + 1) * cells, :] = pooled.astype(BF16)
        rim = jnp.where(low_ref[b : b + 1] == 1, pooled[: cells // 2], pooled[cells // 2 :])
        rim_ref[b * cells // 2 : (b + 1) * cells // 2, :] = rim.astype(BF16)


def outer_pool(main, part, near, far, ids, low, weights, codes):
    slots, edge, rows, width = main.shape
    cells = (edge // 2) ** 3
    return pl.pallas_call(
        outer_pool_kernel,
        out_shape=(
            jax.ShapeDtypeStruct(main.shape, BF16),
            jax.ShapeDtypeStruct((slots * cells + TILE, width), BF16),
            jax.ShapeDtypeStruct((slots * cells // 2 + TILE, width), BF16),
        ),
        in_specs=[VMEM] * 8,
        out_specs=(VMEM, VMEM, VMEM),
        scratch_shapes=[
            pltpu.VMEM((slots, 2 * cells, width), F32),
            pltpu.VMEM((3, 2 * slots, rows, width), F32),
        ],
        compiler_params=PARAMS,
        cost_estimate=pl.CostEstimate(flops=536870912, bytes_accessed=4194304, transcendentals=0),
        name="outer_pool",
    )(ids, low, near, far, part, weights, main, codes)


def x_pair_weights(w_ref, width):
    count = 9 * width
    zero = jnp.zeros((count, width), BF16)
    blocks = []
    for j in range(4):
        sides = [w_ref[(j - p) * count : (j - p + 1) * count] if 0 <= j - p < 3 else zero for p in range(2)]
        blocks.append(jnp.concatenate(sides, axis=1))
    return jnp.concatenate(blocks, axis=0)


def valid_conv(values, weights, cols, edge, width, group):
    size = values[0].shape[0]
    inside = size - 2
    pairs = inside // 2
    even, odd = cols
    bricks = []
    for b, value in enumerate(values):
        flat = value.reshape(size * size, edge, width)
        for k in range(3):
            moved = flat if k == 0 else pltpu.roll(flat, edge - k, 1)
            moved = moved.reshape(size, size, edge, width)
            even[b, k] = moved.reshape(size, size * edge, width).astype(BF16)
            odd[b, k] = moved[:, 1 : size - 1].reshape(size, inside * edge, width).astype(BF16)
        taps = []
        for j in range(4):
            for dy in range(3):
                for k in range(3):
                    if dy == 1:
                        planes = [odd[b, k, j + 2 * i] for i in range(pairs)]
                    else:
                        rows = slice(dy * edge, (dy + inside) * edge)
                        planes = [even[b, k, j + 2 * i, rows] for i in range(pairs)]
                    taps.append(jnp.concatenate(planes, axis=0))
        bricks.append(jnp.concatenate(taps, axis=1))
    rows = inside * edge
    outs = []
    for first in range(0, len(values), group):
        picked = bricks[first : first + group]
        total = jnp.dot(jnp.concatenate(picked, axis=0), weights, preferred_element_type=F32)
        total = jnp.maximum(total, 0.0).astype(BF16).astype(F32)
        for i in range(len(picked)):
            one = total[i * pairs * rows : (i + 1) * pairs * rows]
            sides = [one[:, p * width : (p + 1) * width].reshape(pairs, 1, rows, width) for p in range(2)]
            outs.append(jnp.concatenate(sides, axis=1).reshape(inside, inside, edge, width))
    return outs


def coarse_kernel(
    coarse_slots, meta_ref, own_ref, core_ref, y_ref, yc_ref, z_ref, zy_ref, zc_ref, zyc_ref, enc_ref, w1_ref, w2_ref,
    out_ref, near_ref, far_ref, held, codes, even, odd, even2, odd2, spread, table, code_s, sem,
):
    slots, edge, rows, width = enc_ref.shape
    half = edge // 2
    plane = half * half
    cells = half * plane
    position = lax.axis_index("gx")
    lane = position & (LANES - 1)
    lane_c = position & 1
    whole_rows = slots * cells
    rim_rows = whole_rows // 2
    section = (LANES * slots + 1) * cells
    places = [(ref, 0, whole_rows) for ref in (own_ref, core_ref, y_ref, yc_ref)]
    for ref in (z_ref, zy_ref, zc_ref, zyc_ref):
        places += [(ref, at, rim_rows) for at in (0, rim_rows + TILE)]
    origins = [LANES + (lane ^ i) for i in range(LANES)]
    near_rel = jnp.where(lane_c == 1, 2 * LANES, 0)
    far_rel = 2 * LANES - near_rel
    origins += [near_rel + (lane ^ 1 ^ i) for i in range(LANES)]
    origins += [far_rel + (lane ^ i) for i in range(LANES)]
    lines = 3 * LANES * coarse_slots + 1
    codes[...] = jnp.zeros_like(codes)
    after = lines + LANES * coarse_slots
    codes[after : after + 3] = meta_ref[slots : slots + 3]
    for i, (origin, (ref, at, count)) in enumerate(zip(origins, places)):
        line = ref[at + count : at + count + TILE].astype(F32).astype(jnp.int32)
        row = 1 + origin * coarse_slots
        start = 2 * section if i < LANES else jnp.where(origin >= LANES, 3 * section, section)
        codes[pl.ds(row, coarse_slots)] = line[:coarse_slots] * cells + start
        if i < LANES:
            row = lines + (origin - LANES) * coarse_slots
            codes[pl.ds(row, coarse_slots)] = line[coarse_slots : 2 * coarse_slots]
    copy = pltpu.make_async_copy(codes, table, sem)
    copy.start()
    for i in range(4):
        held[i * section : i * section + cells] = jnp.zeros((cells, width), BF16)
    for i, (origin, (ref, at, count)) in enumerate(zip(origins, places)):
        if i < LANES:
            start = section + cells + origin * whole_rows
            start = pl.multiple_of(start + section - LANES * whole_rows, TILE)
            held[pl.ds(start, count)] = ref[at : at + count]
        else:
            group_start = jnp.where(origin >= LANES, 3 * section - 2 * LANES * whole_rows, section)
            start = group_start + cells + origin * whole_rows
            value = ref[at : at + count].reshape(slots, 1, cells // 2, width)
            start = pl.multiple_of(start, TILE)
            held[pl.ds(start, whole_rows)] = jnp.concatenate([value, value], axis=1).reshape(
                whole_rows, width
            )
    group_first = (position >> 2) * LANES * coarse_slots
    copy.wait()

    row_of = lax.broadcasted_iota(jnp.int32, (1, edge, width), 1)
    from_above = (row_of & 2) == 0
    center = (row_of >= 2) & (row_of < half + 2)
    regions = []
    masks = []
    for b in range(slots):
        own = jnp.where(table[after + 2, b] >= 0, table[after + 2, b], group_first * 8)
        octant = own & 7
        bits = ((octant >> 2) & 1, (octant >> 1) & 1, octant & 1)
        brick = jnp.clip((own >> 3) - group_first, 0, LANES * coarse_slots - 1)
        home = lines + brick
        steps = [scale * (2 * bit - 1) for scale, bit in zip((9, 3, 1), bits)]
        numbers = [13, 13 + steps[2]]
        numbers += [number + steps[1] for number in numbers]
        numbers += [number + steps[0] for number in numbers]
        for cross, number in enumerate(numbers):
            code_s[b, cross] = table[home, number]
        turns = [octant ^ flip for flip in range(8)]
        across = [{0: 0, 1: scale * bit, -1: scale * (1 - bit)} for scale, bit in zip((4, 2, 1), bits)]

        def base_of(ex, ey, ez):
            flip = 4 * abs(ex) + 2 * abs(ey) + abs(ez)
            cross = across[0][ex] + across[1][ey] + across[2][ez]
            base = table[code_s[b, cross], turns[flip]]
            return pl.multiple_of(base + (2 * plane if ex < 0 else 0), TILE)

        x_parts = []
        for ex in OFFSETS:
            planes = half if ex == 0 else 2
            y_parts = []
            for ey in OFFSETS:
                picked = []
                for ez in OFFSETS:
                    value = held[pl.ds(base_of(ex, ey, ez), planes * plane), :].astype(F32)
                    value = value.reshape(planes, 2, edge, width)
                    if ey < 0:
                        value = value[:, 1:]
                    elif ey > 0:
                        value = value[:, :1]
                    picked.append(value.reshape(-1, edge, width))
                sides = jnp.where(from_above, picked[2], picked[0])
                first_y = jnp.where(center, pltpu.roll(picked[1], 2, 1), pltpu.roll(sides, edge - 2, 1))
                second_y = jnp.where(center, pltpu.roll(picked[1], edge - 2, 1), pltpu.roll(sides, 2, 1))
                shape = (planes, -1, 1, edge, width)
                both = jnp.concatenate([first_y.reshape(shape), second_y.reshape(shape)], axis=2)
                y_parts.append(both.reshape(planes, -1, edge, width))
            x_parts.append(jnp.concatenate(y_parts, axis=1))
        regions.append(jnp.concatenate(x_parts, axis=0))
        at_edge = jnp.where(bits[2] == 1, half + 1, 0)
        kinds = []
        for ex in OFFSETS:
            for ey in OFFSETS:
                cross = across[0][ex] + across[1][ey]
                there = jnp.where(row_of == at_edge, code_s[b, cross + 1], code_s[b, cross])
                kinds.append(there > 0)
        masks.append(kinds)

    mids = []
    for value, kinds in zip(valid_conv(regions, x_pair_weights(w1_ref, width), (even, odd), edge, width, ENC_GROUP), masks):
        spans = ((0, 1), (1, half + 1), (half + 1, half + 2))
        x_parts = []
        for i, (x0, x1) in enumerate(spans):
            y_parts = []
            for n, (y0, y1) in enumerate(spans):
                y_parts.append(jnp.where(kinds[3 * i + n][None], value[x0:x1, y0:y1], 0.0))
            x_parts.append(jnp.concatenate(y_parts, axis=1))
        mids.append(jnp.concatenate(x_parts, axis=0))
    fines = valid_conv(mids, x_pair_weights(w2_ref, width), (even2, odd2), edge, width, DEC_GROUP)
    is_odd = lane_c == 1
    for b in range(slots):
        value = jnp.where(table[after + 2, b] >= 0, fines[b], 0.0).reshape(plane * edge, width)
        spread[b, pl.ds(0, plane * edge, stride=2), :] = value
        spread[b, pl.ds(1, plane * edge, stride=2), :] = value
        up = spread[b].reshape(half, half, 2 * edge, width)[:, :, :edge]
        base = enc_ref[b].astype(F32).reshape(half, 2, half, 2, edge, width)
        total = base + up[:, None, :, None]
        total = total.reshape(edge, rows, width).astype(BF16)
        out_ref[b] = total
        last = jnp.where(table[after, b] == b, total[edge - 1], 0)
        head = jnp.where(table[after + 1, b] == b, total[0], 0)
        near_ref[b] = jnp.where(is_odd, head, last)
        far_ref[b] = jnp.where(is_odd, last, head)


def coarse(meta, blocks, enc, w1, w2, coarse_slots):
    slots, edge, rows, width = enc.shape
    half = edge // 2
    inside = edge - 2
    total = 4 * (LANES * slots + 1) * half**3
    lines = 4 * LANES * coarse_slots + 4
    face = jax.ShapeDtypeStruct((slots, rows, width), BF16)
    return pl.pallas_call(
        functools.partial(coarse_kernel, coarse_slots),
        out_shape=(jax.ShapeDtypeStruct(enc.shape, BF16), face, face),
        in_specs=[VMEM] * 12,
        out_specs=(VMEM, VMEM, VMEM),
        scratch_shapes=[
            pltpu.VMEM((total, width), BF16),
            pltpu.VMEM((lines, width), jnp.int32),
            pltpu.VMEM((slots, 3, edge, edge * edge, width), BF16),
            pltpu.VMEM((slots, 3, edge, inside * edge, width), BF16),
            pltpu.VMEM((slots, 3, inside, inside * edge, width), BF16),
            pltpu.VMEM((slots, 3, inside, half * edge, width), BF16),
            pltpu.VMEM((slots, 2 * half * half * edge, width), F32),
            pltpu.SMEM((lines, width), jnp.int32),
            pltpu.SMEM((slots, 8), jnp.int32),
            pltpu.SemaphoreType.DMA,
        ],
        compiler_params=PARAMS,
        cost_estimate=pl.CostEstimate(flops=2147483648, bytes_accessed=8388608, transcendentals=0),
        name="coarse",
    )(meta, *blocks, enc, w1, w2)


def per_device(
    features,
    fine_nbr,
    fine_send,
    fine_parent,
    coarse_child,
    coarse_nbr,
    enc_fine_w,
    enc_coarse_w,
    dec_coarse_w,
    dec_fine_w,
):
    slots, edge, _, _, width = features.shape
    coarse_slots = coarse_nbr.shape[0]
    size = lax.axis_size("gx")

    def swap(value, partner):
        pairs = [(i, partner(i)) for i in range(size) if 0 <= partner(i) < size]
        return lax.ppermute(value, "gx", pairs)

    def core(value):
        return swap(value, lambda i: i ^ 1)

    def next_chip(value):
        return swap(value, lambda i: i + 1 if i % 2 else i - 1)

    def across_y(value):
        return swap(value, lambda i: i ^ 2)

    def across_z(value):
        return swap(value, lambda i: i + 3 if i % 2 else i - 3)

    x = features.reshape(slots, edge, edge * edge, width)
    flat = [w.reshape(27 * width, width) for w in (enc_fine_w, enc_coarse_w, dec_coarse_w, dec_fine_w)]
    near, far, meta, codes, x, first_w, ids, low = first(
        x, flat[0], fine_nbr, fine_send[0], fine_parent.reshape(1, slots), coarse_child, coarse_nbr
    )
    far = next_chip(far)
    near = core(near)
    main, part = inner(x, ids, first_w)
    enc, pooled, rim = outer_pool(main, part, near, far, ids, low, first_w, codes)

    rim_c = core(rim)
    rim_z = across_z(jnp.concatenate([rim, rim_c], axis=0))
    pooled_y = across_y(pooled)
    rim_zy = across_y(rim_z)
    pooled_c = core(pooled)
    pooled_yc = core(pooled_y)
    rim_zc = core(rim_z)
    rim_zyc = core(rim_zy)
    blocks = [pooled, pooled_c, pooled_y, pooled_yc, rim_z, rim_zy, rim_zc, rim_zyc]
    dec_in, near, far = coarse(meta, blocks, enc, flat[1], flat[2], coarse_slots)
    far = next_chip(far)
    near = core(near)
    main, part = inner(dec_in, ids, flat[3])
    out = outer(main, part, near, far, ids, flat[3])
    return out.reshape(features.shape)


def solution(mesh):
    placed = (
        P(("groups", "gx"), None, None, None, None),
        P(("groups", "gx"), None),
        P(("groups", "gx"), None, None),
        P(("groups", "gx")),
        P(("groups", "gx"), None),
        P(("groups", "gx"), None),
        P(),
        P(),
        P(),
        P(),
    )
    return jax.shard_map(
        per_device,
        mesh=mesh,
        in_specs=placed,
        out_specs=P(("groups", "gx"), None, None, None, None),
        check_vma=False,
    )
```
